32 devices in a mesh: gx: 8 (over z, core), gy: 4 (over y, x).
Axes of the slice: x: 2, y: 2, z: 4, core: 2. Of those that a mesh axis runs over, the one named last changes fastest.
Arguments:
- adj_voltage: float32 [8, 256, 128], P('gx', 'gy'), may hold values from -6 to 6
- adj_gating: float32 [8, 256, 128], P('gx', 'gy'), may hold values from -1.2 to 1.2
- fwd_voltage: bfloat16 [2, 8, 256, 128], P(None, 'gx', 'gy'), may hold values from -0.099609375 to 1.09375
- fwd_gating: bfloat16 [2, 8, 256, 128], P(None, 'gx', 'gy'), may hold values from 0 to 2
- region_labels: int32 [8, 256, 1], P('gx', 'gy'), may hold values from 0 to 7
- region_axial: float32 [2, 8], replicated, may hold values from 0.6 to 3
- region_shear: float32 [8], replicated, may hold values from -0.5 to 0.5
- block_rate: float32 [2], replicated, may hold values from 8 to 32
- block_inverse: float32 [2, 128, 128], replicated, as said below
Outputs:
- voltage_adjoint: float32 [8, 256, 128], P('gx', 'gy')
- gating_adjoint: float32 [8, 256, 128], P('gx', 'gy')
The draws below stay inside these ranges and needn't reach their ends.
Inputs may be any that keep to these rules, and one draw needn't show every extreme that they name: block_inverse[b] is the inverse of the 128 x 128 tridiagonal matrix with diagonal 1 + 2 block_rate[b] and off-diagonals -block_rate[b].
All inputs are finite; a program needn't handle non-finite values.
Results may differ from the reference program's by a relative error of at most 0.00065.
Values sent between devices are 32-bit elements; how exact they have to be, the bound alone decides.
No kernel may reach another device: no remote copies, remote signals or barrier semaphores. Data moves between devices by JAX's collectives and lax.ppermute only.
A program may use at most 64 MiB of HBM per device.

```python
import math
import jax
import jax.numpy as jnp
from jax import lax

STEPS = 2
SWEEPS = 11
ZB = 128
LB = 128
REGIONS = 8
NX = 8
NY = 128
NZ = 256
NYB = 1


def rates_and_inverses(key):
    subkey = jax.random.fold_in(key, 4021)
    rate_values = jnp.exp(jax.random.uniform(subkey, (NZ // ZB,), jnp.float32, math.log(8.0), math.log(32.0)))
    decay = (1.0 + 2.0 * rate_values - jnp.sqrt(1.0 + 4.0 * rate_values)) / (2.0 * rate_values)
    log_decay = jnp.log(decay)[:, None, None]
    position = jnp.arange(ZB, dtype=jnp.float32)
    row_pos = position[:, None]
    col_pos = position[None, :]
    apart = jnp.abs(row_pos - col_pos)[None]
    joined = (row_pos + col_pos)[None]

    def power_of(exponent):
        return jnp.exp(exponent * log_decay)
    numerator = power_of(apart) - power_of(joined + 2.0) - power_of(2.0 * ZB - joined) + power_of(2.0 * ZB + 2.0 - apart)
    scale_rate = rate_values[:, None, None]
    decay_full = decay[:, None, None]
    denominator = scale_rate * (1.0 / decay_full - decay_full) * (1.0 - power_of(2.0 * ZB + 2.0 + 0.0 * apart))
    return (rate_values, numerator / denominator)


def draw_block_rate(key, part):
    return rates_and_inverses(key)[0]


def draw_block_inverse(key, part):
    return rates_and_inverses(key)[1]


def touch_ends(values, stream_key, least, high):
    shape = values.shape
    place = [jax.random.randint(jax.random.fold_in(stream_key, axis), (), 0, shape[axis]) for axis in range(len(shape))]
    values = values.at[tuple(place)].set(least)
    longest = shape.index(max(shape))
    place[longest] = (place[longest] + 1) % shape[longest]
    return values.at[tuple(place)].set(high)


def steps_of(own_key, dims, split, least, largest):
    factor_of, own = 1.0, jax.random.fold_in(own_key, 6)
    for dim, parts in split:
        steps = jnp.exp(jax.random.uniform(jax.random.fold_in(own, dim), (parts,), jnp.float32, least / len(split), largest / len(split)))
        factor_of = factor_of * jnp.repeat(steps, dims[dim] // parts).reshape([-1 if axis == dim else 1 for axis in range(len(dims))])
    return factor_of


def centred(key, dims, spread, most, pieces=(), kind=jnp.bfloat16):
    drawn = jax.random.normal(key, dims, jnp.float32) * spread
    if len(pieces) > 0:
        drawn = steps_of(key, dims, pieces, -0.22, 0.18) * drawn
    return jnp.clip(drawn, min=-most, max=most).astype(kind)


def setup_inputs(seed: int = 0) -> dict:
    key_of = jax.random.split(jax.random.key(seed), 10)
    adj_voltage = centred(key_of[0], (NX, NZ, NY), 1.0, 6.0, ((0, 8), (1, 4)), jnp.float32)
    adj_gating = centred(key_of[1], (NX, NZ, NY), 0.2, 1.2, ((0, 8), (1, 4)), jnp.float32)
    fwd_voltage = jnp.clip(-0.099609375 + 1.1933594 * jax.random.uniform(key_of[2], (STEPS, NX, NZ, NY), jnp.float32) ** steps_of(key_of[2], (STEPS, NX, NZ, NY), ((1, 8), (2, 4)), -0.2, 0.2), -0.099609375, 1.09375).astype(jnp.bfloat16)
    fwd_gating = jnp.clip(2.0 * jax.random.uniform(key_of[3], (STEPS, NX, NZ, NY), jnp.float32) ** steps_of(key_of[3], (STEPS, NX, NZ, NY), ((1, 8), (2, 4)), -0.2, 0.2), 0.0, 2.0).astype(jnp.bfloat16)
    region_labels = touch_ends(jax.random.randint(key_of[4], (NX, NZ, NYB), 0, REGIONS), jax.random.fold_in(key_of[4], 1), 0, REGIONS - 1).astype(jnp.int32)
    region_axial = jnp.clip(jnp.exp(jax.random.uniform(key_of[5], (2, REGIONS), jnp.float32, math.log(0.6), math.log(3.0))), 0.6, 3.0)
    region_shear = jnp.clip(jax.random.uniform(key_of[6], (REGIONS,), jnp.float32, -0.5, 0.5), -0.5, 0.5)
    block_rate = draw_block_rate(jax.random.fold_in(key_of[9], 71), 0)
    block_inverse = draw_block_inverse(jax.random.fold_in(key_of[9], 71), 0)
    return {"adj_voltage": adj_voltage, "adj_gating": adj_gating, "fwd_voltage": fwd_voltage, "fwd_gating": fwd_gating, "region_labels": region_labels, "region_axial": region_axial, "region_shear": region_shear, "block_rate": block_rate, "block_inverse": block_inverse}


FULL_PRECISION = lax.Precision.HIGHEST
TIME_STEP = 0.2
RECOVERY_RATE = 0.25
EXCITATION = 8.0
THRESHOLD = 0.15


def couplings(block_rate):
    zero_rate = jnp.zeros((1,), jnp.float32)
    inner_rate = jnp.minimum(block_rate[:-1], block_rate[1:])
    return jnp.concatenate([zero_rate, inner_rate]), jnp.concatenate([inner_rate, zero_rate])


def line_solve(line_cells, block_rate, block_inverse):
    item_count, length_cells, across = line_cells.shape
    blocks_count = length_cells // ZB
    shaped = line_cells.reshape(item_count, blocks_count, ZB, across)
    below_rate, after_rate = couplings(block_rate)
    base_blocks = jnp.einsum("bij,xbjy->xbiy", block_inverse, shaped, precision=FULL_PRECISION)
    zero_row = jnp.zeros((item_count, 1, across), jnp.float32)
    first_column = block_inverse[None, :, :, 0, None]
    last_column = block_inverse[None, :, :, ZB - 1, None]

    def sweep_once(sweep_index, current):
        first_cells = current[:, :, 0, :]
        last_cells = current[:, :, ZB - 1, :]
        from_below = jnp.concatenate([zero_row, last_cells[:, :-1, :]], axis=1) * below_rate[None, :, None]
        from_above = jnp.concatenate([first_cells[:, 1:, :], zero_row], axis=1) * after_rate[None, :, None]
        return base_blocks + first_column * from_below[:, :, None, :] + last_column * from_above[:, :, None, :]

    current = lax.fori_loop(0, SWEEPS, sweep_once, base_blocks)
    return current.reshape(item_count, length_cells, across)


def cross_terms(ext_xx, ext_yy, ext_xy):
    pad_y = ((0, 0), (0, 0), (1, 1))
    ext_yy = jnp.pad(ext_yy, pad_y)
    ext_xy = jnp.pad(ext_xy, pad_y)
    term_xx = ext_xx[2:] - 2.0 * ext_xx[1:-1] + ext_xx[:-2]
    term_yy = ext_yy[1:-1, :, 2:] - 2.0 * ext_yy[1:-1, :, 1:-1] + ext_yy[1:-1, :, :-2]
    term_xy = (ext_xy[2:, :, 2:] - ext_xy[2:, :, :-2] - ext_xy[:-2, :, 2:] + ext_xy[:-2, :, :-2]) * 0.25
    return term_xx + term_yy + 2.0 * term_xy


def reference(adj_voltage, adj_gating, fwd_voltage, fwd_gating, region_labels, region_axial, region_shear, block_rate, block_inverse):
    cell_labels = jnp.repeat(region_labels, LB, axis=2).astype(jnp.int32)
    tissue = (cell_labels > 0).astype(jnp.float32)
    coef_xx = region_axial[0][cell_labels] * tissue
    coef_yy = region_axial[1][cell_labels] * tissue
    coef_xy = region_shear[cell_labels] * tissue
    pad_x = ((1, 1), (0, 0), (0, 0))
    adjoint_v = adj_voltage
    adjoint_w = adj_gating
    for step_index in range(STEPS):
        later_index = STEPS - 1 - step_index
        solved = line_solve(adjoint_v, block_rate, block_inverse)
        spread_term = cross_terms(jnp.pad(coef_xx * solved, pad_x), jnp.pad(coef_yy * solved, pad_x), jnp.pad(coef_xy * solved, pad_x))
        voltage_now = fwd_voltage[later_index].astype(jnp.float32)
        gating_now = fwd_gating[later_index].astype(jnp.float32)
        ionic_slope = EXCITATION * (-3.0 * voltage_now * voltage_now + 2.0 * (1.0 + THRESHOLD) * voltage_now - THRESHOLD) - gating_now
        next_v = tissue * (solved + TIME_STEP * spread_term + TIME_STEP * ionic_slope * solved + TIME_STEP * RECOVERY_RATE * EXCITATION * adjoint_w)
        adjoint_w = tissue * ((1.0 - TIME_STEP * RECOVERY_RATE) * adjoint_w - TIME_STEP * voltage_now * solved)
        adjoint_v = next_v
    return adjoint_v, adjoint_w
```

```python
import jax
import jax.numpy as jnp
from jax import lax
from jax.experimental import pallas as pl
from jax.experimental.pallas import tpu as pltpu
from jax.sharding import PartitionSpec as P

STEPS = 2
SWEEPS = 11
ZB = 128
LB = 128
HB = 64

TIME_STEP = 0.2
RECOVERY_RATE = 0.25
EXCITATION = 8.0
THRESHOLD = 0.15

VMEM = pl.BlockSpec(memory_space=pltpu.VMEM)
SMEM = pl.BlockSpec(memory_space=pltpu.SMEM)


def half_product(field, inv_ref):
    me = lax.axis_index("gy")
    upper = lax.rem(me, 2) == 1
    matrix = inv_ref[lax.div(me, 2)]
    nothing = jnp.zeros_like(field)
    padded = jnp.concatenate(
        [jnp.where(upper, nothing, field), jnp.where(upper, field, nothing)], axis=0
    )
    product = jnp.dot(
        matrix, padded, precision=lax.Precision.HIGHEST, preferred_element_type=jnp.float32
    )
    own = jnp.where(upper, product[HB:], product[:HB])
    inner = jnp.where(upper, product[HB - 1 : HB], product[HB : HB + 1])
    outer = jnp.where(upper, product[ZB - 1 :], product[:1])
    return own, inner, outer


def write_product(field, inv_ref, own_ref, edge_ref):
    own, inner, outer = half_product(field, inv_ref)
    own_ref[...] = own
    row = lax.broadcasted_iota(jnp.int32, edge_ref.shape, 0)
    edge_ref[...] = jnp.where(row == 0, inner, jnp.where(row == 1, outer, 0.0))


def start_kernel(field_ref, inv_ref, own_ref, edge_ref):
    write_product(field_ref[...], inv_ref, own_ref, edge_ref)


def solved_half(own, edges, inv_ref, rate_ref):
    me = lax.axis_index("gy")
    upper = lax.rem(me, 2) == 1
    mine = lax.div(me, 2)
    blocks = inv_ref.shape[0]
    first, last, corner = [], [], []
    for block in range(blocks):
        low = edges[lax.bitwise_xor(2 * block, me)]
        high = edges[lax.bitwise_xor(2 * block + 1, me)]
        top, bottom = inv_ref[block, 0:1], inv_ref[block, ZB - 1 : ZB]
        mid_low, mid_high = inv_ref[block, HB - 1 : HB], inv_ref[block, HB : HB + 1]
        reach_first = top[:, HB : HB + 1] / mid_low[:, HB : HB + 1]
        reach_last = bottom[:, HB - 1 : HB] / mid_high[:, HB - 1 : HB]
        first.append(low[1:2] + reach_first * high[0:1])
        last.append(high[1:2] + reach_last * low[0:1])
        corner.append((top[:, 0:1], top[:, ZB - 1 :], bottom[:, 0:1], bottom[:, ZB - 1 :]))
    zero = jnp.zeros_like(first[0])

    def couple(u_first, u_last):
        below = [zero] + [
            jnp.minimum(rate_ref[b], rate_ref[b + 1]) * u_last[b] for b in range(blocks - 1)
        ]
        above = [
            jnp.minimum(rate_ref[b], rate_ref[b + 1]) * u_first[b + 1] for b in range(blocks - 1)
        ] + [zero]
        return below, above

    u_first, u_last = first, last
    for _ in range(SWEEPS - 1):
        below, above = couple(u_first, u_last)
        u_first = [
            first[b] + corner[b][0] * below[b] + corner[b][1] * above[b] for b in range(blocks)
        ]
        u_last = [
            last[b] + corner[b][2] * below[b] + corner[b][3] * above[b] for b in range(blocks)
        ]
    below, above = couple(u_first, u_last)
    from_below, from_above = below[0], above[0]
    for b in range(1, blocks):
        from_below = jnp.where(mine == b, below[b], from_below)
        from_above = jnp.where(mine == b, above[b], from_above)
    rows = inv_ref[mine, pl.ds(pl.multiple_of(lax.rem(me, 2) * HB, HB), HB), :]
    partner = edges[1][0:1]
    middle = inv_ref[mine, HB - 1 : HB + 1]
    bridge = jnp.where(upper, middle[1:2, HB - 1 : HB], middle[0:1, HB : HB + 1])
    across = jnp.where(upper, rows[:, HB - 1 : HB], rows[:, HB : HB + 1])
    return (
        own
        + across * (partner / bridge)
        + rows[:, 0:1] * from_below
        + rows[:, ZB - 1 :] * from_above
    )


def region_fields(label_ref, axial_ref, shear_ref, width):
    parts = []
    for block in range(width // LB):
        label = jnp.broadcast_to(label_ref[:, block : block + 1], (HB, LB))
        along = jnp.zeros((HB, LB), jnp.float32)
        across, shear = along, along
        for region in range(1, axial_ref.shape[1]):
            here = label == region
            along = jnp.where(here, axial_ref[0, region], along)
            across = jnp.where(here, axial_ref[1, region], across)
            shear = jnp.where(here, shear_ref[region], shear)
        parts.append(((label > 0).astype(jnp.float32), along, across, shear))
    return [jnp.concatenate(p, axis=1) if len(p) > 1 else p[0] for p in zip(*parts)]


def y_neighbours(field):
    width = field.shape[1]
    lane = lax.broadcasted_iota(jnp.int32, field.shape, 1)
    below = jnp.where(lane == 0, 0.0, pltpu.roll(field, 1, 1))
    above = jnp.where(lane == width - 1, 0.0, pltpu.roll(field, width - 1, 1))
    return below, above


def step_kernel(
    count, step, own_ref, *refs
):
    edge_refs = refs[:count]
    (inv_ref, rate_ref, label_ref, axial_ref, shear_ref, voltage_ref, gating_ref, w_ref) = refs[
        count : count + 8
    ]
    stay_ref, pair_ref, next_ref, w_out_ref, edges = refs[count + 8 :]
    for d in range(count):
        edges[d] = edge_refs[d][...]
    solved = solved_half(own_ref[...], edges, inv_ref, rate_ref)
    tissue, along, across, shear = region_fields(label_ref, axial_ref, shear_ref, solved.shape[1])
    voltage = voltage_ref[step].astype(jnp.float32)
    gating = gating_ref[step].astype(jnp.float32)
    slope = (
        EXCITATION
        * (-3.0 * voltage * voltage + 2.0 * (1.0 + THRESHOLD) * voltage - THRESHOLD)
        - gating
    )
    w = w_ref[...]
    flux_x = along * solved
    flux_y = across * solved
    y_below, y_above = y_neighbours(flux_y)
    s_below, s_above = y_neighbours(shear * solved)
    twist = 0.5 * (s_above - s_below)
    spread = y_above - 2.0 * flux_y + y_below - 2.0 * flux_x
    stay_ref[...] = tissue * (
        solved
        + TIME_STEP * spread
        + TIME_STEP * slope * solved
        + TIME_STEP * RECOVERY_RATE * EXCITATION * w
    )
    w_out_ref[...] = tissue * (
        (1.0 - TIME_STEP * RECOVERY_RATE) * w - TIME_STEP * voltage * solved
    )
    even = lax.rem(lax.axis_index("gx"), 2) == 0
    twist = jnp.where(even, -twist, twist)
    pair_ref[...] = TIME_STEP * (flux_x + twist)
    next_ref[...] = TIME_STEP * (flux_x - twist)


def labelled_tissue(label_ref, width):
    parts = [
        jnp.broadcast_to(label_ref[:, b : b + 1], (HB, LB)) > 0 for b in range(width // LB)
    ]
    return jnp.concatenate(parts, axis=1) if len(parts) > 1 else parts[0]


def joined(stay_ref, a_ref, b_ref, label_ref):
    here = labelled_tissue(label_ref, stay_ref.shape[1])
    return stay_ref[...] + jnp.where(here, a_ref[...] + b_ref[...], 0.0)


def between_kernel(stay_ref, a_ref, b_ref, label_ref, inv_ref, own_ref, edge_ref):
    write_product(joined(stay_ref, a_ref, b_ref, label_ref), inv_ref, own_ref, edge_ref)


def end_kernel(stay_ref, a_ref, b_ref, label_ref, out_ref):
    out_ref[...] = joined(stay_ref, a_ref, b_ref, label_ref)


def per_device(
    adj_voltage,
    adj_gating,
    fwd_voltage,
    fwd_gating,
    region_labels,
    region_axial,
    region_shear,
    block_rate,
    block_inverse,
):
    lanes, lines = lax.axis_size("gy"), lax.axis_size("gx")
    _, depth, width = adj_voltage.shape
    assert depth == HB and block_inverse.shape[1] == ZB
    f32 = jnp.float32
    plane = jax.ShapeDtypeStruct((HB, width), f32)
    edge = jax.ShapeDtypeStruct((8, width), f32)
    labels = region_labels[0]
    voltage, gating = fwd_voltage[:, 0], fwd_gating[:, 0]
    own, edges = pl.pallas_call(
        start_kernel, out_shape=(plane, edge), in_specs=[VMEM] * 2, out_specs=(VMEM, VMEM)
    )(adj_voltage[0], block_inverse)
    w = adj_gating[0]
    pair = [(i, i ^ 1) for i in range(lines)]
    after = [(i, j) for a in range(1, lines - 1, 2) for i, j in ((a, a + 1), (a + 1, a))]
    for step_index in range(STEPS):
        later = STEPS - 1 - step_index
        all_edges = [edges] + [
            lax.ppermute(edges, "gy", [(i, i ^ d) for i in range(lanes)]) for d in range(1, lanes)
        ]
        stay, to_pair, to_next, w = pl.pallas_call(
            lambda *refs: step_kernel(lanes, later, *refs),
            out_shape=(plane,) * 4,
            in_specs=[VMEM] * (lanes + 2)
            + [SMEM, VMEM, SMEM, SMEM]
            + [VMEM] * 3,
            out_specs=(VMEM,) * 4,
            scratch_shapes=[pltpu.VMEM((lanes, 8, width), f32)],
        )(
            own,
            *all_edges,
            block_inverse,
            block_rate,
            labels,
            region_axial,
            region_shear,
            voltage,
            gating,
            w,
        )
        a = lax.ppermute(to_pair, "gx", pair)
        b = lax.ppermute(to_next, "gx", after)
        if step_index < STEPS - 1:
            own, edges = pl.pallas_call(
                between_kernel, out_shape=(plane, edge), in_specs=[VMEM] * 5, out_specs=(VMEM, VMEM)
            )(stay, a, b, labels, block_inverse)
    out = pl.pallas_call(
        end_kernel, out_shape=plane, in_specs=[VMEM] * 4, out_specs=VMEM
    )(stay, a, b, labels)
    return (out[None], w[None])


def solution(mesh):
    return jax.shard_map(
        per_device,
        mesh=mesh,
        in_specs=(
            P("gx", "gy", None),
            P("gx", "gy", None),
            P(None, "gx", "gy", None),
            P(None, "gx", "gy", None),
            P("gx", "gy", None),
            P(),
            P(),
            P(),
            P(),
        ),
        out_specs=(P("gx", "gy", None), P("gx", "gy", None)),
        check_vma=False,
    )
```

```python
import jax
import jax.numpy as jnp
from jax import lax
from jax.experimental import pallas as pl
from jax.experimental.pallas import tpu as pltpu
from jax.sharding import PartitionSpec as P

STEPS = 2
SWEEPS = 11
ZB = 128
LB = 128
HB = 64

TIME_STEP = 0.2
RECOVERY_RATE = 0.25
EXCITATION = 8.0
THRESHOLD = 0.15

BOTH = ("gx", "gy")
VMEM = pl.BlockSpec(memory_space=pltpu.VMEM)
SMEM = pl.BlockSpec(memory_space=pltpu.SMEM)
ROOM = pltpu.CompilerParams(vmem_limit_bytes=8 << 20)


def half_product(field, inv_ref):
    me = lax.axis_index("gy")
    upper = lax.rem(me, 2) == 1
    matrix = inv_ref[lax.div(me, 2)]
    nothing = jnp.zeros_like(field)
    padded = jnp.concatenate(
        [jnp.where(upper, nothing, field), jnp.where(upper, field, nothing)], axis=0
    )
    product = jnp.dot(
        matrix, padded, precision=lax.Precision.HIGHEST, preferred_element_type=jnp.float32
    )
    own = jnp.where(upper, product[HB:], product[:HB])
    inner = jnp.where(upper, product[HB - 1 : HB], product[HB : HB + 1])
    outer = jnp.where(upper, product[ZB - 1 :], product[:1])
    return own, inner, outer


def write_product(field, inv_ref, own_ref, edge_ref):
    own, inner, outer = half_product(field, inv_ref)
    own_ref[...] = own
    row = lax.broadcasted_iota(jnp.int32, edge_ref.shape, 0)
    edge_ref[...] = jnp.where(row == 0, inner, jnp.where(row == 1, outer, 0.0))


def start_kernel(field_ref, inv_ref, own_ref, edge_ref):
    write_product(field_ref[...], inv_ref, own_ref, edge_ref)


def solved_half(own, edges, inv_ref, rate_ref):
    me = lax.axis_index("gy")
    upper = lax.rem(me, 2) == 1
    mine = lax.div(me, 2)
    blocks = inv_ref.shape[0]
    first, last, corner = [], [], []
    for block in range(blocks):
        low = edges[lax.bitwise_xor(2 * block, me)]
        high = edges[lax.bitwise_xor(2 * block + 1, me)]
        top, bottom = inv_ref[block, 0:1], inv_ref[block, ZB - 1 : ZB]
        mid_low, mid_high = inv_ref[block, HB - 1 : HB], inv_ref[block, HB : HB + 1]
        reach_first = top[:, HB : HB + 1] / mid_low[:, HB : HB + 1]
        reach_last = bottom[:, HB - 1 : HB] / mid_high[:, HB - 1 : HB]
        first.append(low[1:2] + reach_first * high[0:1])
        last.append(high[1:2] + reach_last * low[0:1])
        corner.append((top[:, 0:1], top[:, ZB - 1 :], bottom[:, 0:1], bottom[:, ZB - 1 :]))
    zero = jnp.zeros_like(first[0])

    def couple(u_first, u_last):
        below = [zero] + [
            jnp.minimum(rate_ref[b], rate_ref[b + 1]) * u_last[b] for b in range(blocks - 1)
        ]
        above = [
            jnp.minimum(rate_ref[b], rate_ref[b + 1]) * u_first[b + 1] for b in range(blocks - 1)
        ] + [zero]
        return below, above

    u_first, u_last = first, last
    for _ in range(SWEEPS - 1):
        below, above = couple(u_first, u_last)
        u_first = [
            first[b] + corner[b][0] * below[b] + corner[b][1] * above[b] for b in range(blocks)
        ]
        u_last = [
            last[b] + corner[b][2] * below[b] + corner[b][3] * above[b] for b in range(blocks)
        ]
    below, above = couple(u_first, u_last)
    from_below, from_above = below[0], above[0]
    for b in range(1, blocks):
        from_below = jnp.where(mine == b, below[b], from_below)
        from_above = jnp.where(mine == b, above[b], from_above)
    rows = inv_ref[mine, pl.ds(pl.multiple_of(lax.rem(me, 2) * HB, HB), HB), :]
    partner = edges[1][0:1]
    middle = inv_ref[mine, HB - 1 : HB + 1]
    bridge = jnp.where(upper, middle[1:2, HB - 1 : HB], middle[0:1, HB : HB + 1])
    across = jnp.where(upper, rows[:, HB - 1 : HB], rows[:, HB : HB + 1])
    return (
        own
        + across * (partner / bridge)
        + rows[:, 0:1] * from_below
        + rows[:, ZB - 1 :] * from_above
    )


def region_fields(label_ref, axial_ref, shear_ref, width):
    parts = []
    for block in range(width // LB):
        label = jnp.broadcast_to(label_ref[:, block : block + 1], (HB, LB))
        along = jnp.zeros((HB, LB), jnp.float32)
        across, shear = along, along
        for region in range(1, axial_ref.shape[1]):
            here = label == region
            along = jnp.where(here, axial_ref[0, region], along)
            across = jnp.where(here, axial_ref[1, region], across)
            shear = jnp.where(here, shear_ref[region], shear)
        parts.append(((label > 0).astype(jnp.float32), along, across, shear))
    return [jnp.concatenate(p, axis=1) if len(p) > 1 else p[0] for p in zip(*parts)]


def y_neighbours(field):
    width = field.shape[1]
    lane = lax.broadcasted_iota(jnp.int32, field.shape, 1)
    below = jnp.where(lane == 0, 0.0, pltpu.roll(field, 1, 1))
    above = jnp.where(lane == width - 1, 0.0, pltpu.roll(field, width - 1, 1))
    return below, above


def step_kernel(
    count, step, own_ref, *refs
):
    edge_refs = refs[:count]
    (inv_ref, rate_ref, label_ref, axial_ref, shear_ref, voltage_ref, gating_ref, w_ref) = refs[
        count : count + 8
    ]
    stay_ref, pair_ref, next_ref, w_out_ref, edges = refs[count + 8 :]
    for d in range(count):
        edges[d] = edge_refs[d][...]
    solved = solved_half(own_ref[...], edges, inv_ref, rate_ref)
    tissue, along, across, shear = region_fields(label_ref, axial_ref, shear_ref, solved.shape[1])
    voltage = voltage_ref[step].astype(jnp.float32)
    gating = gating_ref[step].astype(jnp.float32)
    slope = (
        EXCITATION
        * (-3.0 * voltage * voltage + 2.0 * (1.0 + THRESHOLD) * voltage - THRESHOLD)
        - gating
    )
    w = w_ref[...]
    flux_x = along * solved
    flux_y = across * solved
    y_below, y_above = y_neighbours(flux_y)
    s_below, s_above = y_neighbours(shear * solved)
    twist = 0.5 * (s_above - s_below)
    spread = y_above - 2.0 * flux_y + y_below - 2.0 * flux_x
    stay_ref[...] = tissue * (
        solved
        + TIME_STEP * spread
        + TIME_STEP * slope * solved
        + TIME_STEP * RECOVERY_RATE * EXCITATION * w
    )
    w_out_ref[...] = tissue * (
        (1.0 - TIME_STEP * RECOVERY_RATE) * w - TIME_STEP * voltage * solved
    )
    even = lax.rem(lax.axis_index("gx"), 2) == 0
    twist = jnp.where(even, -twist, twist)
    pair_ref[...] = TIME_STEP * (flux_x + twist)
    next_ref[...] = TIME_STEP * (flux_x - twist)


def labelled_tissue(label_ref, width):
    parts = [
        jnp.broadcast_to(label_ref[:, b : b + 1], (HB, LB)) > 0 for b in range(width // LB)
    ]
    return jnp.concatenate(parts, axis=1) if len(parts) > 1 else parts[0]


def joined(stay_ref, a_ref, b_ref, label_ref):
    here = labelled_tissue(label_ref, stay_ref.shape[1])
    line = lax.axis_index("gx")
    inside = jnp.logical_and(line > 0, line < lax.axis_size("gx") - 1)
    return stay_ref[...] + jnp.where(
        here, a_ref[...] + jnp.where(inside, b_ref[...], 0.0), 0.0
    )


def between_kernel(stay_ref, a_ref, b_ref, label_ref, inv_ref, own_ref, edge_ref):
    write_product(joined(stay_ref, a_ref, b_ref, label_ref), inv_ref, own_ref, edge_ref)


def end_kernel(stay_ref, a_ref, b_ref, label_ref, out_ref):
    out_ref[...] = joined(stay_ref, a_ref, b_ref, label_ref)


def swaps(lines, lanes, partner):
    found = []
    for i in range(lines):
        for j in range(lanes):
            k, m = partner(i, j)
            found.append((i * lanes + j, k * lanes + m))
    return found


def per_device(
    adj_voltage,
    adj_gating,
    fwd_voltage,
    fwd_gating,
    region_labels,
    region_axial,
    region_shear,
    block_rate,
    block_inverse,
):
    lanes, lines = lax.axis_size("gy"), lax.axis_size("gx")
    _, depth, width = adj_voltage.shape
    assert depth == HB and block_inverse.shape[1] == ZB
    f32 = jnp.float32
    plane = jax.ShapeDtypeStruct((HB, width), f32)
    edge = jax.ShapeDtypeStruct((8, width), f32)
    labels = region_labels[0]
    voltage, gating = fwd_voltage[:, 0], fwd_gating[:, 0]
    own, edges = pl.pallas_call(
        start_kernel, out_shape=(plane, edge), in_specs=[VMEM] * 2, out_specs=(VMEM, VMEM), compiler_params=ROOM
    )(adj_voltage[0], block_inverse)
    w = adj_gating[0]
    ends = (0, lines - 1)
    pair = swaps(lines, lanes, lambda i, j: (i ^ 1, j))
    after = swaps(
        lines, lanes, lambda i, j: (i, j ^ 1) if i in ends else (i - 1 + 2 * (i % 2), j)
    )
    around = [
        swaps(lines, lanes, lambda i, j: (i, j ^ d)) for d in range(1, lanes)
    ]
    for step_index in range(STEPS):
        later = STEPS - 1 - step_index
        all_edges = [edges] + [
            lax.ppermute(edges, BOTH, swap) for swap in around
        ]
        stay, to_pair, to_next, w = pl.pallas_call(
            lambda *refs: step_kernel(lanes, later, *refs),
            out_shape=(plane,) * 4,
            in_specs=[VMEM] * (lanes + 2)
            + [SMEM, VMEM, SMEM, SMEM]
            + [VMEM] * 3,
            out_specs=(VMEM,) * 4,
            compiler_params=ROOM,
            scratch_shapes=[pltpu.VMEM((lanes, 8, width), f32)],
        )(
            own,
            *all_edges,
            block_inverse,
            block_rate,
            labels,
            region_axial,
            region_shear,
            voltage,
            gating,
            w,
        )
        a = lax.ppermute(to_pair, BOTH, pair)
        b = lax.ppermute(to_next, BOTH, after)
        if step_index < STEPS - 1:
            own, edges = pl.pallas_call(
                between_kernel, out_shape=(plane, edge), in_specs=[VMEM] * 5, out_specs=(VMEM, VMEM), compiler_params=ROOM
            )(stay, a, b, labels, block_inverse)
    out = pl.pallas_call(
        end_kernel, out_shape=plane, in_specs=[VMEM] * 4, out_specs=VMEM, compiler_params=ROOM
    )(stay, a, b, labels)
    return (out[None], w[None])


def solution(mesh):
    return jax.shard_map(
        per_device,
        mesh=mesh,
        in_specs=(
            P("gx", "gy", None),
            P("gx", "gy", None),
            P(None, "gx", "gy", None),
            P(None, "gx", "gy", None),
            P("gx", "gy", None),
            P(),
            P(),
            P(),
            P(),
        ),
        out_specs=(P("gx", "gy", None), P("gx", "gy", None)),
        check_vma=False,
    )
```

```python
import jax
import jax.numpy as jnp
from jax import lax
from jax.experimental import pallas as pl
from jax.experimental.pallas import tpu as pltpu
from jax.sharding import PartitionSpec as P

SWEEPS = 11
ZB = 128
LB = 128
HB = 64
SLOTS = 5

TIME_STEP = 0.2
RECOVERY_RATE = 0.25
EXCITATION = 8.0
THRESHOLD = 0.15

BOTH = ("gx", "gy")
VMEM = pl.BlockSpec(memory_space=pltpu.VMEM)
HBM = pl.BlockSpec(memory_space=pltpu.HBM)
F32 = jnp.float32
EDGE_IN, EDGE_OUT, SUM_IN, SUM_OUT, WEIGHTS, SHARED = 0, 1, 2, 3, 4, 7


def gain(voltage, gating):
    slope = (
        EXCITATION
        * (-3.0 * voltage * voltage + 2.0 * (1.0 + THRESHOLD) * voltage - THRESHOLD)
        - gating
    )
    return 1.0 + TIME_STEP * slope


def first_kernel(
    voltage_in, gating_in, fwd_v_in, fwd_g_in, label_in, axial_in, shear_in, rate_in, inverse_in,
    near, far, fwd_v, fwd_g, w, inverse, axial, shear, rate, label, sems,
):
    pairs = [
        (fwd_v_in, fwd_v), (fwd_g_in, fwd_g), (gating_in, w), (label_in, label),
        (voltage_in, near.at[pl.ds(0, HB)]), (voltage_in, far.at[pl.ds(0, HB)]),
        (inverse_in, inverse), (axial_in, axial), (shear_in, shear), (rate_in, rate),
    ]
    copies = [pltpu.make_async_copy(a, b, sems.at[n]) for n, (a, b) in enumerate(pairs)]
    for copy in copies:
        copy.start()
    for copy in copies[:4]:
        copy.wait()
    later = fwd_v.shape[0] - 1
    near[HB : 2 * HB] = gain(fwd_v[later].astype(F32), fwd_g[later].astype(F32))
    near[2 * HB : 3 * HB] = TIME_STEP * RECOVERY_RATE * EXCITATION * w[...]
    blocks = label.shape[0]
    near[3 * HB :] = jnp.zeros((8, near.shape[1]), F32)
    near[3 * HB : 3 * HB + blocks, 0:HB] = label[...].astype(F32)
    far[HB:] = near[3 * HB :]
    for copy in copies[4:]:
        copy.wait()


def half_vectors(inverse, mine, upper):
    def row(index):
        return inverse[mine, index : index + 1, :]

    bridge = row(HB - 1)[:, HB : HB + 1]
    inner = jnp.where(upper, pltpu.roll(row(HB - 1), HB, 1), row(HB)) / bridge
    outer = jnp.where(upper, pltpu.roll(row(ZB - 1), HB, 1), row(0))
    rows = inverse[mine, pl.ds(pl.multiple_of(jnp.where(upper, HB, 0), HB), HB), :]
    swapped = jnp.where(upper, pltpu.roll(rows, HB, 1), rows)
    inner_column = jnp.where(upper, swapped[:, ZB - 1 :], swapped[:, HB : HB + 1]) / bridge
    outer_column = jnp.where(upper, swapped[:, HB - 1 : HB], swapped[:, 0:1])
    return inner, outer, inner_column, outer_column, bridge, swapped[:, :HB]


def y_shifts(plus, minus):
    width = plus.shape[1]
    lane = lax.broadcasted_iota(jnp.int32, plus.shape, 1)
    return jnp.where(lane == width - 1, 0.0, pltpu.roll(plus, width - 1, 1)) + jnp.where(
        lane == 0, 0.0, pltpu.roll(minus, 1, 1)
    )


def stencil(slot, field, center, coef, sign):
    along, across, shear, tissue = coef
    level = TIME_STEP * (across(slot) * field[slot])
    twist = (0.5 * TIME_STEP * sign) * (
        shear(slot + 1) * field[slot + 1] - shear(slot - 1) * field[slot - 1]
    )
    beside = TIME_STEP * (
        along(slot + 1) * field[slot + 1] + along(slot - 1) * field[slot - 1]
    )
    return center * field[slot] + tissue(slot) * (y_shifts(level + twist, level - twist) + beside)


def centre(gains, slot, coef):
    along, across, _, tissue = coef
    return tissue(slot) * gains - (2.0 * TIME_STEP) * (along(slot) + across(slot))


def coefficients(planes):
    return [lambda slot, k=k: planes[k * SLOTS + slot] for k in range(4)]


def orientation():
    line = lax.axis_index("gx")
    return jnp.where(lax.rem(line, 2) == 0, 1.0, -1.0)


def gather_kernel(
    near, pair, after, two_a, two_b, inverse, axial, shear,
    share, solved, centres, partial, planes, rows,
):
    width = near.shape[1]
    label_blocks = width // LB
    line, last = lax.axis_index("gx"), lax.axis_size("gx") - 1
    me = lax.axis_index("gy")
    upper, mine = lax.rem(me, 2) == 1, lax.div(me, 2)
    even = lax.rem(line, 2) == 0
    ahead = jnp.logical_or(lax.rem(line, 4) == 0, lax.rem(line, 4) == 3)
    inside = {
        1: jnp.logical_and(line > 0, line < last),
        4: jnp.where(even, line + 2 <= last, line >= 2),
        0: jnp.where(even, line >= 2, line + 2 <= last),
    }

    def two(first, part):
        a, b = two_a[part], two_b[part]
        return jnp.where(ahead, a, b) if first else jnp.where(ahead, b, a)

    body, tail = pl.ds(0, HB), pl.ds(HB, 8)
    fields = [two(False, body), after[0:HB], near[0:HB], pair[0:HB], two(True, body)]
    labels = [
        two(False, tail), after[3 * HB :], near[3 * HB :], pair[3 * HB :], two(True, tail),
    ]
    rows[...] = jnp.zeros(rows.shape, F32)
    for slot in range(SLOTS):
        label = labels[slot][:label_blocks, :LB]
        if slot in inside:
            label = jnp.where(inside[slot], label, 0.0)
        rows[slot * label_blocks : (slot + 1) * label_blocks] = label
    label = rows[...]
    zero = jnp.zeros(label.shape, F32)
    tables = [zero, zero, zero]
    for region in range(1, axial.shape[1]):
        here = label == float(region)
        for k, value in enumerate(
            (axial[0:1, region : region + 1], axial[1:2, region : region + 1],
             shear[0:1, region : region + 1])
        ):
            tables[k] = jnp.where(here, value, tables[k])
    tables.append((label > 0.0).astype(F32))
    columns = jnp.concatenate(tables, axis=0).T[:HB]
    count = label.shape[0]
    for k in range(4):
        for slot in range(SLOTS):
            for block in range(label_blocks):
                at = k * count + slot * label_blocks + block
                planes[k * SLOTS + slot, :, block * LB : (block + 1) * LB] = jnp.broadcast_to(
                    columns[:, at : at + 1], (HB, LB)
                )
    coef = coefficients(planes)
    sign = orientation()
    inner, outer, inner_column, outer_column, bridge, own = half_vectors(inverse, mine, upper)
    inner_plane = jnp.broadcast_to(inner_column, (HB, width))
    outer_plane = jnp.broadcast_to(outer_column, (HB, width))
    product = jnp.dot(
        own, jnp.concatenate(fields, axis=1),
        precision=lax.Precision.HIGHEST, preferred_element_type=F32,
    )
    parts = [product[:, slot * width : (slot + 1) * width] for slot in range(SLOTS)]
    share[...] = jnp.zeros(share.shape, F32)

    def total(tile, slot, value):
        share[tile, slot : slot + 1, :] = jnp.sum(value, axis=0, keepdims=True)

    for slot in range(SLOTS):
        solved[slot] = parts[slot]
        total(EDGE_IN, slot, bridge * (inner_plane * fields[slot]))
        total(EDGE_OUT, slot, outer_plane * fields[slot])
    weights = (inner_plane * inner_plane, inner_plane * outer_plane, outer_plane * outer_plane)
    sources = {1: after, 2: near, 3: pair}
    for slot in (1, 2, 3):
        gains = sources[slot][HB : 2 * HB]
        lead = sources[slot][2 * HB : 3 * HB]
        center = centre(gains, slot, coef)
        part = stencil(slot, parts, center, coef, sign) + coef[3](slot) * lead
        centres[slot - 1] = center
        partial[slot - 1] = part
        total(SUM_IN, slot, inner_plane * part)
        total(SUM_OUT, slot, outer_plane * part)
        for k, weight in enumerate(weights):
            total(WEIGHTS + k, slot, weight * center)
    if label_blocks == 1:
        lane = lax.broadcasted_iota(jnp.int32, (1, ZB), 1)
        inner = jnp.where(lane < HB, inner, 0.0)
        outer = jnp.where(lane < HB, outer, 0.0)
        vectors = (inner * inner, inner * outer, outer * outer)
        along, across, shears, tissue = tables
        up, down = count - 1, 1
        kinds = (
            across,
            tissue * pltpu.roll(along, up, 0),
            tissue * pltpu.roll(along, down, 0),
            tissue * pltpu.roll(shears, up, 0),
            tissue * pltpu.roll(shears, down, 0),
        )
        lanes = lax.broadcasted_iota(jnp.int32, (8, ZB), 1)
        packed = jnp.zeros((8, ZB), F32)
        for n, kind in enumerate(kinds):
            for k, vector in enumerate(vectors):
                value = jnp.sum(kind * vector, axis=1, keepdims=True)
                packed = jnp.where(lanes == 3 * n + k, value, packed)
        share[SHARED] = packed
    else:
        ones = jnp.ones((HB, width), F32)
        none = jnp.zeros((HB, width), F32)
        for slot in (1, 2, 3):
            here = coef[3](slot)
            kinds = (
                here * y_shifts(coef[1](slot), none),
                here * y_shifts(none, coef[1](slot)),
                here * coef[0](slot + 1),
                here * coef[0](slot - 1),
                here * y_shifts(coef[2](slot + 1), none),
                here * y_shifts(none, coef[2](slot + 1)),
                here * y_shifts(coef[2](slot - 1), none),
                here * y_shifts(none, coef[2](slot - 1)),
            )
            for n, kind in enumerate(kinds):
                for k, weight in enumerate(weights):
                    total(SHARED + 3 * n + k, slot, weight * kind)


def share_tiles(width):
    return SHARED + (1 if width == LB else 24)


def edge_couplings(edge_in, edge_out, inverse, rate, only=None):
    blocks = inverse.shape[0]
    first, last, corner, reach = [], [], [], []
    for b in range(blocks):
        top, bottom = inverse[b, 0:1], inverse[b, ZB - 1 : ZB]
        middle = inverse[b, HB - 1 : HB]
        bridge = middle[:, HB : HB + 1]
        first.append(edge_out[2 * b] + (top[:, HB : HB + 1] / bridge) * edge_in[2 * b + 1])
        last.append(edge_out[2 * b + 1] + (bottom[:, HB - 1 : HB] / bridge) * edge_in[2 * b])
        corner.append((top[:, 0:1], top[:, ZB - 1 :], bottom[:, 0:1], bottom[:, ZB - 1 :]))
        reach.append((middle[:, ZB - 1 :], inverse[b, HB : HB + 1][:, 0:1]))
    links = [jnp.minimum(rate[:, b : b + 1], rate[:, b + 1 : b + 2]) for b in range(blocks - 1)]
    down = [None] + [
        (links[b - 1] * corner[b][0], links[b] * corner[b][1] if b < blocks - 1 else None)
        for b in range(1, blocks)
    ]
    ups = [
        (links[b - 1] * corner[b][2] if b else None, links[b] * corner[b][3])
        for b in range(blocks - 1)
    ]
    u_first, u_last = list(first), list(last)
    for _ in range(SWEEPS - 1):
        n_first, n_last = list(first), list(last)
        for b in range(1, blocks):
            n_first[b] = first[b] + down[b][0] * u_last[b - 1]
            if down[b][1] is not None:
                n_first[b] = n_first[b] + down[b][1] * u_first[b + 1]
        for b in range(blocks - 1):
            n_last[b] = last[b] + ups[b][1] * u_first[b + 1]
            if ups[b][0] is not None:
                n_last[b] = n_last[b] + ups[b][0] * u_last[b - 1]
        u_first, u_last = n_first, n_last
    factors = []
    zero = jnp.zeros_like(first[0])
    for b in range(blocks):
        below = links[b - 1] * u_last[b - 1] if b else zero
        above = links[b] * u_first[b + 1] if b < blocks - 1 else zero
        factors.append((edge_in[2 * b + 1] + reach[b][0] * above, below))
        factors.append((edge_in[2 * b] + reach[b][1] * below, above))
    return factors


def shift_lanes(tile, by):
    width = tile.shape[1]
    lane = lax.broadcasted_iota(jnp.int32, tile.shape, 1)
    if by > 0:
        return jnp.where(lane == width - 1, 0.0, pltpu.roll(tile, width - 1, 1))
    return jnp.where(lane == 0, 0.0, pltpu.roll(tile, 1, 1))


def finish_kernel(halves, *refs):
    shares = refs[:halves]
    (solved, centres, partial, planes, inverse, rate, fwd_v, fwd_g, w_in) = refs[halves : halves + 9]
    out_v, out_w, board = refs[halves + 9 :]
    width = out_v.shape[1]
    me = lax.axis_index("gy")
    upper, mine = lax.rem(me, 2) == 1, lax.div(me, 2)
    sign = orientation()
    for d in range(halves):
        board[d] = shares[d][...]

    def tile(half, which):
        return board[lax.bitwise_xor(half, me), which]

    every = range(halves)
    first = edge_couplings(
        [tile(h, EDGE_IN) for h in every], [tile(h, EDGE_OUT) for h in every], inverse, rate
    )
    _, _, inner_column, outer_column, _, own = half_vectors(inverse, mine, upper)
    inner_plane = jnp.broadcast_to(inner_column, (HB, width))
    outer_plane = jnp.broadcast_to(outer_column, (HB, width))
    coef = coefficients(planes)

    def pick(factors):
        chosen = factors[0]
        for h in range(1, halves):
            chosen = [jnp.where(me == h, new, old) for new, old in zip(factors[h], chosen)]
        return chosen

    alpha, beta = pick(first)
    added = [
        inner_plane * alpha[s : s + 1] + outer_plane * beta[s : s + 1] for s in range(SLOTS)
    ]
    nexts = [
        partial[s - 1] + stencil(s, added, centres[s - 1], coef, sign) for s in (1, 2, 3)
    ]
    product = jnp.dot(
        own, jnp.concatenate(nexts, axis=1),
        precision=lax.Precision.HIGHEST, preferred_element_type=F32,
    )

    rolls = (7, 1)
    sums_in, sums_out = [], []
    half_sign = 0.5 * sign
    for h in every:
        totals = [tile(h, SUM_IN), tile(h, SUM_OUT)]
        if width == LB:
            packed = tile(h, SHARED)

            def shared(kind, k):
                at = 3 * kind + k
                return jnp.broadcast_to(packed[:, at : at + 1], (8, width))

            kinds = [0, 0, 1, 2, 3, 3, 4, 4]
        else:

            def shared(kind, k):
                return tile(h, SHARED + 3 * kind + k)

            kinds = range(8)
        for v, factor in enumerate(first[h]):
            high, low = shift_lanes(factor, 1), shift_lanes(factor, -1)
            up, down = (pltpu.roll(factor, r, 0) for r in rolls)
            up_high, down_high = (pltpu.roll(high, r, 0) for r in rolls)
            up_low, down_low = (pltpu.roll(low, r, 0) for r in rolls)
            for g in range(2):
                k = v + g
                spread = (
                    shared(kinds[2], k) * up
                    + shared(kinds[3], k) * down
                )
                if width == LB:
                    spread = spread + shared(0, k) * (high + low)
                    spread = spread + half_sign * (
                        shared(3, k) * (up_high - up_low) - shared(4, k) * (down_high - down_low)
                    )
                else:
                    spread = spread + shared(0, k) * high + shared(1, k) * low
                    spread = spread + half_sign * (
                        shared(4, k) * up_high - shared(5, k) * up_low
                        - shared(6, k) * down_high + shared(7, k) * down_low
                    )
                totals[g] = totals[g] + tile(h, WEIGHTS + k) * factor + TIME_STEP * spread
        bridge = inverse[h // 2, HB - 1 : HB][:, HB : HB + 1]
        sums_in.append(bridge * totals[0])
        sums_out.append(totals[1])
    alpha, beta = pick(edge_couplings(sums_in, sums_out, inverse, rate))
    final = [None] * SLOTS
    for s in (1, 2, 3):
        final[s] = (
            product[:, (s - 1) * width : s * width]
            + inner_plane * alpha[s : s + 1]
            + outer_plane * beta[s : s + 1]
        )
    tissue = coef[3](2)
    v_late, v_early = fwd_v[1].astype(F32), fwd_v[0].astype(F32)
    w = tissue * (
        (1.0 - TIME_STEP * RECOVERY_RATE) * w_in[...]
        - TIME_STEP * v_late * (solved[2] + added[2])
    )
    center = centre(gain(v_early, fwd_g[0].astype(F32)), 2, coef)
    out_v[...] = (
        stencil(2, final, center, coef, sign)
        + (TIME_STEP * RECOVERY_RATE * EXCITATION) * (tissue * w)
    )
    out_w[...] = tissue * (
        (1.0 - TIME_STEP * RECOVERY_RATE) * w - TIME_STEP * v_early * final[2]
    )


def swaps(lines, lanes, partner):
    found = []
    for i in range(lines):
        for j in range(lanes):
            k, m = partner(i, j)
            found.append((i * lanes + j, k * lanes + m))
    return found


def per_device(
    adj_voltage,
    adj_gating,
    fwd_voltage,
    fwd_gating,
    region_labels,
    region_axial,
    region_shear,
    block_rate,
    block_inverse,
):
    lanes, lines = lax.axis_size("gy"), lax.axis_size("gx")
    _, depth, width = adj_voltage.shape
    label_blocks = region_labels.shape[2]
    assert depth == HB and block_inverse.shape[1] == ZB and lines % 4 == 0
    shape = jax.ShapeDtypeStruct
    room = pltpu.CompilerParams(vmem_limit_bytes=(8 << 20) * (width // LB))
    near, far, fwd_v, fwd_g, w, inverse, axial, shear, rate = pl.pallas_call(
        first_kernel,
        out_shape=(
            shape((3 * HB + 8, width), F32), shape((HB + 8, width), F32),
            shape((2, HB, width), fwd_voltage.dtype), shape((2, HB, width), fwd_gating.dtype),
            shape((HB, width), F32), shape(block_inverse.shape, F32),
            shape(region_axial.shape, F32),
            shape((1,) + region_shear.shape, F32), shape((1,) + block_rate.shape, F32),
        ),
        in_specs=[HBM] * 9,
        out_specs=(VMEM,) * 9,
        scratch_shapes=[pltpu.VMEM((label_blocks, HB), jnp.int32), pltpu.SemaphoreType.DMA((10,))],
        compiler_params=room,
    )(
        *[
            pltpu.with_memory_space_constraint(x, pltpu.HBM)
            for x in (
                adj_voltage[0], adj_gating[0], fwd_voltage[:, 0], fwd_gating[:, 0],
                region_labels[0].T, region_axial, region_shear[None], block_rate[None],
                block_inverse,
            )
        ]
    )
    ends = (0, lines - 1)
    wide = ends + (1, lines - 2)
    pair = lax.ppermute(near, BOTH, swaps(lines, lanes, lambda i, j: (i ^ 1, j)))
    after = lax.ppermute(
        near, BOTH,
        swaps(lines, lanes, lambda i, j: (i, j ^ 1) if i in ends else (i - 1 + 2 * (i % 2), j)),
    )
    two_a = lax.ppermute(far, BOTH, swaps(lines, lanes, lambda i, j: (i ^ 2, j)))
    two_b = lax.ppermute(
        far, BOTH,
        swaps(lines, lanes, lambda i, j: (i ^ 1, j) if i in wide else (((i - 2) ^ 2) + 2, j)),
    )
    count = -(-SLOTS * label_blocks // 8) * 8
    share_shape = (share_tiles(width), 8, width)
    share, solved, centres, partial, planes = pl.pallas_call(
        gather_kernel,
        out_shape=(
            shape(share_shape, F32), shape((SLOTS, HB, width), F32), shape((3, HB, width), F32),
            shape((3, HB, width), F32), shape((4 * SLOTS, HB, width), F32),
        ),
        in_specs=[VMEM] * 8,
        out_specs=(VMEM,) * 5,
        scratch_shapes=[pltpu.VMEM((count, LB), F32)],
        compiler_params=room,
    )(near, pair, after, two_a, two_b, inverse, axial, shear)
    shares = [share] + [
        lax.ppermute(share, BOTH, swaps(lines, lanes, lambda i, j: (i, j ^ d)))
        for d in range(1, lanes)
    ]
    out_v, out_w = pl.pallas_call(
        lambda *refs: finish_kernel(lanes, *refs),
        out_shape=(shape((HB, width), F32),) * 2,
        in_specs=[VMEM] * (lanes + 9),
        out_specs=(VMEM,) * 2,
        scratch_shapes=[pltpu.VMEM((lanes,) + share_shape, F32)],
        compiler_params=room,
    )(*shares, solved, centres, partial, planes, inverse, rate, fwd_v, fwd_g, w)
    return (out_v[None], out_w[None])


def solution(mesh):
    return jax.shard_map(
        per_device,
        mesh=mesh,
        in_specs=(
            P("gx", "gy", None),
            P("gx", "gy", None),
            P(None, "gx", "gy", None),
            P(None, "gx", "gy", None),
            P("gx", "gy", None),
            P(),
            P(),
            P(),
            P(),
        ),
        out_specs=(P("gx", "gy", None), P("gx", "gy", None)),
        check_vma=False,
    )
```

```python
import jax
import jax.numpy as jnp
from jax import lax
from jax.experimental import pallas as pl
from jax.experimental.pallas import tpu as pltpu
from jax.sharding import PartitionSpec as P

SWEEPS = 11
ZB = 128
LB = 128
HB = 64
SLOTS = 5

TIME_STEP = 0.2
RECOVERY_RATE = 0.25
EXCITATION = 8.0
THRESHOLD = 0.15

BOTH = ("gx", "gy")
VMEM = pl.BlockSpec(memory_space=pltpu.VMEM)
HBM = pl.BlockSpec(memory_space=pltpu.HBM)
F32 = jnp.float32
FAR = HB + 8
GAIN, LEAD = slice(FAR, FAR + HB), slice(FAR + HB, FAR + 2 * HB)
EDGE_IN, SUM_IN, EDGE_OUT, SUM_OUT, WEIGHTS, SHARED = 0, 1, 2, 3, 4, 7


def gain(voltage, gating):
    slope = (
        EXCITATION
        * (-3.0 * voltage * voltage + 2.0 * (1.0 + THRESHOLD) * voltage - THRESHOLD)
        - gating
    )
    return 1.0 + TIME_STEP * slope


def first_kernel(
    voltage_in, gating_in, fwd_v_in, fwd_g_in, label_in, axial_in, shear_in, rate_in,
    near, fwd_v, fwd_g, w, axial, shear, rate, label, sems,
):
    pairs = [
        (fwd_v_in, fwd_v), (fwd_g_in, fwd_g), (gating_in, w), (label_in, label),
        (voltage_in, near.at[pl.ds(0, HB)]),
        (axial_in, axial), (shear_in, shear), (rate_in, rate),
    ]
    copies = [pltpu.make_async_copy(a, b, sems.at[n]) for n, (a, b) in enumerate(pairs)]
    for copy in copies:
        copy.start()
    for copy in copies[:4]:
        copy.wait()
    later = fwd_v.shape[0] - 1
    near[GAIN] = gain(fwd_v[later].astype(F32), fwd_g[later].astype(F32))
    near[LEAD] = TIME_STEP * RECOVERY_RATE * EXCITATION * w[...]
    blocks = label.shape[0]
    near[HB : FAR] = jnp.zeros((8, near.shape[1]), F32)
    near[HB : HB + blocks, 0:HB] = label[...].astype(F32)
    for copy in copies[4:]:
        copy.wait()


def half_vectors(inverse, mine, upper):
    def row(index):
        return inverse[mine, index : index + 1, :]

    bridge = row(HB - 1)[:, HB : HB + 1]
    inner = jnp.where(upper, pltpu.roll(row(HB - 1), HB, 1), row(HB)) / bridge
    outer = jnp.where(upper, pltpu.roll(row(ZB - 1), HB, 1), row(0))
    rows = inverse[mine, pl.ds(pl.multiple_of(jnp.where(upper, HB, 0), HB), HB), :]
    swapped = jnp.where(upper, pltpu.roll(rows, HB, 1), rows)
    inner_column = jnp.where(upper, swapped[:, ZB - 1 :], swapped[:, HB : HB + 1]) / bridge
    outer_column = jnp.where(upper, swapped[:, HB - 1 : HB], swapped[:, 0:1])
    return inner, outer, inner_column, outer_column, bridge, swapped[:, :HB]


def y_shifts(plus, minus):
    width = plus.shape[1]
    lane = lax.broadcasted_iota(jnp.int32, plus.shape, 1)
    return jnp.where(lane == width - 1, 0.0, pltpu.roll(plus, width - 1, 1)) + jnp.where(
        lane == 0, 0.0, pltpu.roll(minus, 1, 1)
    )


def stencil(slot, field, center, coef, sign):
    along, across, shear, tissue = coef
    level = TIME_STEP * (across(slot) * field[slot])
    twist = (0.5 * TIME_STEP * sign) * (
        shear(slot + 1) * field[slot + 1] - shear(slot - 1) * field[slot - 1]
    )
    beside = TIME_STEP * (
        along(slot + 1) * field[slot + 1] + along(slot - 1) * field[slot - 1]
    )
    return center * field[slot] + tissue(slot) * (y_shifts(level + twist, level - twist) + beside)


def centre(gains, slot, coef):
    along, across, _, tissue = coef
    return tissue(slot) * gains - (2.0 * TIME_STEP) * (along(slot) + across(slot))


def coefficients(planes):
    return [lambda slot, k=k: planes[k * SLOTS + slot] for k in range(4)]


def orientation():
    line = lax.axis_index("gx")
    return jnp.where(lax.rem(line, 2) == 0, 1.0, -1.0)


def gather_kernel(
    near, pair, after, before, beyond, inverse, axial, shear,
    share, solved, centres, partial, planes, rows,
):
    width = near.shape[1]
    label_blocks = width // LB
    line, last = lax.axis_index("gx"), lax.axis_size("gx") - 1
    me = lax.axis_index("gy")
    upper, mine = lax.rem(me, 2) == 1, lax.div(me, 2)
    even = lax.rem(line, 2) == 0
    inside = {
        1: jnp.logical_and(line > 0, line < last),
        4: jnp.where(even, line + 2 <= last, line >= 2),
        0: jnp.where(even, line >= 2, line + 2 <= last),
    }

    given = (before, after, near, pair, beyond)
    fields = [ref[0:HB] for ref in given]
    rows[...] = jnp.zeros(rows.shape, F32)
    for slot in range(SLOTS):
        label = given[slot][HB : HB + label_blocks, :LB]
        if slot in inside:
            label = jnp.where(inside[slot], label, 0.0)
        rows[slot * label_blocks : (slot + 1) * label_blocks] = label
    label = rows[...]
    zero = jnp.zeros(label.shape, F32)
    tables = [zero, zero, zero]
    for region in range(1, axial.shape[1]):
        here = label == float(region)
        for k, value in enumerate(
            (axial[0:1, region : region + 1], axial[1:2, region : region + 1],
             shear[0:1, region : region + 1])
        ):
            tables[k] = jnp.where(here, value, tables[k])
    tables.append((label > 0.0).astype(F32))
    columns = jnp.concatenate(tables, axis=0).T[:HB]
    count = label.shape[0]
    for k in range(4):
        for slot in range(SLOTS):
            for block in range(label_blocks):
                at = k * count + slot * label_blocks + block
                planes[k * SLOTS + slot, :, block * LB : (block + 1) * LB] = jnp.broadcast_to(
                    columns[:, at : at + 1], (HB, LB)
                )
    coef = coefficients(planes)
    sign = orientation()
    inner, outer, inner_column, outer_column, bridge, own = half_vectors(inverse, mine, upper)
    inner_plane = jnp.broadcast_to(inner_column, (HB, width))
    outer_plane = jnp.broadcast_to(outer_column, (HB, width))
    product = jnp.dot(
        own, jnp.concatenate(fields, axis=1),
        precision=lax.Precision.HIGHEST, preferred_element_type=F32,
    )
    parts = [product[:, slot * width : (slot + 1) * width] for slot in range(SLOTS)]
    share[...] = jnp.zeros(share.shape, F32)

    def total(kind, slot, value):
        row = slot + 4 * (kind % 2)
        share[kind // 2, row : row + 1, :] = jnp.sum(value, axis=0, keepdims=True)

    for slot in range(SLOTS):
        solved[slot] = parts[slot]
        total(EDGE_IN, slot, bridge * (inner_plane * fields[slot]))
        total(EDGE_OUT, slot, outer_plane * fields[slot])
    weights = (inner_plane * inner_plane, inner_plane * outer_plane, outer_plane * outer_plane)
    for slot in (1, 2, 3):
        gains = given[slot][GAIN]
        lead = given[slot][LEAD]
        center = centre(gains, slot, coef)
        part = stencil(slot, parts, center, coef, sign) + coef[3](slot) * lead
        centres[slot - 1] = center
        partial[slot - 1] = part
        total(SUM_IN, slot, inner_plane * part)
        total(SUM_OUT, slot, outer_plane * part)
        for k, weight in enumerate(weights):
            total(WEIGHTS + k, slot, weight * center)
    if label_blocks == 1:
        lane = lax.broadcasted_iota(jnp.int32, (1, ZB), 1)
        inner = jnp.where(lane < HB, inner, 0.0)
        outer = jnp.where(lane < HB, outer, 0.0)
        vectors = (inner * inner, inner * outer, outer * outer)
        along, across, shears, tissue = tables
        up, down = count - 1, 1
        kinds = (
            across,
            tissue * pltpu.roll(along, up, 0),
            tissue * pltpu.roll(along, down, 0),
            tissue * pltpu.roll(shears, up, 0),
            tissue * pltpu.roll(shears, down, 0),
        )
        lanes = lax.broadcasted_iota(jnp.int32, (8, ZB), 1)
        packed = jnp.zeros((8, ZB), F32)
        for n, kind in enumerate(kinds):
            for k, vector in enumerate(vectors):
                value = jnp.sum(kind * vector, axis=1, keepdims=True)
                packed = jnp.where(lanes == 3 * n + k, value, packed)
        share[SHARED // 2, 5:8] = packed[1:4]
    else:
        ones = jnp.ones((HB, width), F32)
        none = jnp.zeros((HB, width), F32)
        for slot in (1, 2, 3):
            here = coef[3](slot)
            kinds = (
                here * y_shifts(coef[1](slot), none),
                here * y_shifts(none, coef[1](slot)),
                here * coef[0](slot + 1),
                here * coef[0](slot - 1),
                here * y_shifts(coef[2](slot + 1), none),
                here * y_shifts(none, coef[2](slot + 1)),
                here * y_shifts(coef[2](slot - 1), none),
                here * y_shifts(none, coef[2](slot - 1)),
            )
            for n, kind in enumerate(kinds):
                for k, weight in enumerate(weights):
                    total(SHARED + 3 * n + k, slot, weight * kind)


def share_tiles(width):
    return -(-(SHARED + (1 if width == LB else 24)) // 2)


def edge_couplings(edge_in, edge_out, inverse, rate, only=None):
    blocks = inverse.shape[0]
    first, last, corner, reach = [], [], [], []
    for b in range(blocks):
        top, bottom = inverse[b, 0:1], inverse[b, ZB - 1 : ZB]
        middle = inverse[b, HB - 1 : HB]
        bridge = middle[:, HB : HB + 1]
        first.append(edge_out[2 * b] + (top[:, HB : HB + 1] / bridge) * edge_in[2 * b + 1])
        last.append(edge_out[2 * b + 1] + (bottom[:, HB - 1 : HB] / bridge) * edge_in[2 * b])
        corner.append((top[:, 0:1], top[:, ZB - 1 :], bottom[:, 0:1], bottom[:, ZB - 1 :]))
        reach.append((middle[:, ZB - 1 :], inverse[b, HB : HB + 1][:, 0:1]))
    links = [jnp.minimum(rate[:, b : b + 1], rate[:, b + 1 : b + 2]) for b in range(blocks - 1)]
    down = [None] + [
        (links[b - 1] * corner[b][0], links[b] * corner[b][1] if b < blocks - 1 else None)
        for b in range(1, blocks)
    ]
    ups = [
        (links[b - 1] * corner[b][2] if b else None, links[b] * corner[b][3])
        for b in range(blocks - 1)
    ]
    u_first, u_last = list(first), list(last)
    for _ in range(SWEEPS - 1):
        n_first, n_last = list(first), list(last)
        for b in range(1, blocks):
            n_first[b] = first[b] + down[b][0] * u_last[b - 1]
            if down[b][1] is not None:
                n_first[b] = n_first[b] + down[b][1] * u_first[b + 1]
        for b in range(blocks - 1):
            n_last[b] = last[b] + ups[b][1] * u_first[b + 1]
            if ups[b][0] is not None:
                n_last[b] = n_last[b] + ups[b][0] * u_last[b - 1]
        u_first, u_last = n_first, n_last
    factors = []
    zero = jnp.zeros_like(first[0])
    for b in range(blocks):
        below = links[b - 1] * u_last[b - 1] if b else zero
        above = links[b] * u_first[b + 1] if b < blocks - 1 else zero
        factors.append((edge_in[2 * b + 1] + reach[b][0] * above, below))
        factors.append((edge_in[2 * b] + reach[b][1] * below, above))
    return factors


def shift_lanes(tile, by):
    width = tile.shape[1]
    lane = lax.broadcasted_iota(jnp.int32, tile.shape, 1)
    if by > 0:
        return jnp.where(lane == width - 1, 0.0, pltpu.roll(tile, width - 1, 1))
    return jnp.where(lane == 0, 0.0, pltpu.roll(tile, 1, 1))


def finish_kernel(halves, *refs):
    shares = refs[:halves]
    (solved, centres, partial, planes, inverse, rate, fwd_v, fwd_g, w_in) = refs[halves : halves + 9]
    out_v, out_w, board = refs[halves + 9 :]
    width = out_v.shape[1]
    me = lax.axis_index("gy")
    upper, mine = lax.rem(me, 2) == 1, lax.div(me, 2)
    sign = orientation()
    for d in range(halves):
        board[d] = shares[d][...]

    def tile(half, kind):
        found = board[lax.bitwise_xor(half, me), kind // 2]
        return pltpu.roll(found, 4, 0) if kind % 2 else found

    every = range(halves)
    first = edge_couplings(
        [tile(h, EDGE_IN) for h in every], [tile(h, EDGE_OUT) for h in every], inverse, rate
    )
    _, _, inner_column, outer_column, _, own = half_vectors(inverse, mine, upper)
    inner_plane = jnp.broadcast_to(inner_column, (HB, width))
    outer_plane = jnp.broadcast_to(outer_column, (HB, width))
    coef = coefficients(planes)

    def pick(factors):
        chosen = factors[0]
        for h in range(1, halves):
            chosen = [jnp.where(me == h, new, old) for new, old in zip(factors[h], chosen)]
        return chosen

    alpha, beta = pick(first)
    added = [
        inner_plane * alpha[s : s + 1] + outer_plane * beta[s : s + 1] for s in range(SLOTS)
    ]
    nexts = [
        partial[s - 1] + stencil(s, added, centres[s - 1], coef, sign) for s in (1, 2, 3)
    ]
    product = jnp.dot(
        own, jnp.concatenate(nexts, axis=1),
        precision=lax.Precision.HIGHEST, preferred_element_type=F32,
    )

    rolls = (7, 1)
    sums_in, sums_out = [], []
    half_sign = 0.5 * sign
    for h in every:
        totals = [tile(h, SUM_IN), tile(h, SUM_OUT)]
        if width == LB:
            packed = tile(h, SHARED)

            def shared(kind, k):
                at = 3 * kind + k
                return jnp.broadcast_to(packed[:, at : at + 1], (8, width))

            kinds = [0, 0, 1, 2, 3, 3, 4, 4]
        else:

            def shared(kind, k):
                return tile(h, SHARED + 3 * kind + k)

            kinds = range(8)
        for v, factor in enumerate(first[h]):
            high, low = shift_lanes(factor, 1), shift_lanes(factor, -1)
            up, down = (pltpu.roll(factor, r, 0) for r in rolls)
            up_high, down_high = (pltpu.roll(high, r, 0) for r in rolls)
            up_low, down_low = (pltpu.roll(low, r, 0) for r in rolls)
            for g in range(2):
                k = v + g
                spread = (
                    shared(kinds[2], k) * up
                    + shared(kinds[3], k) * down
                )
                if width == LB:
                    spread = spread + shared(0, k) * (high + low)
                    spread = spread + half_sign * (
                        shared(3, k) * (up_high - up_low) - shared(4, k) * (down_high - down_low)
                    )
                else:
                    spread = spread + shared(0, k) * high + shared(1, k) * low
                    spread = spread + half_sign * (
                        shared(4, k) * up_high - shared(5, k) * up_low
                        - shared(6, k) * down_high + shared(7, k) * down_low
                    )
                totals[g] = totals[g] + tile(h, WEIGHTS + k) * factor + TIME_STEP * spread
        bridge = inverse[h // 2, HB - 1 : HB][:, HB : HB + 1]
        sums_in.append(bridge * totals[0])
        sums_out.append(totals[1])
    alpha, beta = pick(edge_couplings(sums_in, sums_out, inverse, rate))
    final = [None] * SLOTS
    for s in (1, 2, 3):
        final[s] = (
            product[:, (s - 1) * width : s * width]
            + inner_plane * alpha[s : s + 1]
            + outer_plane * beta[s : s + 1]
        )
    tissue = coef[3](2)
    v_late, v_early = fwd_v[1].astype(F32), fwd_v[0].astype(F32)
    w = tissue * (
        (1.0 - TIME_STEP * RECOVERY_RATE) * w_in[...]
        - TIME_STEP * v_late * (solved[2] + added[2])
    )
    center = centre(gain(v_early, fwd_g[0].astype(F32)), 2, coef)
    out_v[...] = (
        stencil(2, final, center, coef, sign)
        + (TIME_STEP * RECOVERY_RATE * EXCITATION) * (tissue * w)
    )
    out_w[...] = tissue * (
        (1.0 - TIME_STEP * RECOVERY_RATE) * w - TIME_STEP * v_early * final[2]
    )


def swaps(lines, lanes, partner):
    found = []
    for i in range(lines):
        for j in range(lanes):
            k, m = partner(i, j)
            found.append((i * lanes + j, k * lanes + m))
    return found


def per_device(
    adj_voltage,
    adj_gating,
    fwd_voltage,
    fwd_gating,
    region_labels,
    region_axial,
    region_shear,
    block_rate,
    block_inverse,
):
    lanes, lines = lax.axis_size("gy"), lax.axis_size("gx")
    _, depth, width = adj_voltage.shape
    label_blocks = region_labels.shape[2]
    assert depth == HB and block_inverse.shape[1] == ZB and lines % 4 == 0
    shape = jax.ShapeDtypeStruct
    room = pltpu.CompilerParams(vmem_limit_bytes=(8 << 20) * (width // LB))
    near, fwd_v, fwd_g, w, axial, shear, rate = pl.pallas_call(
        first_kernel,
        out_shape=(
            shape((3 * HB + 8, width), F32),
            shape((2, HB, width), fwd_voltage.dtype), shape((2, HB, width), fwd_gating.dtype),
            shape((HB, width), F32), shape(region_axial.shape, F32),
            shape((1,) + region_shear.shape, F32), shape((1,) + block_rate.shape, F32),
        ),
        in_specs=[HBM] * 8,
        out_specs=(VMEM,) * 7,
        scratch_shapes=[pltpu.VMEM((label_blocks, HB), jnp.int32), pltpu.SemaphoreType.DMA((8,))],
        compiler_params=room,
    )(
        *[
            pltpu.with_memory_space_constraint(x, pltpu.HBM)
            for x in (
                adj_voltage[0], adj_gating[0], fwd_voltage[:, 0], fwd_gating[:, 0],
                region_labels[0].T, region_axial, region_shear[None], block_rate[None],
            )
        ]
    )
    ends = (0, lines - 1)
    cycle = list(range(0, lines, 2)) + list(range(lines - 1, 0, -2))
    onward = {i: cycle[(n + 1) % lines] for n, i in enumerate(cycle)}
    pairing = swaps(lines, lanes, lambda i, j: (i ^ 1, j))
    after = lax.ppermute(
        near, BOTH,
        swaps(lines, lanes, lambda i, j: (i, j ^ 1) if i in ends else (i - 1 + 2 * (i % 2), j)),
    )
    before = lax.ppermute(near, BOTH, swaps(lines, lanes, lambda i, j: (onward[i], j)))
    pair = lax.ppermute(near, BOTH, pairing)
    beyond = lax.ppermute(after[:FAR], BOTH, pairing)
    count = -(-SLOTS * label_blocks // 8) * 8
    share_shape = (share_tiles(width), 8, width)
    share, solved, centres, partial, planes = pl.pallas_call(
        gather_kernel,
        out_shape=(
            shape(share_shape, F32), shape((SLOTS, HB, width), F32), shape((3, HB, width), F32),
            shape((3, HB, width), F32), shape((4 * SLOTS, HB, width), F32),
        ),
        in_specs=[VMEM] * 8,
        out_specs=(VMEM,) * 5,
        scratch_shapes=[pltpu.VMEM((count, LB), F32)],
        compiler_params=room,
    )(near, pair, after, before, beyond, block_inverse, axial, shear)
    shares = [share] + [
        lax.ppermute(share, BOTH, swaps(lines, lanes, lambda i, j: (i, j ^ d)))
        for d in range(1, lanes)
    ]
    out_v, out_w = pl.pallas_call(
        lambda *refs: finish_kernel(lanes, *refs),
        out_shape=(shape((HB, width), F32),) * 2,
        in_specs=[VMEM] * (lanes + 9),
        out_specs=(VMEM,) * 2,
        scratch_shapes=[pltpu.VMEM((lanes,) + share_shape, F32)],
        compiler_params=room,
    )(
        *shares, solved, centres, partial, planes, block_inverse, rate, fwd_v, fwd_g, w
    )
    return (out_v[None], out_w[None])


def solution(mesh):
    return jax.shard_map(
        per_device,
        mesh=mesh,
        in_specs=(
            P("gx", "gy", None),
            P("gx", "gy", None),
            P(None, "gx", "gy", None),
            P(None, "gx", "gy", None),
            P("gx", "gy", None),
            P(),
            P(),
            P(),
            P(),
        ),
        out_specs=(P("gx", "gy", None), P("gx", "gy", None)),
        check_vma=False,
    )
```

```python
import jax
import jax.numpy as jnp
from jax import lax
from jax.experimental import pallas as pl
from jax.experimental.pallas import tpu as pltpu
from jax.sharding import PartitionSpec as P

SWEEPS = 11
ZB = 128
LB = 128
HB = 64
SLOTS = 5

TIME_STEP = 0.2
RECOVERY_RATE = 0.25
EXCITATION = 8.0
THRESHOLD = 0.15

BOTH = ("gx", "gy")
VMEM = pl.BlockSpec(memory_space=pltpu.VMEM)
HBM = pl.BlockSpec(memory_space=pltpu.HBM)
F32 = jnp.float32
FAR = HB + 8
GAIN, LEAD = pl.ds(FAR, HB), pl.ds(FAR + HB, HB)
EDGE_IN, SUM_IN, EDGE_OUT, SUM_OUT, WEIGHTS, SHARED = 0, 1, 2, 3, 4, 7


def gain(voltage, gating):
    slope = (
        EXCITATION
        * (-3.0 * voltage * voltage + 2.0 * (1.0 + THRESHOLD) * voltage - THRESHOLD)
        - gating
    )
    return 1.0 + TIME_STEP * slope


def start_copies(pairs, sems):
    copies = [pltpu.make_async_copy(a, b, sems.at[n]) for n, (a, b) in enumerate(pairs)]
    for copy in copies:
        copy.start()
    return copies


def first_kernel(voltage_in, gating_in, fwd_v_in, fwd_g_in, label_in, near, v, g, label, sems):
    later = fwd_v_in.shape[0] - 1
    copies = start_copies(
        [
            (fwd_v_in.at[later], v), (fwd_g_in.at[later], g), (label_in, label),
            (gating_in, near.at[LEAD]), (voltage_in, near.at[pl.ds(0, HB)]),
        ],
        sems,
    )
    for copy in copies[:3]:
        copy.wait()
    near[GAIN] = gain(v[...].astype(F32), g[...].astype(F32))
    blocks = label.shape[0]
    near[HB:FAR] = jnp.zeros((8, near.shape[1]), F32)
    near[HB : HB + blocks, 0:HB] = label[...].astype(F32)
    for copy in copies[3:]:
        copy.wait()


def lookup(label, axial, shear):
    zero = jnp.zeros(label.shape, F32)
    tables = [zero, zero, zero]
    for region in range(1, axial.shape[1]):
        here = label == float(region)
        for k, value in enumerate(
            (axial[0:1, region : region + 1], axial[1:2, region : region + 1],
             shear[0:1, region : region + 1])
        ):
            tables[k] = jnp.where(here, value, tables[k])
    tables.append((label > 0.0).astype(F32))
    return tables


def fill_plane(plane, columns, at, label_blocks):
    for block in range(label_blocks):
        plane[:, block * LB : (block + 1) * LB] = jnp.broadcast_to(
            columns[:, at + block : at + block + 1], (HB, LB)
        )


def aside_kernel(
    near, gating_in, fwd_v_in, fwd_g_in, axial_in, shear_in, rate_in, inverse_in,
    axial, shear, rate, inverse, vectors, own, lines, planes, early, w, v, g, label, sems,
):
    width = w.shape[1]
    label_blocks = width // LB
    me = lax.axis_index("gy")
    upper, mine = lax.rem(me, 2) == 1, lax.div(me, 2)
    for copy in start_copies(
        [
            (inverse_in, inverse), (axial_in, axial), (shear_in, shear), (rate_in, rate),
            (gating_in, w), (fwd_v_in, v), (fwd_g_in, g),
        ],
        sems,
    ):
        copy.wait()
    inner, outer, inner_column, outer_column, bridge, square = half_vectors(inverse, mine, upper)
    vectors[0] = jnp.broadcast_to(inner_column, (HB, width))
    vectors[1] = jnp.broadcast_to(outer_column, (HB, width))
    own[...] = square
    lines[0:1] = inner
    lines[1:2] = outer
    lines[2:3] = jnp.broadcast_to(bridge, (1, ZB))
    label[...] = jnp.zeros(label.shape, F32)
    label[0:label_blocks] = near[HB : HB + label_blocks, :LB]
    columns = jnp.concatenate(lookup(label[...], axial, shear), axis=0).T[:HB]
    for k in range(4):
        fill_plane(planes.at[k], columns, 8 * k, label_blocks)
    tissue = planes[3]
    late_v, early_v = v[1].astype(F32), v[0].astype(F32)
    early[0] = (1.0 - TIME_STEP * RECOVERY_RATE) * (tissue * w[...])
    early[1] = TIME_STEP * (tissue * late_v)
    early[2] = TIME_STEP * (tissue * early_v)
    early[3] = tissue * gain(early_v, g[0].astype(F32)) - (2.0 * TIME_STEP) * (
        planes[0] + planes[1]
    )


def half_vectors(inverse, mine, upper):
    def row(index):
        return inverse[mine, index : index + 1, :]

    bridge = row(HB - 1)[:, HB : HB + 1]
    inner = jnp.where(upper, pltpu.roll(row(HB - 1), HB, 1), row(HB)) / bridge
    outer = jnp.where(upper, pltpu.roll(row(ZB - 1), HB, 1), row(0))
    rows = inverse[mine, pl.ds(pl.multiple_of(jnp.where(upper, HB, 0), HB), HB), :]
    swapped = jnp.where(upper, pltpu.roll(rows, HB, 1), rows)
    inner_column = jnp.where(upper, swapped[:, ZB - 1 :], swapped[:, HB : HB + 1]) / bridge
    outer_column = jnp.where(upper, swapped[:, HB - 1 : HB], swapped[:, 0:1])
    return inner, outer, inner_column, outer_column, bridge, swapped[:, :HB]


def y_shifts(plus, minus):
    width = plus.shape[1]
    lane = lax.broadcasted_iota(jnp.int32, plus.shape, 1)
    return jnp.where(lane == width - 1, 0.0, pltpu.roll(plus, width - 1, 1)) + jnp.where(
        lane == 0, 0.0, pltpu.roll(minus, 1, 1)
    )


def stencil(slot, field, center, coef, sign):
    along, across, shear, tissue = coef
    level = TIME_STEP * (across(slot) * field[slot])
    twist = (0.5 * TIME_STEP * sign) * (
        shear(slot + 1) * field[slot + 1] - shear(slot - 1) * field[slot - 1]
    )
    beside = TIME_STEP * (
        along(slot + 1) * field[slot + 1] + along(slot - 1) * field[slot - 1]
    )
    return center * field[slot] + tissue(slot) * (y_shifts(level + twist, level - twist) + beside)


def centre(gains, slot, coef):
    along, across, _, tissue = coef
    return tissue(slot) * gains - (2.0 * TIME_STEP) * (along(slot) + across(slot))


def coefficients(planes, here):
    return [
        lambda slot, k=k: here[k] if slot == 2 else planes[k * SLOTS + slot] for k in range(4)
    ]


def orientation():
    line = lax.axis_index("gx")
    return jnp.where(lax.rem(line, 2) == 0, 1.0, -1.0)


def gather_kernel(
    near, pair, after, before, beyond, axial, shear, vectors, own, lines, here,
    share, solved, centres, partial, planes, rows,
):
    width = near.shape[1]
    label_blocks = width // LB
    line, last = lax.axis_index("gx"), lax.axis_size("gx") - 1
    even = lax.rem(line, 2) == 0
    inside = {
        1: jnp.logical_and(line > 0, line < last),
        4: jnp.where(even, line + 2 <= last, line >= 2),
        0: jnp.where(even, line >= 2, line + 2 <= last),
    }

    given = (before, after, near, pair, beyond)
    fields = [ref[0:HB] for ref in given]
    rows[...] = jnp.zeros(rows.shape, F32)
    for slot in range(SLOTS):
        label = given[slot][HB : HB + label_blocks, :LB]
        if slot in inside:
            label = jnp.where(inside[slot], label, 0.0)
        rows[slot * label_blocks : (slot + 1) * label_blocks] = label
    tables = lookup(rows[...], axial, shear)
    columns = jnp.concatenate(tables, axis=0).T[:HB]
    count = rows.shape[0]
    for k in range(4):
        for slot in range(SLOTS):
            if slot == 2 or (slot in (0, 4) and k in (1, 3)):
                continue
            fill_plane(planes.at[k * SLOTS + slot], columns, k * count + slot * label_blocks, label_blocks)
    coef = coefficients(planes, here)
    sign = orientation()
    inner, outer, bridge = lines[0:1], lines[1:2], lines[2:3, 0:1]
    inner_plane, outer_plane = vectors[0], vectors[1]
    product = jnp.dot(
        own[...], jnp.concatenate(fields, axis=1),
        precision=lax.Precision.HIGHEST, preferred_element_type=F32,
    )
    parts = [product[:, slot * width : (slot + 1) * width] for slot in range(SLOTS)]
    share[...] = jnp.zeros(share.shape, F32)

    def total(kind, slot, value):
        row = slot + 4 * (kind % 2)
        share[kind // 2, row : row + 1, :] = jnp.sum(value, axis=0, keepdims=True)

    for slot in range(SLOTS):
        solved[slot] = parts[slot]
        total(EDGE_IN, slot, bridge * (inner_plane * fields[slot]))
        total(EDGE_OUT, slot, outer_plane * fields[slot])
    weights = (inner_plane * inner_plane, inner_plane * outer_plane, outer_plane * outer_plane)
    for slot in (1, 2, 3):
        gains = given[slot][GAIN]
        lead = given[slot][LEAD]
        center = centre(gains, slot, coef)
        part = stencil(slot, parts, center, coef, sign) + coef[3](slot) * ((TIME_STEP * RECOVERY_RATE * EXCITATION) * lead)
        centres[slot - 1] = center
        partial[slot - 1] = part
        total(SUM_IN, slot, inner_plane * part)
        total(SUM_OUT, slot, outer_plane * part)
        for k, weight in enumerate(weights):
            total(WEIGHTS + k, slot, weight * center)
    if label_blocks == 1:
        lane = lax.broadcasted_iota(jnp.int32, (1, ZB), 1)
        inner = jnp.where(lane < HB, inner, 0.0)
        outer = jnp.where(lane < HB, outer, 0.0)
        pairs = (inner * inner, inner * outer, outer * outer)
        along, across, shears, tissue = tables
        up, down = count - 1, 1
        kinds = (
            across,
            tissue * pltpu.roll(along, up, 0),
            tissue * pltpu.roll(along, down, 0),
            tissue * pltpu.roll(shears, up, 0),
            tissue * pltpu.roll(shears, down, 0),
        )
        lanes = lax.broadcasted_iota(jnp.int32, (8, ZB), 1)
        packed = jnp.zeros((8, ZB), F32)
        for n, kind in enumerate(kinds):
            for k, vector in enumerate(pairs):
                value = jnp.sum(kind * vector, axis=1, keepdims=True)
                packed = jnp.where(lanes == 3 * n + k, value, packed)
        share[SHARED // 2, 5:8] = packed[1:4]
    else:
        ones = jnp.ones((HB, width), F32)
        none = jnp.zeros((HB, width), F32)
        for slot in (1, 2, 3):
            here = coef[3](slot)
            kinds = (
                here * y_shifts(coef[1](slot), none),
                here * y_shifts(none, coef[1](slot)),
                here * coef[0](slot + 1),
                here * coef[0](slot - 1),
                here * y_shifts(coef[2](slot + 1), none),
                here * y_shifts(none, coef[2](slot + 1)),
                here * y_shifts(coef[2](slot - 1), none),
                here * y_shifts(none, coef[2](slot - 1)),
            )
            for n, kind in enumerate(kinds):
                for k, weight in enumerate(weights):
                    total(SHARED + 3 * n + k, slot, weight * kind)


def share_tiles(width):
    return -(-(SHARED + (1 if width == LB else 24)) // 2)


def edge_couplings(edge_in, edge_out, inverse, rate, only=None):
    blocks = inverse.shape[0]
    first, last, corner, reach = [], [], [], []
    for b in range(blocks):
        top, bottom = inverse[b, 0:1], inverse[b, ZB - 1 : ZB]
        middle = inverse[b, HB - 1 : HB]
        bridge = middle[:, HB : HB + 1]
        first.append(edge_out[2 * b] + (top[:, HB : HB + 1] / bridge) * edge_in[2 * b + 1])
        last.append(edge_out[2 * b + 1] + (bottom[:, HB - 1 : HB] / bridge) * edge_in[2 * b])
        corner.append((top[:, 0:1], top[:, ZB - 1 :], bottom[:, 0:1], bottom[:, ZB - 1 :]))
        reach.append((middle[:, ZB - 1 :], inverse[b, HB : HB + 1][:, 0:1]))
    links = [jnp.minimum(rate[:, b : b + 1], rate[:, b + 1 : b + 2]) for b in range(blocks - 1)]
    down = [None] + [
        (links[b - 1] * corner[b][0], links[b] * corner[b][1] if b < blocks - 1 else None)
        for b in range(1, blocks)
    ]
    ups = [
        (links[b - 1] * corner[b][2] if b else None, links[b] * corner[b][3])
        for b in range(blocks - 1)
    ]
    u_first, u_last = list(first), list(last)
    for _ in range(SWEEPS - 1):
        n_first, n_last = list(first), list(last)
        for b in range(1, blocks):
            n_first[b] = first[b] + down[b][0] * u_last[b - 1]
            if down[b][1] is not None:
                n_first[b] = n_first[b] + down[b][1] * u_first[b + 1]
        for b in range(blocks - 1):
            n_last[b] = last[b] + ups[b][1] * u_first[b + 1]
            if ups[b][0] is not None:
                n_last[b] = n_last[b] + ups[b][0] * u_last[b - 1]
        u_first, u_last = n_first, n_last
    factors = []
    zero = jnp.zeros_like(first[0])
    for b in range(blocks):
        below = links[b - 1] * u_last[b - 1] if b else zero
        above = links[b] * u_first[b + 1] if b < blocks - 1 else zero
        factors.append((edge_in[2 * b + 1] + reach[b][0] * above, below))
        factors.append((edge_in[2 * b] + reach[b][1] * below, above))
    return factors


def shift_lanes(tile, by):
    width = tile.shape[1]
    lane = lax.broadcasted_iota(jnp.int32, tile.shape, 1)
    if by > 0:
        return jnp.where(lane == width - 1, 0.0, pltpu.roll(tile, width - 1, 1))
    return jnp.where(lane == 0, 0.0, pltpu.roll(tile, 1, 1))


def finish_kernel(halves, *refs):
    shares = refs[:halves]
    (solved, centres, partial, planes, here, vectors, own, early, inverse, rate) = refs[
        halves : halves + 10
    ]
    out_v, out_w, board = refs[halves + 10 :]
    width = out_v.shape[1]
    me = lax.axis_index("gy")
    sign = orientation()
    for d in range(halves):
        board[d] = shares[d][...]

    def tile(half, kind):
        found = board[lax.bitwise_xor(half, me), kind // 2]
        return pltpu.roll(found, 4, 0) if kind % 2 else found

    every = range(halves)
    first = edge_couplings(
        [tile(h, EDGE_IN) for h in every], [tile(h, EDGE_OUT) for h in every], inverse, rate
    )
    inner_plane, outer_plane = vectors[0], vectors[1]
    coef = coefficients(planes, here)

    def pick(factors):
        chosen = factors[0]
        for h in range(1, halves):
            chosen = [jnp.where(me == h, new, old) for new, old in zip(factors[h], chosen)]
        return chosen

    alpha, beta = pick(first)
    added = [
        inner_plane * alpha[s : s + 1] + outer_plane * beta[s : s + 1] for s in range(SLOTS)
    ]
    nexts = [
        partial[s - 1] + stencil(s, added, centres[s - 1], coef, sign) for s in (1, 2, 3)
    ]
    product = jnp.dot(
        own[...], jnp.concatenate(nexts, axis=1),
        precision=lax.Precision.HIGHEST, preferred_element_type=F32,
    )

    rolls = (7, 1)
    sums_in, sums_out = [], []
    half_sign = 0.5 * sign
    for h in every:
        totals = [tile(h, SUM_IN), tile(h, SUM_OUT)]
        if width == LB:
            packed = tile(h, SHARED)

            def shared(kind, k):
                at = 3 * kind + k
                return jnp.broadcast_to(packed[:, at : at + 1], (8, width))

            kinds = [0, 0, 1, 2, 3, 3, 4, 4]
        else:

            def shared(kind, k):
                return tile(h, SHARED + 3 * kind + k)

            kinds = range(8)
        for v, factor in enumerate(first[h]):
            high, low = shift_lanes(factor, 1), shift_lanes(factor, -1)
            up, down = (pltpu.roll(factor, r, 0) for r in rolls)
            up_high, down_high = (pltpu.roll(high, r, 0) for r in rolls)
            up_low, down_low = (pltpu.roll(low, r, 0) for r in rolls)
            for g in range(2):
                k = v + g
                spread = (
                    shared(kinds[2], k) * up
                    + shared(kinds[3], k) * down
                )
                if width == LB:
                    spread = spread + shared(0, k) * (high + low)
                    spread = spread + half_sign * (
                        shared(3, k) * (up_high - up_low) - shared(4, k) * (down_high - down_low)
                    )
                else:
                    spread = spread + shared(0, k) * high + shared(1, k) * low
                    spread = spread + half_sign * (
                        shared(4, k) * up_high - shared(5, k) * up_low
                        - shared(6, k) * down_high + shared(7, k) * down_low
                    )
                totals[g] = totals[g] + tile(h, WEIGHTS + k) * factor + TIME_STEP * spread
        bridge = inverse[h // 2, HB - 1 : HB][:, HB : HB + 1]
        sums_in.append(bridge * totals[0])
        sums_out.append(totals[1])
    alpha, beta = pick(edge_couplings(sums_in, sums_out, inverse, rate))
    final = [None] * SLOTS
    for s in (1, 2, 3):
        final[s] = (
            product[:, (s - 1) * width : s * width]
            + inner_plane * alpha[s : s + 1]
            + outer_plane * beta[s : s + 1]
        )
    w = early[0] - early[1] * (solved[2] + added[2])
    out_w[...] = (1.0 - TIME_STEP * RECOVERY_RATE) * w - early[2] * final[2]
    out_v[...] = stencil(2, final, early[3], coef, sign) + (
        TIME_STEP * RECOVERY_RATE * EXCITATION
    ) * w


def swaps(lines, lanes, partner):
    found = []
    for i in range(lines):
        for j in range(lanes):
            k, m = partner(i, j)
            found.append((i * lanes + j, k * lanes + m))
    return found


def per_device(
    adj_voltage,
    adj_gating,
    fwd_voltage,
    fwd_gating,
    region_labels,
    region_axial,
    region_shear,
    block_rate,
    block_inverse,
):
    lanes, lines = lax.axis_size("gy"), lax.axis_size("gx")
    _, depth, width = adj_voltage.shape
    label_blocks = region_labels.shape[2]
    assert depth == HB and block_inverse.shape[1] == ZB and lines % 4 == 0
    shape = jax.ShapeDtypeStruct
    room = pltpu.CompilerParams(vmem_limit_bytes=(8 << 20) * (width // LB))
    in_hbm = lambda *arrays: [pltpu.with_memory_space_constraint(x, pltpu.HBM) for x in arrays]
    voltages, gatings = fwd_voltage[:, 0], fwd_gating[:, 0]
    late = pltpu.VMEM((HB, width), fwd_voltage.dtype)
    near = pl.pallas_call(
        first_kernel,
        out_shape=shape((3 * HB + 8, width), F32),
        in_specs=[HBM] * 5,
        out_specs=VMEM,
        scratch_shapes=[
            late, late, pltpu.VMEM((label_blocks, HB), jnp.int32), pltpu.SemaphoreType.DMA((5,)),
        ],
        compiler_params=room,
    )(*in_hbm(adj_voltage[0], adj_gating[0], voltages, gatings, region_labels[0].T))
    both = pltpu.VMEM((2, HB, width), fwd_voltage.dtype)
    axial, shear, rate, inverse, vectors, own, own_rows, here, early = pl.pallas_call(
        aside_kernel,
        out_shape=(
            shape(region_axial.shape, F32), shape((1,) + region_shear.shape, F32),
            shape((1,) + block_rate.shape, F32), shape(block_inverse.shape, F32),
            shape((2, HB, width), F32), shape((HB, HB), F32), shape((8, ZB), F32),
            shape((4, HB, width), F32), shape((4, HB, width), F32),
        ),
        in_specs=[VMEM] + [HBM] * 7,
        out_specs=(VMEM,) * 9,
        scratch_shapes=[
            pltpu.VMEM((HB, width), F32), both, both, pltpu.VMEM((8, LB), F32),
            pltpu.SemaphoreType.DMA((7,)),
        ],
        compiler_params=room,
        cost_estimate=pl.CostEstimate(flops=1 << 20, bytes_accessed=1 << 20, transcendentals=0),
    )(
        near,
        *in_hbm(
            adj_gating[0], voltages, gatings, region_axial, region_shear[None], block_rate[None],
            block_inverse,
        ),
    )
    ends = (0, lines - 1)
    cycle = list(range(0, lines, 2)) + list(range(lines - 1, 0, -2))
    onward = {i: cycle[(n + 1) % lines] for n, i in enumerate(cycle)}
    pairing = swaps(lines, lanes, lambda i, j: (i ^ 1, j))
    after = lax.ppermute(
        near, BOTH,
        swaps(lines, lanes, lambda i, j: (i, j ^ 1) if i in ends else (i - 1 + 2 * (i % 2), j)),
    )
    before = lax.ppermute(near, BOTH, swaps(lines, lanes, lambda i, j: (onward[i], j)))
    pair = lax.ppermute(near, BOTH, pairing)
    relayed, own_rows = lax.optimization_barrier((after[:FAR], own_rows))
    beyond = lax.ppermute(relayed, BOTH, pairing)
    count = -(-SLOTS * label_blocks // 8) * 8
    share_shape = (share_tiles(width), 8, width)
    share, solved, centres, partial, planes = pl.pallas_call(
        gather_kernel,
        out_shape=(
            shape(share_shape, F32), shape((SLOTS, HB, width), F32), shape((3, HB, width), F32),
            shape((3, HB, width), F32), shape((4 * SLOTS, HB, width), F32),
        ),
        in_specs=[VMEM] * 11,
        out_specs=(VMEM,) * 5,
        scratch_shapes=[pltpu.VMEM((count, LB), F32)],
        compiler_params=room,
    )(near, pair, after, before, beyond, axial, shear, vectors, own, own_rows, here)
    shares = [share] + [
        lax.ppermute(share, BOTH, swaps(lines, lanes, lambda i, j: (i, j ^ d)))
        for d in range(1, lanes)
    ]
    out_v, out_w = pl.pallas_call(
        lambda *refs: finish_kernel(lanes, *refs),
        out_shape=(shape((HB, width), F32),) * 2,
        in_specs=[VMEM] * (lanes + 10),
        out_specs=(VMEM,) * 2,
        scratch_shapes=[pltpu.VMEM((lanes,) + share_shape, F32)],
        compiler_params=room,
    )(
        *shares, solved, centres, partial, planes, here, vectors, own, early, inverse, rate
    )
    return (out_v[None], out_w[None])


def solution(mesh):
    return jax.shard_map(
        per_device,
        mesh=mesh,
        in_specs=(
            P("gx", "gy", None),
            P("gx", "gy", None),
            P(None, "gx", "gy", None),
            P(None, "gx", "gy", None),
            P("gx", "gy", None),
            P(),
            P(),
            P(),
            P(),
        ),
        out_specs=(P("gx", "gy", None), P("gx", "gy", None)),
        check_vma=False,
    )
```

```python
import jax
import jax.numpy as jnp
from jax import lax
from jax.experimental import pallas as pl
from jax.experimental.pallas import tpu as pltpu
from jax.sharding import PartitionSpec as P

SWEEPS = 11
ZB = 128
LB = 128
HB = 64
SLOTS = 5

TIME_STEP = 0.2
RECOVERY_RATE = 0.25
EXCITATION = 8.0
THRESHOLD = 0.15

BOTH = ("gx", "gy")
VMEM = pl.BlockSpec(memory_space=pltpu.VMEM)
HBM = pl.BlockSpec(memory_space=pltpu.HBM)
F32 = jnp.float32
FAR = HB + 8
GAIN, LEAD = pl.ds(FAR, HB), pl.ds(FAR + HB, HB)
EDGE_IN, SUM_IN, EDGE_OUT, SUM_OUT, WEIGHTS, SHARED = 0, 1, 2, 3, 4, 7


def gain(voltage, gating):
    slope = (
        EXCITATION
        * (-3.0 * voltage * voltage + 2.0 * (1.0 + THRESHOLD) * voltage - THRESHOLD)
        - gating
    )
    return 1.0 + TIME_STEP * slope


def start_copies(pairs, sems):
    copies = [pltpu.make_async_copy(a, b, sems.at[n]) for n, (a, b) in enumerate(pairs)]
    for copy in copies:
        copy.start()
    return copies


def first_kernel(voltage_in, gating_in, fwd_v_in, fwd_g_in, label_in, near, v, g, label, sems):
    later = fwd_v_in.shape[0] - 1
    copies = start_copies(
        [
            (fwd_v_in.at[later], v), (fwd_g_in.at[later], g), (label_in, label),
            (gating_in, near.at[LEAD]), (voltage_in, near.at[pl.ds(0, HB)]),
        ],
        sems,
    )
    for copy in copies[:3]:
        copy.wait()
    near[GAIN] = gain(v[...].astype(F32), g[...].astype(F32))
    blocks = label.shape[0]
    near[HB:FAR] = jnp.zeros((8, near.shape[1]), F32)
    near[HB : HB + blocks, 0:HB] = label[...].astype(F32)
    for copy in copies[3:]:
        copy.wait()


def lookup(label, axial, shear):
    zero = jnp.zeros(label.shape, F32)
    tables = [zero, zero, zero]
    for region in range(1, axial.shape[1]):
        here = label == float(region)
        for k, value in enumerate(
            (axial[0:1, region : region + 1], axial[1:2, region : region + 1],
             shear[0:1, region : region + 1])
        ):
            tables[k] = jnp.where(here, value, tables[k])
    tables.append((label > 0.0).astype(F32))
    return tables


def fill_plane(plane, columns, at, label_blocks):
    for block in range(label_blocks):
        plane[:, block * LB : (block + 1) * LB] = jnp.broadcast_to(
            columns[:, at + block : at + block + 1], (HB, LB)
        )


def aside_kernel(
    near, gating_in, fwd_v_in, fwd_g_in, axial_in, shear_in, rate_in, inverse_in,
    axial, shear, rate, inverse, vectors, own, lines, planes, early, w, v, g, label, sems,
):
    width = w.shape[1]
    label_blocks = width // LB
    me = lax.axis_index("gy")
    upper, mine = lax.rem(me, 2) == 1, lax.div(me, 2)
    for copy in start_copies(
        [
            (inverse_in, inverse), (axial_in, axial), (shear_in, shear), (rate_in, rate),
            (gating_in, w), (fwd_v_in, v), (fwd_g_in, g),
        ],
        sems,
    ):
        copy.wait()
    inner, outer, inner_column, outer_column, bridge, square = half_vectors(inverse, mine, upper)
    vectors[0] = jnp.broadcast_to(inner_column, (HB, width))
    vectors[1] = jnp.broadcast_to(outer_column, (HB, width))
    own[...] = square
    lines[0:1] = inner
    lines[1:2] = outer
    lines[2:3] = jnp.broadcast_to(bridge, (1, ZB))
    label[...] = jnp.zeros(label.shape, F32)
    label[0:label_blocks] = near[HB : HB + label_blocks, :LB]
    columns = jnp.concatenate(lookup(label[...], axial, shear), axis=0).T[:HB]
    for k in range(4):
        fill_plane(planes.at[k], columns, 8 * k, label_blocks)
    tissue = planes[3]
    late_v, early_v = v[1].astype(F32), v[0].astype(F32)
    early[0] = (1.0 - TIME_STEP * RECOVERY_RATE) * (tissue * w[...])
    early[1] = TIME_STEP * (tissue * late_v)
    early[2] = TIME_STEP * (tissue * early_v)
    early[3] = tissue * gain(early_v, g[0].astype(F32)) - (2.0 * TIME_STEP) * (
        planes[0] + planes[1]
    )


def half_vectors(inverse, mine, upper):
    def row(index):
        return inverse[mine, index : index + 1, :]

    bridge = row(HB - 1)[:, HB : HB + 1]
    inner = jnp.where(upper, pltpu.roll(row(HB - 1), HB, 1), row(HB)) / bridge
    outer = jnp.where(upper, pltpu.roll(row(ZB - 1), HB, 1), row(0))
    rows = inverse[mine, pl.ds(pl.multiple_of(jnp.where(upper, HB, 0), HB), HB), :]
    swapped = jnp.where(upper, pltpu.roll(rows, HB, 1), rows)
    inner_column = jnp.where(upper, swapped[:, ZB - 1 :], swapped[:, HB : HB + 1]) / bridge
    outer_column = jnp.where(upper, swapped[:, HB - 1 : HB], swapped[:, 0:1])
    return inner, outer, inner_column, outer_column, bridge, swapped[:, :HB]


def y_shifts(plus, minus):
    width = plus.shape[1]
    lane = lax.broadcasted_iota(jnp.int32, plus.shape, 1)
    return jnp.where(lane == width - 1, 0.0, pltpu.roll(plus, width - 1, 1)) + jnp.where(
        lane == 0, 0.0, pltpu.roll(minus, 1, 1)
    )


def stencil(slot, field, center, coef, sign):
    along, across, shear, tissue = coef
    level = TIME_STEP * (across(slot) * field[slot])
    twist, beside = 0.0, 0.0
    for step in (1, -1):
        other = slot + step
        if field[other] is not None:
            twist = twist + (step * 0.5 * TIME_STEP * sign) * (shear(other) * field[other])
            beside = beside + TIME_STEP * (along(other) * field[other])
    return center * field[slot] + tissue(slot) * (y_shifts(level + twist, level - twist) + beside)


def reach(slot, other, field, coef, sign):
    twist = ((other - slot) * 0.5 * TIME_STEP * sign) * (coef[2](other) * field)
    return coef[3](slot) * (y_shifts(twist, -twist) + TIME_STEP * (coef[0](other) * field))


def centre(gains, slot, coef):
    along, across, _, tissue = coef
    return tissue(slot) * gains - (2.0 * TIME_STEP) * (along(slot) + across(slot))


def coefficients(here, beside, beyond):
    def reader(k):
        def read(slot):
            if slot == 2:
                return here[k]
            if slot in (1, 3):
                return beside[2 * k + slot // 2]
            return beyond[k + slot // 4]

        return read

    return [reader(k) for k in range(4)]


def orientation():
    line = lax.axis_index("gx")
    return jnp.where(lax.rem(line, 2) == 0, 1.0, -1.0)


def upright(row):
    z = lax.broadcasted_iota(jnp.int32, (HB, LB), 0)
    lane = lax.broadcasted_iota(jnp.int32, (HB, LB), 1)
    column = jnp.sum(jnp.where(z == lane, row, 0.0), axis=1, keepdims=True)
    return jnp.broadcast_to(column, (HB, LB))


def put_total(share, kind, slot, value):
    row = slot + 4 * (kind % 2)
    share[kind // 2, row : row + 1, :] = jnp.sum(value, axis=0, keepdims=True)


def label_rows(rows, given, label_blocks):
    line, last = lax.axis_index("gx"), lax.axis_size("gx") - 1
    even = lax.rem(line, 2) == 0
    inside = {
        1: jnp.logical_and(line > 0, line < last),
        4: jnp.where(even, line + 2 <= last, line >= 2),
        0: jnp.where(even, line >= 2, line + 2 <= last),
    }
    rows[...] = jnp.zeros(rows.shape, F32)
    for slot, ref in given.items():
        label = ref[HB : HB + label_blocks, :LB]
        if slot in inside:
            label = jnp.where(inside[slot], label, 0.0)
        rows[slot * label_blocks : (slot + 1) * label_blocks] = label
    return rows[...]


def solve_planes(own, fields, width):
    product = jnp.dot(
        own[...], jnp.concatenate(fields, axis=1),
        precision=lax.Precision.HIGHEST, preferred_element_type=F32,
    )
    return [product[:, n * width : (n + 1) * width] for n in range(len(fields))]


def gather_kernel(
    near, pair, after, axial, shear, vectors, own, lines, here,
    share, solved, centres, partial, beside, rows,
):
    width = near.shape[1]
    label_blocks = width // LB
    given = {1: after, 2: near, 3: pair}
    tables = lookup(label_rows(rows, {1: after, 3: pair}, label_blocks), axial, shear)
    columns = jnp.concatenate(tables, axis=0).T[:HB]
    for k in range(4):
        for slot in (1, 3):
            fill_plane(
                beside.at[2 * k + slot // 2], columns,
                k * rows.shape[0] + slot * label_blocks, label_blocks,
            )
    coef = coefficients(here, beside, None)
    sign = orientation()
    bridge = lines[2:3, 0:1]
    inner_plane, outer_plane = vectors[0], vectors[1]
    fields = [given[slot][0:HB] for slot in (1, 2, 3)]
    parts = [None] + solve_planes(own, fields, width) + [None]
    solved[...] = parts[2]
    share[...] = jnp.zeros(share.shape, F32)
    for slot in (1, 2, 3):
        put_total(share, EDGE_IN, slot, bridge * (inner_plane * fields[slot - 1]))
        put_total(share, EDGE_OUT, slot, outer_plane * fields[slot - 1])
    weights = (inner_plane * inner_plane, inner_plane * outer_plane, outer_plane * outer_plane)
    for slot in (1, 2, 3):
        center = centre(given[slot][GAIN], slot, coef)
        lead = (TIME_STEP * RECOVERY_RATE * EXCITATION) * given[slot][LEAD]
        part = stencil(slot, parts, center, coef, sign) + coef[3](slot) * lead
        centres[slot - 1] = center
        partial[slot - 1] = part
        if slot == 2:
            put_total(share, SUM_IN, slot, inner_plane * part)
            put_total(share, SUM_OUT, slot, outer_plane * part)
        for k, weight in enumerate(weights):
            put_total(share, WEIGHTS + k, slot, weight * center)


def complete_kernel(
    near, pair, after, before, beyond, axial, shear, vectors, own, lines, here,
    begun, most, beside, share, outside, distant, rows,
):
    width = near.shape[1]
    label_blocks = width // LB
    given = {0: before, 1: after, 2: near, 3: pair, 4: beyond}
    tables = lookup(label_rows(rows, given, label_blocks), axial, shear)
    for k in range(2):
        for slot in (0, 4):
            for block in range(label_blocks):
                at = slot * label_blocks + block
                distant[2 * k + slot // 4, :, block * LB : (block + 1) * LB] = upright(
                    tables[2 * k][at : at + 1]
                )
    coef = coefficients(here, beside, distant)
    sign = orientation()
    inner, outer, bridge = lines[0:1], lines[1:2], lines[2:3, 0:1]
    inner_plane, outer_plane = vectors[0], vectors[1]
    share[...] = begun[...]

    def total(kind, slot, value):
        put_total(share, kind, slot, value)

    fields = [before[0:HB], beyond[0:HB]]
    parts = solve_planes(own, fields, width)
    for n, slot in enumerate((0, 4)):
        total(EDGE_IN, slot, bridge * (inner_plane * fields[n]))
        total(EDGE_OUT, slot, outer_plane * fields[n])
        middle = 1 + 2 * n
        part = most[middle - 1] + reach(middle, slot, parts[n], coef, sign)
        outside[n] = part
        total(SUM_IN, middle, inner_plane * part)
        total(SUM_OUT, middle, outer_plane * part)
    if label_blocks == 1:
        lane = lax.broadcasted_iota(jnp.int32, (1, ZB), 1)
        inner = jnp.where(lane < HB, inner, 0.0)
        outer = jnp.where(lane < HB, outer, 0.0)
        pairs = (inner * inner, inner * outer, outer * outer)
        along, across, shears, tissue = tables
        up, down = rows.shape[0] - 1, 1
        kinds = (
            across,
            tissue * pltpu.roll(along, up, 0),
            tissue * pltpu.roll(along, down, 0),
            tissue * pltpu.roll(shears, up, 0),
            tissue * pltpu.roll(shears, down, 0),
        )
        lanes = lax.broadcasted_iota(jnp.int32, (8, ZB), 1)
        packed = jnp.zeros((8, ZB), F32)
        for n, kind in enumerate(kinds):
            for k, vector in enumerate(pairs):
                value = jnp.sum(kind * vector, axis=1, keepdims=True)
                packed = jnp.where(lanes == 3 * n + k, value, packed)
        share[SHARED // 2, 5:8] = packed[1:4]
    else:
        none = jnp.zeros((HB, width), F32)
        weights = (
            inner_plane * inner_plane, inner_plane * outer_plane, outer_plane * outer_plane
        )
        for slot in (1, 2, 3):
            here = coef[3](slot)
            kinds = (
                here * y_shifts(coef[1](slot), none),
                here * y_shifts(none, coef[1](slot)),
                here * coef[0](slot + 1),
                here * coef[0](slot - 1),
                here * y_shifts(coef[2](slot + 1), none),
                here * y_shifts(none, coef[2](slot + 1)),
                here * y_shifts(coef[2](slot - 1), none),
                here * y_shifts(none, coef[2](slot - 1)),
            )
            for n, kind in enumerate(kinds):
                for k, weight in enumerate(weights):
                    total(SHARED + 3 * n + k, slot, weight * kind)


def share_tiles(width):
    return -(-(SHARED + (1 if width == LB else 24)) // 2)


def edge_couplings(edge_in, edge_out, inverse, rate, only=None):
    blocks = inverse.shape[0]
    first, last, corner, reach = [], [], [], []
    for b in range(blocks):
        top, bottom = inverse[b, 0:1], inverse[b, ZB - 1 : ZB]
        middle = inverse[b, HB - 1 : HB]
        bridge = middle[:, HB : HB + 1]
        first.append(edge_out[2 * b] + (top[:, HB : HB + 1] / bridge) * edge_in[2 * b + 1])
        last.append(edge_out[2 * b + 1] + (bottom[:, HB - 1 : HB] / bridge) * edge_in[2 * b])
        corner.append((top[:, 0:1], top[:, ZB - 1 :], bottom[:, 0:1], bottom[:, ZB - 1 :]))
        reach.append((middle[:, ZB - 1 :], inverse[b, HB : HB + 1][:, 0:1]))
    links = [jnp.minimum(rate[:, b : b + 1], rate[:, b + 1 : b + 2]) for b in range(blocks - 1)]
    down = [None] + [
        (links[b - 1] * corner[b][0], links[b] * corner[b][1] if b < blocks - 1 else None)
        for b in range(1, blocks)
    ]
    ups = [
        (links[b - 1] * corner[b][2] if b else None, links[b] * corner[b][3])
        for b in range(blocks - 1)
    ]
    u_first, u_last = list(first), list(last)
    for _ in range(SWEEPS - 1):
        n_first, n_last = list(first), list(last)
        for b in range(1, blocks):
            n_first[b] = first[b] + down[b][0] * u_last[b - 1]
            if down[b][1] is not None:
                n_first[b] = n_first[b] + down[b][1] * u_first[b + 1]
        for b in range(blocks - 1):
            n_last[b] = last[b] + ups[b][1] * u_first[b + 1]
            if ups[b][0] is not None:
                n_last[b] = n_last[b] + ups[b][0] * u_last[b - 1]
        u_first, u_last = n_first, n_last
    factors = []
    zero = jnp.zeros_like(first[0])
    for b in range(blocks):
        below = links[b - 1] * u_last[b - 1] if b else zero
        above = links[b] * u_first[b + 1] if b < blocks - 1 else zero
        factors.append((edge_in[2 * b + 1] + reach[b][0] * above, below))
        factors.append((edge_in[2 * b] + reach[b][1] * below, above))
    return factors


def shift_lanes(tile, by):
    width = tile.shape[1]
    lane = lax.broadcasted_iota(jnp.int32, tile.shape, 1)
    if by > 0:
        return jnp.where(lane == width - 1, 0.0, pltpu.roll(tile, width - 1, 1))
    return jnp.where(lane == 0, 0.0, pltpu.roll(tile, 1, 1))


def finish_kernel(halves, *refs):
    shares = refs[:halves]
    (
        solved, centres, partial, outside, here, beside, distant, vectors, own, early, inverse, rate,
    ) = refs[halves : halves + 12]
    out_v, out_w, board = refs[halves + 12 :]
    width = out_v.shape[1]
    me = lax.axis_index("gy")
    sign = orientation()
    for d in range(halves):
        board[d] = shares[d][...]

    def tile(half, kind):
        found = board[lax.bitwise_xor(half, me), kind // 2]
        return pltpu.roll(found, 4, 0) if kind % 2 else found

    every = range(halves)
    first = edge_couplings(
        [tile(h, EDGE_IN) for h in every], [tile(h, EDGE_OUT) for h in every], inverse, rate
    )
    inner_plane, outer_plane = vectors[0], vectors[1]
    coef = coefficients(here, beside, distant)

    def pick(factors):
        chosen = factors[0]
        for h in range(1, halves):
            chosen = [jnp.where(me == h, new, old) for new, old in zip(factors[h], chosen)]
        return chosen

    alpha, beta = pick(first)
    added = [
        inner_plane * alpha[s : s + 1] + outer_plane * beta[s : s + 1] for s in range(SLOTS)
    ]
    nexts = [
        (partial[1] if s == 2 else outside[s // 2])
        + stencil(s, added, centres[s - 1], coef, sign)
        for s in (1, 2, 3)
    ]
    product = jnp.dot(
        own[...], jnp.concatenate(nexts, axis=1),
        precision=lax.Precision.HIGHEST, preferred_element_type=F32,
    )

    rolls = (7, 1)
    sums_in, sums_out = [], []
    half_sign = 0.5 * sign
    for h in every:
        totals = [tile(h, SUM_IN), tile(h, SUM_OUT)]
        if width == LB:
            packed = tile(h, SHARED)

            def shared(kind, k):
                at = 3 * kind + k
                return jnp.broadcast_to(packed[:, at : at + 1], (8, width))

            kinds = [0, 0, 1, 2, 3, 3, 4, 4]
        else:

            def shared(kind, k):
                return tile(h, SHARED + 3 * kind + k)

            kinds = range(8)
        for v, factor in enumerate(first[h]):
            high, low = shift_lanes(factor, 1), shift_lanes(factor, -1)
            up, down = (pltpu.roll(factor, r, 0) for r in rolls)
            up_high, down_high = (pltpu.roll(high, r, 0) for r in rolls)
            up_low, down_low = (pltpu.roll(low, r, 0) for r in rolls)
            for g in range(2):
                k = v + g
                spread = (
                    shared(kinds[2], k) * up
                    + shared(kinds[3], k) * down
                )
                if width == LB:
                    spread = spread + shared(0, k) * (high + low)
                    spread = spread + half_sign * (
                        shared(3, k) * (up_high - up_low) - shared(4, k) * (down_high - down_low)
                    )
                else:
                    spread = spread + shared(0, k) * high + shared(1, k) * low
                    spread = spread + half_sign * (
                        shared(4, k) * up_high - shared(5, k) * up_low
                        - shared(6, k) * down_high + shared(7, k) * down_low
                    )
                totals[g] = totals[g] + tile(h, WEIGHTS + k) * factor + TIME_STEP * spread
        bridge = inverse[h // 2, HB - 1 : HB][:, HB : HB + 1]
        sums_in.append(bridge * totals[0])
        sums_out.append(totals[1])
    alpha, beta = pick(edge_couplings(sums_in, sums_out, inverse, rate))
    final = [None] * SLOTS
    for s in (1, 2, 3):
        final[s] = (
            product[:, (s - 1) * width : s * width]
            + inner_plane * alpha[s : s + 1]
            + outer_plane * beta[s : s + 1]
        )
    w = early[0] - early[1] * (solved[...] + added[2])
    out_w[...] = (1.0 - TIME_STEP * RECOVERY_RATE) * w - early[2] * final[2]
    out_v[...] = stencil(2, final, early[3], coef, sign) + (
        TIME_STEP * RECOVERY_RATE * EXCITATION
    ) * w


def swaps(lines, lanes, partner):
    found = []
    for i in range(lines):
        for j in range(lanes):
            k, m = partner(i, j)
            found.append((i * lanes + j, k * lanes + m))
    return found


def per_device(
    adj_voltage,
    adj_gating,
    fwd_voltage,
    fwd_gating,
    region_labels,
    region_axial,
    region_shear,
    block_rate,
    block_inverse,
):
    lanes, lines = lax.axis_size("gy"), lax.axis_size("gx")
    _, depth, width = adj_voltage.shape
    label_blocks = region_labels.shape[2]
    assert depth == HB and block_inverse.shape[1] == ZB and lines % 4 == 0
    shape = jax.ShapeDtypeStruct
    room = pltpu.CompilerParams(vmem_limit_bytes=(8 << 20) * (width // LB))
    in_hbm = lambda *arrays: [pltpu.with_memory_space_constraint(x, pltpu.HBM) for x in arrays]
    voltages, gatings = fwd_voltage[:, 0], fwd_gating[:, 0]
    late = pltpu.VMEM((HB, width), fwd_voltage.dtype)
    near = pl.pallas_call(
        first_kernel,
        out_shape=shape((3 * HB + 8, width), F32),
        in_specs=[HBM] * 5,
        out_specs=VMEM,
        scratch_shapes=[
            late, late, pltpu.VMEM((label_blocks, HB), jnp.int32), pltpu.SemaphoreType.DMA((5,)),
        ],
        compiler_params=room,
    )(*in_hbm(adj_voltage[0], adj_gating[0], voltages, gatings, region_labels[0].T))
    both = pltpu.VMEM((2, HB, width), fwd_voltage.dtype)
    axial, shear, rate, inverse, vectors, own, own_rows, here, early = pl.pallas_call(
        aside_kernel,
        out_shape=(
            shape(region_axial.shape, F32), shape((1,) + region_shear.shape, F32),
            shape((1,) + block_rate.shape, F32), shape(block_inverse.shape, F32),
            shape((2, HB, width), F32), shape((HB, HB), F32), shape((8, ZB), F32),
            shape((4, HB, width), F32), shape((4, HB, width), F32),
        ),
        in_specs=[VMEM] + [HBM] * 7,
        out_specs=(VMEM,) * 9,
        scratch_shapes=[
            pltpu.VMEM((HB, width), F32), both, both, pltpu.VMEM((8, LB), F32),
            pltpu.SemaphoreType.DMA((7,)),
        ],
        compiler_params=room,
        cost_estimate=pl.CostEstimate(flops=1 << 20, bytes_accessed=1 << 20, transcendentals=0),
    )(
        near,
        *in_hbm(
            adj_gating[0], voltages, gatings, region_axial, region_shear[None], block_rate[None],
            block_inverse,
        ),
    )
    ends = (0, lines - 1)
    cycle = list(range(0, lines, 2)) + list(range(lines - 1, 0, -2))
    onward = {i: cycle[(n + 1) % lines] for n, i in enumerate(cycle)}
    pairing = swaps(lines, lanes, lambda i, j: (i ^ 1, j))
    after = lax.ppermute(
        near, BOTH,
        swaps(lines, lanes, lambda i, j: (i, j ^ 1) if i in ends else (i - 1 + 2 * (i % 2), j)),
    )
    before = lax.ppermute(near[:FAR], BOTH, swaps(lines, lanes, lambda i, j: (onward[i], j)))
    pair = lax.ppermute(near, BOTH, pairing)
    relayed, own_rows = lax.optimization_barrier((after[:FAR], own_rows))
    beyond = lax.ppermute(relayed, BOTH, pairing)
    count = -(-SLOTS * label_blocks // 8) * 8
    share_shape = (share_tiles(width), 8, width)
    label_scratch = [pltpu.VMEM((count, LB), F32)]
    begun, solved, centres, partial, beside = pl.pallas_call(
        gather_kernel,
        out_shape=(
            shape(share_shape, F32), shape((HB, width), F32), shape((3, HB, width), F32),
            shape((3, HB, width), F32), shape((8, HB, width), F32),
        ),
        in_specs=[VMEM] * 9,
        out_specs=(VMEM,) * 5,
        scratch_shapes=label_scratch,
        compiler_params=room,
        cost_estimate=pl.CostEstimate(flops=1 << 20, bytes_accessed=1 << 20, transcendentals=0),
    )(near, pair, after, axial, shear, vectors, own, own_rows, here)
    share, outside, distant = pl.pallas_call(
        complete_kernel,
        out_shape=(
            shape(share_shape, F32), shape((2, HB, width), F32), shape((4, HB, width), F32),
        ),
        in_specs=[VMEM] * 14,
        out_specs=(VMEM,) * 3,
        scratch_shapes=label_scratch,
        compiler_params=room,
    )(
        near, pair, after, before, beyond, axial, shear, vectors, own, own_rows, here, begun,
        partial, beside,
    )
    shares = [share] + [
        lax.ppermute(share, BOTH, swaps(lines, lanes, lambda i, j: (i, j ^ d)))
        for d in range(1, lanes)
    ]
    out_v, out_w = pl.pallas_call(
        lambda *refs: finish_kernel(lanes, *refs),
        out_shape=(shape((HB, width), F32),) * 2,
        in_specs=[VMEM] * (lanes + 12),
        out_specs=(VMEM,) * 2,
        scratch_shapes=[pltpu.VMEM((lanes,) + share_shape, F32)],
        compiler_params=room,
    )(
        *shares, solved, centres, partial, outside, here, beside, distant, vectors, own, early,
        inverse, rate,
    )
    return (out_v[None], out_w[None])


def solution(mesh):
    return jax.shard_map(
        per_device,
        mesh=mesh,
        in_specs=(
            P("gx", "gy", None),
            P("gx", "gy", None),
            P(None, "gx", "gy", None),
            P(None, "gx", "gy", None),
            P("gx", "gy", None),
            P(),
            P(),
            P(),
            P(),
        ),
        out_specs=(P("gx", "gy", None), P("gx", "gy", None)),
        check_vma=False,
    )
```

```python
import jax
import jax.numpy as jnp
from jax import lax
from jax.experimental import pallas as pl
from jax.experimental.pallas import tpu as pltpu
from jax.sharding import PartitionSpec as P

SWEEPS = 11
ZB = 128
LB = 128
HB = 64
SLOTS = 5

TIME_STEP = 0.2
RECOVERY_RATE = 0.25
EXCITATION = 8.0
THRESHOLD = 0.15

BOTH = ("gx", "gy")
VMEM = pl.BlockSpec(memory_space=pltpu.VMEM)
HBM = pl.BlockSpec(memory_space=pltpu.HBM)
F32 = jnp.float32
FAR = HB + 8
GAIN, LEAD = pl.ds(FAR, HB), pl.ds(FAR + HB, HB)
EDGE_IN, SUM_IN, EDGE_OUT, SUM_OUT, WEIGHTS, SHARED = 0, 1, 2, 3, 4, 7


def gain(voltage, gating):
    slope = (
        EXCITATION
        * (-3.0 * voltage * voltage + 2.0 * (1.0 + THRESHOLD) * voltage - THRESHOLD)
        - gating
    )
    return 1.0 + TIME_STEP * slope


def start_copies(pairs, sems):
    copies = [pltpu.make_async_copy(a, b, sems.at[n]) for n, (a, b) in enumerate(pairs)]
    for copy in copies:
        copy.start()
    return copies


def first_kernel(voltage_in, gating_in, fwd_v_in, fwd_g_in, label_in, near, v, g, label, sems):
    later = fwd_v_in.shape[0] - 1
    copies = start_copies(
        [
            (fwd_v_in.at[later], v), (fwd_g_in.at[later], g), (label_in, label),
            (gating_in, near.at[LEAD]), (voltage_in, near.at[pl.ds(0, HB)]),
        ],
        sems,
    )
    for copy in copies[:3]:
        copy.wait()
    near[GAIN] = gain(v[...].astype(F32), g[...].astype(F32))
    blocks = label.shape[0]
    near[HB:FAR] = jnp.zeros((8, near.shape[1]), F32)
    near[HB : HB + blocks, 0:HB] = label[...].astype(F32)
    for copy in copies[3:]:
        copy.wait()


def lookup(label, axial, shear):
    zero = jnp.zeros(label.shape, F32)
    tables = [zero, zero, zero]
    for region in range(1, axial.shape[1]):
        here = label == float(region)
        for k, value in enumerate(
            (axial[0:1, region : region + 1], axial[1:2, region : region + 1],
             shear[0:1, region : region + 1])
        ):
            tables[k] = jnp.where(here, value, tables[k])
    tables.append((label > 0.0).astype(F32))
    return tables


def upright(row):
    z = lax.broadcasted_iota(jnp.int32, (HB, LB), 0)
    lane = lax.broadcasted_iota(jnp.int32, (HB, LB), 1)
    column = jnp.sum(jnp.where(z == lane, row, 0.0), axis=1, keepdims=True)
    return jnp.broadcast_to(column, (HB, LB))


def fill_plane(plane, table, at, label_blocks):
    for block in range(label_blocks):
        plane[:, block * LB : (block + 1) * LB] = upright(table[at + block : at + block + 1])


def aside_kernel(
    near, gating_in, fwd_v_in, fwd_g_in, axial_in, shear_in, rate_in, inverse_in,
    axial, shear, numbers, vectors, own, lines, planes, early, w, v, g, label, inverse, rate, sems,
):
    width = w.shape[1]
    label_blocks = width // LB
    me = lax.axis_index("gy")
    upper, mine = lax.rem(me, 2) == 1, lax.div(me, 2)
    for copy in start_copies(
        [
            (inverse_in, inverse), (axial_in, axial), (shear_in, shear), (rate_in, rate),
            (gating_in, w), (fwd_v_in, v), (fwd_g_in, g),
        ],
        sems,
    ):
        copy.wait()
    inner, outer, inner_column, outer_column, bridge, square = half_vectors(inverse, mine, upper)
    vectors[0] = jnp.broadcast_to(inner_column, (HB, width))
    vectors[1] = jnp.broadcast_to(outer_column, (HB, width))
    own[...] = square
    for n, value in enumerate(edge_constants(inverse, rate)):
        numbers[n : n + 1] = jnp.broadcast_to(value, (1, width))
    lines[0:1] = inner
    lines[1:2] = outer
    lines[2:3] = jnp.broadcast_to(bridge, (1, ZB))
    label[...] = jnp.zeros(label.shape, F32)
    label[0:label_blocks] = near[HB : HB + label_blocks, :LB]
    for k, table in enumerate(lookup(label[...], axial, shear)):
        fill_plane(planes.at[k], table, 0, label_blocks)
    tissue = planes[3]
    late_v, early_v = v[1].astype(F32), v[0].astype(F32)
    early[0] = (1.0 - TIME_STEP * RECOVERY_RATE) * (tissue * w[...])
    early[1] = TIME_STEP * (tissue * late_v)
    early[2] = TIME_STEP * (tissue * early_v)
    early[3] = tissue * gain(early_v, g[0].astype(F32)) - (2.0 * TIME_STEP) * (
        planes[0] + planes[1]
    )


def half_vectors(inverse, mine, upper):
    def row(index):
        return inverse[mine, index : index + 1, :]

    bridge = row(HB - 1)[:, HB : HB + 1]
    inner = jnp.where(upper, pltpu.roll(row(HB - 1), HB, 1), row(HB)) / bridge
    outer = jnp.where(upper, pltpu.roll(row(ZB - 1), HB, 1), row(0))
    rows = inverse[mine, pl.ds(pl.multiple_of(jnp.where(upper, HB, 0), HB), HB), :]
    swapped = jnp.where(upper, pltpu.roll(rows, HB, 1), rows)
    inner_column = jnp.where(upper, swapped[:, ZB - 1 :], swapped[:, HB : HB + 1]) / bridge
    outer_column = jnp.where(upper, swapped[:, HB - 1 : HB], swapped[:, 0:1])
    return inner, outer, inner_column, outer_column, bridge, swapped[:, :HB]


def y_shifts(plus, minus):
    width = plus.shape[1]
    lane = lax.broadcasted_iota(jnp.int32, plus.shape, 1)
    return jnp.where(lane == width - 1, 0.0, pltpu.roll(plus, width - 1, 1)) + jnp.where(
        lane == 0, 0.0, pltpu.roll(minus, 1, 1)
    )


def stencil(slot, field, center, coef, sign):
    along, across, shear, tissue = coef
    level = TIME_STEP * (across(slot) * field[slot])
    twist, beside = 0.0, 0.0
    for step in (1, -1):
        other = slot + step
        if field[other] is not None:
            twist = twist + (step * 0.5 * TIME_STEP * sign) * (shear(other) * field[other])
            beside = beside + TIME_STEP * (along(other) * field[other])
    return center * field[slot] + tissue(slot) * (y_shifts(level + twist, level - twist) + beside)


def reach(slot, other, field, coef, sign):
    twist = ((other - slot) * 0.5 * TIME_STEP * sign) * (coef[2](other) * field)
    return coef[3](slot) * (y_shifts(twist, -twist) + TIME_STEP * (coef[0](other) * field))


def centre(gains, slot, coef):
    along, across, _, tissue = coef
    return tissue(slot) * gains - (2.0 * TIME_STEP) * (along(slot) + across(slot))


def coefficients(here, beside, beyond):
    def reader(k):
        def read(slot):
            if slot == 2:
                return here[k]
            if slot in (1, 3):
                return beside[2 * k + slot // 2]
            return beyond[k + slot // 4]

        return read

    return [reader(k) for k in range(4)]


def orientation():
    line = lax.axis_index("gx")
    return jnp.where(lax.rem(line, 2) == 0, 1.0, -1.0)


def put_total(share, kind, slot, value):
    row = slot + 4 * (kind % 2)
    share[kind // 2, row : row + 1, :] = jnp.sum(value, axis=0, keepdims=True)


def label_rows(rows, given, label_blocks):
    line, last = lax.axis_index("gx"), lax.axis_size("gx") - 1
    even = lax.rem(line, 2) == 0
    inside = {
        1: jnp.logical_and(line > 0, line < last),
        4: jnp.where(even, line + 2 <= last, line >= 2),
        0: jnp.where(even, line >= 2, line + 2 <= last),
    }
    rows[...] = jnp.zeros(rows.shape, F32)
    for slot, ref in given.items():
        label = ref[HB : HB + label_blocks, :LB]
        if slot in inside:
            label = jnp.where(inside[slot], label, 0.0)
        rows[slot * label_blocks : (slot + 1) * label_blocks] = label
    return rows[...]


def solve_planes(own, fields, width):
    product = jnp.dot(
        own[...], jnp.concatenate(fields, axis=1),
        precision=lax.Precision.HIGHEST, preferred_element_type=F32,
    )
    return [product[:, n * width : (n + 1) * width] for n in range(len(fields))]


def gather_kernel(
    near, pair, after, axial, shear, vectors, own, lines, here,
    share, solved, centres, partial, beside, rows,
):
    width = near.shape[1]
    label_blocks = width // LB
    given = {1: after, 2: near, 3: pair}
    tables = lookup(label_rows(rows, {1: after, 3: pair}, label_blocks), axial, shear)
    for k in range(4):
        for slot in (1, 3):
            fill_plane(beside.at[2 * k + slot // 2], tables[k], slot * label_blocks, label_blocks)
    coef = coefficients(here, beside, None)
    sign = orientation()
    bridge = lines[2:3, 0:1]
    inner_plane, outer_plane = vectors[0], vectors[1]
    fields = [given[slot][0:HB] for slot in (1, 2, 3)]
    parts = [None] + solve_planes(own, fields, width) + [None]
    solved[...] = parts[2]
    share[...] = jnp.zeros(share.shape, F32)
    for slot in (1, 2, 3):
        put_total(share, EDGE_IN, slot, bridge * (inner_plane * fields[slot - 1]))
        put_total(share, EDGE_OUT, slot, outer_plane * fields[slot - 1])
    weights = (inner_plane * inner_plane, inner_plane * outer_plane, outer_plane * outer_plane)
    for slot in (1, 2, 3):
        center = centre(given[slot][GAIN], slot, coef)
        lead = (TIME_STEP * RECOVERY_RATE * EXCITATION) * given[slot][LEAD]
        part = stencil(slot, parts, center, coef, sign) + coef[3](slot) * lead
        centres[slot - 1] = center
        partial[slot - 1] = part
        if slot == 2:
            put_total(share, SUM_IN, slot, inner_plane * part)
            put_total(share, SUM_OUT, slot, outer_plane * part)
        for k, weight in enumerate(weights):
            put_total(share, WEIGHTS + k, slot, weight * center)


def complete_kernel(
    near, pair, after, before, beyond, axial, shear, vectors, own, lines, here,
    begun, most, beside, share, outside, distant, rows,
):
    width = near.shape[1]
    label_blocks = width // LB
    given = {0: before, 1: after, 2: near, 3: pair, 4: beyond}
    tables = lookup(label_rows(rows, given, label_blocks), axial, shear)
    for k in range(2):
        for slot in (0, 4):
            fill_plane(
                distant.at[2 * k + slot // 4], tables[2 * k], slot * label_blocks, label_blocks
            )
    coef = coefficients(here, beside, distant)
    sign = orientation()
    inner, outer, bridge = lines[0:1], lines[1:2], lines[2:3, 0:1]
    inner_plane, outer_plane = vectors[0], vectors[1]
    share[...] = begun[...]

    def total(kind, slot, value):
        put_total(share, kind, slot, value)

    fields = [before[0:HB], beyond[0:HB]]
    parts = solve_planes(own, fields, width)
    for n, slot in enumerate((0, 4)):
        total(EDGE_IN, slot, bridge * (inner_plane * fields[n]))
        total(EDGE_OUT, slot, outer_plane * fields[n])
        middle = 1 + 2 * n
        part = most[middle - 1] + reach(middle, slot, parts[n], coef, sign)
        outside[n] = part
        total(SUM_IN, middle, inner_plane * part)
        total(SUM_OUT, middle, outer_plane * part)
    if label_blocks == 1:
        lane = lax.broadcasted_iota(jnp.int32, (1, ZB), 1)
        inner = jnp.where(lane < HB, inner, 0.0)
        outer = jnp.where(lane < HB, outer, 0.0)
        pairs = (inner * inner, inner * outer, outer * outer)
        along, across, shears, tissue = tables
        up, down = rows.shape[0] - 1, 1
        kinds = (
            across,
            tissue * pltpu.roll(along, up, 0),
            tissue * pltpu.roll(along, down, 0),
            tissue * pltpu.roll(shears, up, 0),
            tissue * pltpu.roll(shears, down, 0),
        )
        lanes = lax.broadcasted_iota(jnp.int32, (8, ZB), 1)
        packed = jnp.zeros((8, ZB), F32)
        for n, kind in enumerate(kinds):
            for k, vector in enumerate(pairs):
                value = jnp.sum(kind * vector, axis=1, keepdims=True)
                packed = jnp.where(lanes == 3 * n + k, value, packed)
        share[SHARED // 2, 5:8] = packed[1:4]
    else:
        none = jnp.zeros((HB, width), F32)
        weights = (
            inner_plane * inner_plane, inner_plane * outer_plane, outer_plane * outer_plane
        )
        for slot in (1, 2, 3):
            here = coef[3](slot)
            kinds = (
                here * y_shifts(coef[1](slot), none),
                here * y_shifts(none, coef[1](slot)),
                here * coef[0](slot + 1),
                here * coef[0](slot - 1),
                here * y_shifts(coef[2](slot + 1), none),
                here * y_shifts(none, coef[2](slot + 1)),
                here * y_shifts(coef[2](slot - 1), none),
                here * y_shifts(none, coef[2](slot - 1)),
            )
            for n, kind in enumerate(kinds):
                for k, weight in enumerate(weights):
                    total(SHARED + 3 * n + k, slot, weight * kind)


def share_tiles(width):
    return -(-(SHARED + (1 if width == LB else 24)) // 2)


def edge_constants(inverse, rate):
    blocks = inverse.shape[0]
    links = [jnp.minimum(rate[:, b : b + 1], rate[:, b + 1 : b + 2]) for b in range(blocks - 1)]
    none = jnp.zeros((1, 1), F32)
    links = [none] + links + [none]
    found = []
    for b in range(blocks):
        top, bottom = inverse[b, 0:1], inverse[b, ZB - 1 : ZB]
        middle = inverse[b, HB - 1 : HB]
        bridge = middle[:, HB : HB + 1]
        below, above = links[b], links[b + 1]
        found += [
            top[:, HB : HB + 1] / bridge, bottom[:, HB - 1 : HB] / bridge,
            below * top[:, 0:1], above * top[:, ZB - 1 :],
            below * bottom[:, 0:1], above * bottom[:, ZB - 1 :],
            middle[:, ZB - 1 :], inverse[b, HB : HB + 1][:, 0:1],
            below, above, bridge,
        ]
    return found


KINDS = 11


def edge_couplings(edge_in, edge_out, numbers):
    blocks = numbers.shape[0] // KINDS

    def number(b, kind):
        return numbers[KINDS * b + kind : KINDS * b + kind + 1]

    first = [edge_out[2 * b] + number(b, 0) * edge_in[2 * b + 1] for b in range(blocks)]
    last = [edge_out[2 * b + 1] + number(b, 1) * edge_in[2 * b] for b in range(blocks)]
    down = [None] + [
        (number(b, 2), number(b, 3) if b < blocks - 1 else None) for b in range(1, blocks)
    ]
    ups = [(number(b, 4) if b else None, number(b, 5)) for b in range(blocks - 1)]
    u_first, u_last = list(first), list(last)
    for _ in range(SWEEPS - 1):
        n_first, n_last = list(first), list(last)
        for b in range(1, blocks):
            n_first[b] = first[b] + down[b][0] * u_last[b - 1]
            if down[b][1] is not None:
                n_first[b] = n_first[b] + down[b][1] * u_first[b + 1]
        for b in range(blocks - 1):
            n_last[b] = last[b] + ups[b][1] * u_first[b + 1]
            if ups[b][0] is not None:
                n_last[b] = n_last[b] + ups[b][0] * u_last[b - 1]
        u_first, u_last = n_first, n_last
    factors = []
    zero = jnp.zeros_like(first[0])
    for b in range(blocks):
        below = number(b, 8) * u_last[b - 1] if b else zero
        above = number(b, 9) * u_first[b + 1] if b < blocks - 1 else zero
        factors.append((edge_in[2 * b + 1] + number(b, 6) * above, below))
        factors.append((edge_in[2 * b] + number(b, 7) * below, above))
    return factors


def shift_lanes(tile, by):
    width = tile.shape[1]
    lane = lax.broadcasted_iota(jnp.int32, tile.shape, 1)
    if by > 0:
        return jnp.where(lane == width - 1, 0.0, pltpu.roll(tile, width - 1, 1))
    return jnp.where(lane == 0, 0.0, pltpu.roll(tile, 1, 1))


def finish_kernel(halves, *refs):
    shares = refs[:halves]
    (
        solved, centres, partial, outside, here, beside, distant, vectors, own, early, numbers,
    ) = refs[halves : halves + 11]
    out_v, out_w, board = refs[halves + 11 :]
    width = out_v.shape[1]
    me = lax.axis_index("gy")
    sign = orientation()
    for d in range(halves):
        board[d] = shares[d][...]

    def tile(half, kind):
        found = board[lax.bitwise_xor(half, me), kind // 2]
        return pltpu.roll(found, 4, 0) if kind % 2 else found

    every = range(halves)
    first = edge_couplings(
        [tile(h, EDGE_IN) for h in every], [tile(h, EDGE_OUT) for h in every], numbers
    )
    inner_plane, outer_plane = vectors[0], vectors[1]
    coef = coefficients(here, beside, distant)

    def pick(factors):
        chosen = factors[0]
        for h in range(1, halves):
            chosen = [jnp.where(me == h, new, old) for new, old in zip(factors[h], chosen)]
        return chosen

    alpha, beta = pick(first)
    added = [
        inner_plane * alpha[s : s + 1] + outer_plane * beta[s : s + 1] for s in range(SLOTS)
    ]
    nexts = [
        (partial[1] if s == 2 else outside[s // 2])
        + stencil(s, added, centres[s - 1], coef, sign)
        for s in (1, 2, 3)
    ]
    product = jnp.dot(
        own[...], jnp.concatenate(nexts, axis=1),
        precision=lax.Precision.HIGHEST, preferred_element_type=F32,
    )

    rolls = (7, 1)
    sums_in, sums_out = [], []
    half_sign = 0.5 * sign
    for h in every:
        totals = [tile(h, SUM_IN), tile(h, SUM_OUT)]
        if width == LB:
            packed = tile(h, SHARED)

            def shared(kind, k):
                at = 3 * kind + k
                return jnp.broadcast_to(packed[:, at : at + 1], (8, width))

            kinds = [0, 0, 1, 2, 3, 3, 4, 4]
        else:

            def shared(kind, k):
                return tile(h, SHARED + 3 * kind + k)

            kinds = range(8)
        for v, factor in enumerate(first[h]):
            high, low = shift_lanes(factor, 1), shift_lanes(factor, -1)
            up, down = (pltpu.roll(factor, r, 0) for r in rolls)
            up_high, down_high = (pltpu.roll(high, r, 0) for r in rolls)
            up_low, down_low = (pltpu.roll(low, r, 0) for r in rolls)
            for g in range(2):
                k = v + g
                spread = (
                    shared(kinds[2], k) * up
                    + shared(kinds[3], k) * down
                )
                if width == LB:
                    spread = spread + shared(0, k) * (high + low)
                    spread = spread + half_sign * (
                        shared(3, k) * (up_high - up_low) - shared(4, k) * (down_high - down_low)
                    )
                else:
                    spread = spread + shared(0, k) * high + shared(1, k) * low
                    spread = spread + half_sign * (
                        shared(4, k) * up_high - shared(5, k) * up_low
                        - shared(6, k) * down_high + shared(7, k) * down_low
                    )
                totals[g] = totals[g] + tile(h, WEIGHTS + k) * factor + TIME_STEP * spread
        at = KINDS * (h // 2) + 10
        sums_in.append(numbers[at : at + 1] * totals[0])
        sums_out.append(totals[1])
    alpha, beta = pick(edge_couplings(sums_in, sums_out, numbers))
    final = [None] * SLOTS
    for s in (1, 2, 3):
        final[s] = (
            product[:, (s - 1) * width : s * width]
            + inner_plane * alpha[s : s + 1]
            + outer_plane * beta[s : s + 1]
        )
    w = early[0] - early[1] * (solved[...] + added[2])
    out_w[...] = (1.0 - TIME_STEP * RECOVERY_RATE) * w - early[2] * final[2]
    out_v[...] = stencil(2, final, early[3], coef, sign) + (
        TIME_STEP * RECOVERY_RATE * EXCITATION
    ) * w


def swaps(lines, lanes, partner):
    found = []
    for i in range(lines):
        for j in range(lanes):
            k, m = partner(i, j)
            found.append((i * lanes + j, k * lanes + m))
    return found


def per_device(
    adj_voltage,
    adj_gating,
    fwd_voltage,
    fwd_gating,
    region_labels,
    region_axial,
    region_shear,
    block_rate,
    block_inverse,
):
    lanes, lines = lax.axis_size("gy"), lax.axis_size("gx")
    _, depth, width = adj_voltage.shape
    label_blocks = region_labels.shape[2]
    assert depth == HB and block_inverse.shape[1] == ZB and lines % 4 == 0
    shape = jax.ShapeDtypeStruct
    room = pltpu.CompilerParams(vmem_limit_bytes=(8 << 20) * (width // LB))
    in_hbm = lambda *arrays: [pltpu.with_memory_space_constraint(x, pltpu.HBM) for x in arrays]
    voltages, gatings = fwd_voltage[:, 0], fwd_gating[:, 0]
    late = pltpu.VMEM((HB, width), fwd_voltage.dtype)
    near = pl.pallas_call(
        first_kernel,
        out_shape=shape((3 * HB + 8, width), F32),
        in_specs=[HBM] * 5,
        out_specs=VMEM,
        scratch_shapes=[
            late, late, pltpu.VMEM((label_blocks, HB), jnp.int32), pltpu.SemaphoreType.DMA((5,)),
        ],
        compiler_params=room,
    )(*in_hbm(adj_voltage[0], adj_gating[0], voltages, gatings, region_labels[0].T))
    both = pltpu.VMEM((2, HB, width), fwd_voltage.dtype)
    axial, shear, numbers, vectors, own, own_rows, here, early = pl.pallas_call(
        aside_kernel,
        out_shape=(
            shape(region_axial.shape, F32), shape((1,) + region_shear.shape, F32),
            shape((KINDS * block_inverse.shape[0], width), F32),
            shape((2, HB, width), F32), shape((HB, HB), F32), shape((8, ZB), F32),
            shape((4, HB, width), F32), shape((4, HB, width), F32),
        ),
        in_specs=[VMEM] + [HBM] * 7,
        out_specs=(VMEM,) * 8,
        scratch_shapes=[
            pltpu.VMEM((HB, width), F32), both, both, pltpu.VMEM((8, LB), F32),
            pltpu.VMEM(block_inverse.shape, F32), pltpu.VMEM((1,) + block_rate.shape, F32),
            pltpu.SemaphoreType.DMA((7,)),
        ],
        compiler_params=room,
        cost_estimate=pl.CostEstimate(flops=1 << 20, bytes_accessed=1 << 20, transcendentals=0),
    )(
        near,
        *in_hbm(
            adj_gating[0], voltages, gatings, region_axial, region_shear[None], block_rate[None],
            block_inverse,
        ),
    )
    ends = (0, lines - 1)
    cycle = list(range(0, lines, 2)) + list(range(lines - 1, 0, -2))
    onward = {i: cycle[(n + 1) % lines] for n, i in enumerate(cycle)}
    pairing = swaps(lines, lanes, lambda i, j: (i ^ 1, j))
    after = lax.ppermute(
        near, BOTH,
        swaps(lines, lanes, lambda i, j: (i, j ^ 1) if i in ends else (i - 1 + 2 * (i % 2), j)),
    )
    before = lax.ppermute(near[:FAR], BOTH, swaps(lines, lanes, lambda i, j: (onward[i], j)))
    pair = lax.ppermute(near, BOTH, pairing)
    relayed, own_rows = lax.optimization_barrier((after[:FAR], own_rows))
    beyond = lax.ppermute(relayed, BOTH, pairing)
    count = -(-SLOTS * label_blocks // 8) * 8
    share_shape = (share_tiles(width), 8, width)
    label_scratch = [pltpu.VMEM((count, LB), F32)]
    begun, solved, centres, partial, beside = pl.pallas_call(
        gather_kernel,
        out_shape=(
            shape(share_shape, F32), shape((HB, width), F32), shape((3, HB, width), F32),
            shape((3, HB, width), F32), shape((8, HB, width), F32),
        ),
        in_specs=[VMEM] * 9,
        out_specs=(VMEM,) * 5,
        scratch_shapes=label_scratch,
        compiler_params=room,
        cost_estimate=pl.CostEstimate(flops=1 << 20, bytes_accessed=1 << 20, transcendentals=0),
    )(near, pair, after, axial, shear, vectors, own, own_rows, here)
    share, outside, distant = pl.pallas_call(
        complete_kernel,
        out_shape=(
            shape(share_shape, F32), shape((2, HB, width), F32), shape((4, HB, width), F32),
        ),
        in_specs=[VMEM] * 14,
        out_specs=(VMEM,) * 3,
        scratch_shapes=label_scratch,
        compiler_params=room,
    )(
        near, pair, after, before, beyond, axial, shear, vectors, own, own_rows, here, begun,
        partial, beside,
    )
    shares = [share] + [
        lax.ppermute(share, BOTH, swaps(lines, lanes, lambda i, j: (i, j ^ d)))
        for d in range(1, lanes)
    ]
    out_v, out_w = pl.pallas_call(
        lambda *refs: finish_kernel(lanes, *refs),
        out_shape=(shape((HB, width), F32),) * 2,
        in_specs=[VMEM] * (lanes + 11),
        out_specs=(VMEM,) * 2,
        scratch_shapes=[pltpu.VMEM((lanes,) + share_shape, F32)],
        compiler_params=room,
    )(
        *shares, solved, centres, partial, outside, here, beside, distant, vectors, own, early,
        numbers,
    )
    return (out_v[None], out_w[None])


def solution(mesh):
    return jax.shard_map(
        per_device,
        mesh=mesh,
        in_specs=(
            P("gx", "gy", None),
            P("gx", "gy", None),
            P(None, "gx", "gy", None),
            P(None, "gx", "gy", None),
            P("gx", "gy", None),
            P(),
            P(),
            P(),
            P(),
        ),
        out_specs=(P("gx", "gy", None), P("gx", "gy", None)),
        check_vma=False,
    )
```

```python
import jax
import jax.numpy as jnp
from jax import lax
from jax.experimental import pallas as pl
from jax.experimental.pallas import tpu as pltpu
from jax.sharding import PartitionSpec as P

SWEEPS = 11
ZB = 128
LB = 128
HB = 64
SLOTS = 5

TIME_STEP = 0.2
RECOVERY_RATE = 0.25
EXCITATION = 8.0
THRESHOLD = 0.15

BOTH = ("gx", "gy")
VMEM = pl.BlockSpec(memory_space=pltpu.VMEM)
HBM = pl.BlockSpec(memory_space=pltpu.HBM)
F32 = jnp.float32
FAR = HB + 8
GAIN, LEAD = pl.ds(FAR, HB), pl.ds(FAR + HB, HB)
EDGE_IN, SUM_IN, EDGE_OUT, SUM_OUT, WEIGHTS, SHARED = 0, 1, 2, 3, 4, 7


def gain(voltage, gating):
    slope = (
        EXCITATION
        * (-3.0 * voltage * voltage + 2.0 * (1.0 + THRESHOLD) * voltage - THRESHOLD)
        - gating
    )
    return 1.0 + TIME_STEP * slope


def start_copies(pairs, sems):
    copies = [pltpu.make_async_copy(a, b, sems.at[n]) for n, (a, b) in enumerate(pairs)]
    for copy in copies:
        copy.start()
    return copies


def first_kernel(voltage_in, gating_in, fwd_v_in, fwd_g_in, label_in, near, v, g, label, sems):
    later = fwd_v_in.shape[0] - 1
    copies = start_copies(
        [
            (fwd_v_in.at[later], v), (fwd_g_in.at[later], g), (label_in, label),
            (gating_in, near.at[LEAD]), (voltage_in, near.at[pl.ds(0, HB)]),
        ],
        sems,
    )
    for copy in copies[:3]:
        copy.wait()
    near[GAIN] = gain(v[...].astype(F32), g[...].astype(F32))
    blocks = label.shape[0]
    near[HB:FAR] = jnp.zeros((8, near.shape[1]), F32)
    near[HB : HB + blocks, 0:HB] = label[...].astype(F32)
    for copy in copies[3:]:
        copy.wait()


def lookup(label, axial, shear):
    zero = jnp.zeros(label.shape, F32)
    tables = [zero, zero, zero]
    for region in range(1, axial.shape[1]):
        here = label == float(region)
        for k, value in enumerate(
            (axial[0:1, region : region + 1], axial[1:2, region : region + 1],
             shear[0:1, region : region + 1])
        ):
            tables[k] = jnp.where(here, value, tables[k])
    tables.append((label > 0.0).astype(F32))
    return tables


def upright(row):
    z = lax.broadcasted_iota(jnp.int32, (HB, LB), 0)
    lane = lax.broadcasted_iota(jnp.int32, (HB, LB), 1)
    column = jnp.sum(jnp.where(z == lane, row, 0.0), axis=1, keepdims=True)
    return jnp.broadcast_to(column, (HB, LB))


def fill_plane(plane, table, at, label_blocks):
    for block in range(label_blocks):
        plane[:, block * LB : (block + 1) * LB] = upright(table[at + block : at + block + 1])


def aside_kernel(
    near, gating_in, fwd_v_in, fwd_g_in, axial_in, shear_in, rate_in, inverse_in,
    axial, shear, numbers, vectors, own, lines, planes, early, w, v, g, label, inverse, rate, sems,
):
    width = w.shape[1]
    label_blocks = width // LB
    me = lax.axis_index("gy")
    upper, mine = lax.rem(me, 2) == 1, lax.div(me, 2)
    for copy in start_copies(
        [
            (inverse_in, inverse), (axial_in, axial), (shear_in, shear), (rate_in, rate),
            (gating_in, w), (fwd_v_in, v), (fwd_g_in, g),
        ],
        sems,
    ):
        copy.wait()
    inner, outer, inner_column, outer_column, bridge, square = half_vectors(inverse, mine, upper)
    vectors[0] = jnp.broadcast_to(inner_column, (HB, width))
    vectors[1] = jnp.broadcast_to(outer_column, (HB, width))
    own[...] = left_parts(square)
    for n, value in enumerate(edge_constants(inverse, rate)):
        numbers[n : n + 1] = jnp.broadcast_to(value, (1, width))
    lines[0:1] = inner
    lines[1:2] = outer
    lines[2:3] = jnp.broadcast_to(bridge, (1, ZB))
    label[...] = jnp.zeros(label.shape, F32)
    label[0:label_blocks] = near[HB : HB + label_blocks, :LB]
    for k, table in enumerate(lookup(label[...], axial, shear)):
        fill_plane(planes.at[k], table, 0, label_blocks)
    tissue = planes[3]
    late_v, early_v = v[1].astype(F32), v[0].astype(F32)
    early[0] = (1.0 - TIME_STEP * RECOVERY_RATE) * (tissue * w[...])
    early[1] = TIME_STEP * (tissue * late_v)
    early[2] = TIME_STEP * (tissue * early_v)
    early[3] = tissue * gain(early_v, g[0].astype(F32)) - (2.0 * TIME_STEP) * (
        planes[0] + planes[1]
    )


def two_parts(value):
    high = value.astype(jnp.bfloat16)
    return high, (value - high.astype(F32)).astype(jnp.bfloat16)


def left_parts(matrix):
    high, low = two_parts(matrix)
    return jnp.concatenate([high, high, low, low], axis=1)


def times(parts, field):
    high, low = two_parts(field)
    return jnp.dot(
        parts, jnp.concatenate([high, low, high, low], axis=0), preferred_element_type=F32
    )


def half_vectors(inverse, mine, upper):
    def row(index):
        return inverse[mine, index : index + 1, :]

    bridge = row(HB - 1)[:, HB : HB + 1]
    inner = jnp.where(upper, pltpu.roll(row(HB - 1), HB, 1), row(HB)) / bridge
    outer = jnp.where(upper, pltpu.roll(row(ZB - 1), HB, 1), row(0))
    rows = inverse[mine, pl.ds(pl.multiple_of(jnp.where(upper, HB, 0), HB), HB), :]
    swapped = jnp.where(upper, pltpu.roll(rows, HB, 1), rows)
    inner_column = jnp.where(upper, swapped[:, ZB - 1 :], swapped[:, HB : HB + 1]) / bridge
    outer_column = jnp.where(upper, swapped[:, HB - 1 : HB], swapped[:, 0:1])
    return inner, outer, inner_column, outer_column, bridge, swapped[:, :HB]


def y_shifts(plus, minus):
    width = plus.shape[1]
    lane = lax.broadcasted_iota(jnp.int32, plus.shape, 1)
    return jnp.where(lane == width - 1, 0.0, pltpu.roll(plus, width - 1, 1)) + jnp.where(
        lane == 0, 0.0, pltpu.roll(minus, 1, 1)
    )


def stencil(slot, field, center, coef, sign):
    along, across, shear, tissue = coef
    level = TIME_STEP * (across(slot) * field[slot])
    twist, beside = 0.0, 0.0
    for step in (1, -1):
        other = slot + step
        if field[other] is not None:
            twist = twist + (step * 0.5 * TIME_STEP * sign) * (shear(other) * field[other])
            beside = beside + TIME_STEP * (along(other) * field[other])
    return center * field[slot] + tissue(slot) * (y_shifts(level + twist, level - twist) + beside)


def reach(slot, other, field, coef, sign):
    twist = ((other - slot) * 0.5 * TIME_STEP * sign) * (coef[2](other) * field)
    return coef[3](slot) * (y_shifts(twist, -twist) + TIME_STEP * (coef[0](other) * field))


def centre(gains, slot, coef):
    along, across, _, tissue = coef
    return tissue(slot) * gains - (2.0 * TIME_STEP) * (along(slot) + across(slot))


def coefficients(here, beside, beyond):
    def reader(k):
        def read(slot):
            if slot == 2:
                return here[k]
            if slot in (1, 3):
                return beside[2 * k + slot // 2]
            return beyond[k + slot // 4]

        return read

    return [reader(k) for k in range(4)]


def orientation():
    line = lax.axis_index("gx")
    return jnp.where(lax.rem(line, 2) == 0, 1.0, -1.0)


def put_total(share, kind, slot, value):
    row = slot + 4 * (kind % 2)
    share[kind // 2, row : row + 1, :] = jnp.sum(value, axis=0, keepdims=True)


def label_rows(rows, given, label_blocks):
    line, last = lax.axis_index("gx"), lax.axis_size("gx") - 1
    even = lax.rem(line, 2) == 0
    inside = {
        1: jnp.logical_and(line > 0, line < last),
        4: jnp.where(even, line + 2 <= last, line >= 2),
        0: jnp.where(even, line >= 2, line + 2 <= last),
    }
    rows[...] = jnp.zeros(rows.shape, F32)
    for slot, ref in given.items():
        label = ref[HB : HB + label_blocks, :LB]
        if slot in inside:
            label = jnp.where(inside[slot], label, 0.0)
        rows[slot * label_blocks : (slot + 1) * label_blocks] = label
    return rows[...]


def solve_planes(own, fields, width):
    product = times(own[...], jnp.concatenate(fields, axis=1))
    return [product[:, n * width : (n + 1) * width] for n in range(len(fields))]


def gather_kernel(
    near, pair, after, axial, shear, vectors, own, lines, here,
    share, solved, centres, partial, beside, rows,
):
    width = near.shape[1]
    label_blocks = width // LB
    given = {1: after, 2: near, 3: pair}
    tables = lookup(label_rows(rows, {1: after, 3: pair}, label_blocks), axial, shear)
    for k in range(4):
        for slot in (1, 3):
            fill_plane(beside.at[2 * k + slot // 2], tables[k], slot * label_blocks, label_blocks)
    coef = coefficients(here, beside, None)
    sign = orientation()
    bridge = lines[2:3, 0:1]
    inner_plane, outer_plane = vectors[0], vectors[1]
    fields = [given[slot][0:HB] for slot in (1, 2, 3)]
    parts = [None] + solve_planes(own, fields, width) + [None]
    solved[...] = parts[2]
    share[...] = jnp.zeros(share.shape, F32)
    for slot in (1, 2, 3):
        put_total(share, EDGE_IN, slot, bridge * (inner_plane * fields[slot - 1]))
        put_total(share, EDGE_OUT, slot, outer_plane * fields[slot - 1])
    weights = (inner_plane * inner_plane, inner_plane * outer_plane, outer_plane * outer_plane)
    for slot in (1, 2, 3):
        center = centre(given[slot][GAIN], slot, coef)
        lead = (TIME_STEP * RECOVERY_RATE * EXCITATION) * given[slot][LEAD]
        part = stencil(slot, parts, center, coef, sign) + coef[3](slot) * lead
        centres[slot - 1] = center
        partial[slot - 1] = part
        if slot == 2:
            put_total(share, SUM_IN, slot, inner_plane * part)
            put_total(share, SUM_OUT, slot, outer_plane * part)
        for k, weight in enumerate(weights):
            put_total(share, WEIGHTS + k, slot, weight * center)


def complete_kernel(
    near, pair, after, before, beyond, axial, shear, vectors, own, lines, here,
    begun, most, beside, share, outside, distant, rows,
):
    width = near.shape[1]
    label_blocks = width // LB
    given = {0: before, 1: after, 2: near, 3: pair, 4: beyond}
    tables = lookup(label_rows(rows, given, label_blocks), axial, shear)
    for k in range(2):
        for slot in (0, 4):
            fill_plane(
                distant.at[2 * k + slot // 4], tables[2 * k], slot * label_blocks, label_blocks
            )
    coef = coefficients(here, beside, distant)
    sign = orientation()
    inner, outer, bridge = lines[0:1], lines[1:2], lines[2:3, 0:1]
    inner_plane, outer_plane = vectors[0], vectors[1]
    share[...] = begun[...]

    def total(kind, slot, value):
        put_total(share, kind, slot, value)

    fields = [before[0:HB], beyond[0:HB]]
    parts = solve_planes(own, fields, width)
    for n, slot in enumerate((0, 4)):
        total(EDGE_IN, slot, bridge * (inner_plane * fields[n]))
        total(EDGE_OUT, slot, outer_plane * fields[n])
        middle = 1 + 2 * n
        part = most[middle - 1] + reach(middle, slot, parts[n], coef, sign)
        outside[n] = part
        total(SUM_IN, middle, inner_plane * part)
        total(SUM_OUT, middle, outer_plane * part)
    if label_blocks == 1:
        lane = lax.broadcasted_iota(jnp.int32, (1, ZB), 1)
        inner = jnp.where(lane < HB, inner, 0.0)
        outer = jnp.where(lane < HB, outer, 0.0)
        pairs = (inner * inner, inner * outer, outer * outer)
        along, across, shears, tissue = tables
        up, down = rows.shape[0] - 1, 1
        kinds = (
            across,
            tissue * pltpu.roll(along, up, 0),
            tissue * pltpu.roll(along, down, 0),
            tissue * pltpu.roll(shears, up, 0),
            tissue * pltpu.roll(shears, down, 0),
        )
        lanes = lax.broadcasted_iota(jnp.int32, (8, ZB), 1)
        packed = jnp.zeros((8, ZB), F32)
        for n, kind in enumerate(kinds):
            for k, vector in enumerate(pairs):
                value = jnp.sum(kind * vector, axis=1, keepdims=True)
                packed = jnp.where(lanes == 3 * n + k, value, packed)
        share[SHARED // 2, 5:8] = packed[1:4]
    else:
        none = jnp.zeros((HB, width), F32)
        weights = (
            inner_plane * inner_plane, inner_plane * outer_plane, outer_plane * outer_plane
        )
        for slot in (1, 2, 3):
            here = coef[3](slot)
            kinds = (
                here * y_shifts(coef[1](slot), none),
                here * y_shifts(none, coef[1](slot)),
                here * coef[0](slot + 1),
                here * coef[0](slot - 1),
                here * y_shifts(coef[2](slot + 1), none),
                here * y_shifts(none, coef[2](slot + 1)),
                here * y_shifts(coef[2](slot - 1), none),
                here * y_shifts(none, coef[2](slot - 1)),
            )
            for n, kind in enumerate(kinds):
                for k, weight in enumerate(weights):
                    total(SHARED + 3 * n + k, slot, weight * kind)


def share_tiles(width):
    return -(-(SHARED + (1 if width == LB else 24)) // 2)


def edge_constants(inverse, rate):
    blocks = inverse.shape[0]
    links = [jnp.minimum(rate[:, b : b + 1], rate[:, b + 1 : b + 2]) for b in range(blocks - 1)]
    none = jnp.zeros((1, 1), F32)
    links = [none] + links + [none]
    found = []
    for b in range(blocks):
        top, bottom = inverse[b, 0:1], inverse[b, ZB - 1 : ZB]
        middle = inverse[b, HB - 1 : HB]
        bridge = middle[:, HB : HB + 1]
        below, above = links[b], links[b + 1]
        found += [
            top[:, HB : HB + 1] / bridge, bottom[:, HB - 1 : HB] / bridge,
            below * top[:, 0:1], above * top[:, ZB - 1 :],
            below * bottom[:, 0:1], above * bottom[:, ZB - 1 :],
            middle[:, ZB - 1 :], inverse[b, HB : HB + 1][:, 0:1],
            below, above, bridge,
        ]
    return found


KINDS = 11


def edge_couplings(edge_in, edge_out, numbers):
    blocks = numbers.shape[0] // KINDS

    def number(b, kind):
        return numbers[KINDS * b + kind : KINDS * b + kind + 1]

    first = [edge_out[2 * b] + number(b, 0) * edge_in[2 * b + 1] for b in range(blocks)]
    last = [edge_out[2 * b + 1] + number(b, 1) * edge_in[2 * b] for b in range(blocks)]
    down = [None] + [
        (number(b, 2), number(b, 3) if b < blocks - 1 else None) for b in range(1, blocks)
    ]
    ups = [(number(b, 4) if b else None, number(b, 5)) for b in range(blocks - 1)]
    u_first, u_last = list(first), list(last)
    for _ in range(SWEEPS - 1):
        n_first, n_last = list(first), list(last)
        for b in range(1, blocks):
            n_first[b] = first[b] + down[b][0] * u_last[b - 1]
            if down[b][1] is not None:
                n_first[b] = n_first[b] + down[b][1] * u_first[b + 1]
        for b in range(blocks - 1):
            n_last[b] = last[b] + ups[b][1] * u_first[b + 1]
            if ups[b][0] is not None:
                n_last[b] = n_last[b] + ups[b][0] * u_last[b - 1]
        u_first, u_last = n_first, n_last
    factors = []
    zero = jnp.zeros_like(first[0])
    for b in range(blocks):
        below = number(b, 8) * u_last[b - 1] if b else zero
        above = number(b, 9) * u_first[b + 1] if b < blocks - 1 else zero
        factors.append((edge_in[2 * b + 1] + number(b, 6) * above, below))
        factors.append((edge_in[2 * b] + number(b, 7) * below, above))
    return factors


def shift_lanes(tile, by):
    width = tile.shape[1]
    lane = lax.broadcasted_iota(jnp.int32, tile.shape, 1)
    if by > 0:
        return jnp.where(lane == width - 1, 0.0, pltpu.roll(tile, width - 1, 1))
    return jnp.where(lane == 0, 0.0, pltpu.roll(tile, 1, 1))


def finish_kernel(halves, *refs):
    shares = refs[:halves]
    (
        solved, centres, partial, outside, here, beside, distant, vectors, own, early, numbers,
    ) = refs[halves : halves + 11]
    out_v, out_w, board = refs[halves + 11 :]
    width = out_v.shape[1]
    me = lax.axis_index("gy")
    sign = orientation()
    for d in range(halves):
        board[d] = shares[d][...]

    def tile(half, kind):
        found = board[lax.bitwise_xor(half, me), kind // 2]
        return pltpu.roll(found, 4, 0) if kind % 2 else found

    every = range(halves)
    first = edge_couplings(
        [tile(h, EDGE_IN) for h in every], [tile(h, EDGE_OUT) for h in every], numbers
    )
    inner_plane, outer_plane = vectors[0], vectors[1]
    coef = coefficients(here, beside, distant)

    def pick(factors):
        chosen = factors[0]
        for h in range(1, halves):
            chosen = [jnp.where(me == h, new, old) for new, old in zip(factors[h], chosen)]
        return chosen

    alpha, beta = pick(first)
    added = [
        inner_plane * alpha[s : s + 1] + outer_plane * beta[s : s + 1] for s in range(SLOTS)
    ]
    nexts = [
        (partial[1] if s == 2 else outside[s // 2])
        + stencil(s, added, centres[s - 1], coef, sign)
        for s in (1, 2, 3)
    ]
    product = times(own[...], jnp.concatenate(nexts, axis=1))

    rolls = (7, 1)
    sums_in, sums_out = [], []
    half_sign = 0.5 * sign
    for h in every:
        totals = [tile(h, SUM_IN), tile(h, SUM_OUT)]
        if width == LB:
            packed = tile(h, SHARED)

            def shared(kind, k):
                at = 3 * kind + k
                return jnp.broadcast_to(packed[:, at : at + 1], (8, width))

            kinds = [0, 0, 1, 2, 3, 3, 4, 4]
        else:

            def shared(kind, k):
                return tile(h, SHARED + 3 * kind + k)

            kinds = range(8)
        for v, factor in enumerate(first[h]):
            high, low = shift_lanes(factor, 1), shift_lanes(factor, -1)
            up, down = (pltpu.roll(factor, r, 0) for r in rolls)
            up_high, down_high = (pltpu.roll(high, r, 0) for r in rolls)
            up_low, down_low = (pltpu.roll(low, r, 0) for r in rolls)
            for g in range(2):
                k = v + g
                spread = (
                    shared(kinds[2], k) * up
                    + shared(kinds[3], k) * down
                )
                if width == LB:
                    spread = spread + shared(0, k) * (high + low)
                    spread = spread + half_sign * (
                        shared(3, k) * (up_high - up_low) - shared(4, k) * (down_high - down_low)
                    )
                else:
                    spread = spread + shared(0, k) * high + shared(1, k) * low
                    spread = spread + half_sign * (
                        shared(4, k) * up_high - shared(5, k) * up_low
                        - shared(6, k) * down_high + shared(7, k) * down_low
                    )
                totals[g] = totals[g] + tile(h, WEIGHTS + k) * factor + TIME_STEP * spread
        at = KINDS * (h // 2) + 10
        sums_in.append(numbers[at : at + 1] * totals[0])
        sums_out.append(totals[1])
    alpha, beta = pick(edge_couplings(sums_in, sums_out, numbers))
    final = [None] * SLOTS
    for s in (1, 2, 3):
        final[s] = (
            product[:, (s - 1) * width : s * width]
            + inner_plane * alpha[s : s + 1]
            + outer_plane * beta[s : s + 1]
        )
    w = early[0] - early[1] * (solved[...] + added[2])
    out_w[...] = (1.0 - TIME_STEP * RECOVERY_RATE) * w - early[2] * final[2]
    out_v[...] = stencil(2, final, early[3], coef, sign) + (
        TIME_STEP * RECOVERY_RATE * EXCITATION
    ) * w


def swaps(lines, lanes, partner):
    found = []
    for i in range(lines):
        for j in range(lanes):
            k, m = partner(i, j)
            found.append((i * lanes + j, k * lanes + m))
    return found


def per_device(
    adj_voltage,
    adj_gating,
    fwd_voltage,
    fwd_gating,
    region_labels,
    region_axial,
    region_shear,
    block_rate,
    block_inverse,
):
    lanes, lines = lax.axis_size("gy"), lax.axis_size("gx")
    _, depth, width = adj_voltage.shape
    label_blocks = region_labels.shape[2]
    assert depth == HB and block_inverse.shape[1] == ZB and lines % 4 == 0
    shape = jax.ShapeDtypeStruct
    room = pltpu.CompilerParams(vmem_limit_bytes=(8 << 20) * (width // LB))
    in_hbm = lambda *arrays: [pltpu.with_memory_space_constraint(x, pltpu.HBM) for x in arrays]
    voltages, gatings = fwd_voltage[:, 0], fwd_gating[:, 0]
    late = pltpu.VMEM((HB, width), fwd_voltage.dtype)
    near = pl.pallas_call(
        first_kernel,
        out_shape=shape((3 * HB + 8, width), F32),
        in_specs=[HBM] * 5,
        out_specs=VMEM,
        scratch_shapes=[
            late, late, pltpu.VMEM((label_blocks, HB), jnp.int32), pltpu.SemaphoreType.DMA((5,)),
        ],
        compiler_params=room,
    )(*in_hbm(adj_voltage[0], adj_gating[0], voltages, gatings, region_labels[0].T))
    both = pltpu.VMEM((2, HB, width), fwd_voltage.dtype)
    axial, shear, numbers, vectors, own, own_rows, here, early = pl.pallas_call(
        aside_kernel,
        out_shape=(
            shape(region_axial.shape, F32), shape((1,) + region_shear.shape, F32),
            shape((KINDS * block_inverse.shape[0], width), F32),
            shape((2, HB, width), F32), shape((HB, 4 * HB), jnp.bfloat16), shape((8, ZB), F32),
            shape((4, HB, width), F32), shape((4, HB, width), F32),
        ),
        in_specs=[VMEM] + [HBM] * 7,
        out_specs=(VMEM,) * 8,
        scratch_shapes=[
            pltpu.VMEM((HB, width), F32), both, both, pltpu.VMEM((8, LB), F32),
            pltpu.VMEM(block_inverse.shape, F32), pltpu.VMEM((1,) + block_rate.shape, F32),
            pltpu.SemaphoreType.DMA((7,)),
        ],
        compiler_params=room,
        cost_estimate=pl.CostEstimate(flops=1 << 20, bytes_accessed=1 << 20, transcendentals=0),
    )(
        near,
        *in_hbm(
            adj_gating[0], voltages, gatings, region_axial, region_shear[None], block_rate[None],
            block_inverse,
        ),
    )
    ends = (0, lines - 1)
    cycle = list(range(0, lines, 2)) + list(range(lines - 1, 0, -2))
    onward = {i: cycle[(n + 1) % lines] for n, i in enumerate(cycle)}
    pairing = swaps(lines, lanes, lambda i, j: (i ^ 1, j))
    after = lax.ppermute(
        near, BOTH,
        swaps(lines, lanes, lambda i, j: (i, j ^ 1) if i in ends else (i - 1 + 2 * (i % 2), j)),
    )
    before = lax.ppermute(near[:FAR], BOTH, swaps(lines, lanes, lambda i, j: (onward[i], j)))
    pair = lax.ppermute(near, BOTH, pairing)
    relayed, own_rows = lax.optimization_barrier((after[:FAR], own_rows))
    beyond = lax.ppermute(relayed, BOTH, pairing)
    count = -(-SLOTS * label_blocks // 8) * 8
    share_shape = (share_tiles(width), 8, width)
    label_scratch = [pltpu.VMEM((count, LB), F32)]
    begun, solved, centres, partial, beside = pl.pallas_call(
        gather_kernel,
        out_shape=(
            shape(share_shape, F32), shape((HB, width), F32), shape((3, HB, width), F32),
            shape((3, HB, width), F32), shape((8, HB, width), F32),
        ),
        in_specs=[VMEM] * 9,
        out_specs=(VMEM,) * 5,
        scratch_shapes=label_scratch,
        compiler_params=room,
        cost_estimate=pl.CostEstimate(flops=1 << 20, bytes_accessed=1 << 20, transcendentals=0),
    )(near, pair, after, axial, shear, vectors, own, own_rows, here)
    share, outside, distant = pl.pallas_call(
        complete_kernel,
        out_shape=(
            shape(share_shape, F32), shape((2, HB, width), F32), shape((4, HB, width), F32),
        ),
        in_specs=[VMEM] * 14,
        out_specs=(VMEM,) * 3,
        scratch_shapes=label_scratch,
        compiler_params=room,
    )(
        near, pair, after, before, beyond, axial, shear, vectors, own, own_rows, here, begun,
        partial, beside,
    )
    shares = [share] + [
        lax.ppermute(share, BOTH, swaps(lines, lanes, lambda i, j: (i, j ^ d)))
        for d in range(1, lanes)
    ]
    out_v, out_w = pl.pallas_call(
        lambda *refs: finish_kernel(lanes, *refs),
        out_shape=(shape((HB, width), F32),) * 2,
        in_specs=[VMEM] * (lanes + 11),
        out_specs=(VMEM,) * 2,
        scratch_shapes=[pltpu.VMEM((lanes,) + share_shape, F32)],
        compiler_params=room,
    )(
        *shares, solved, centres, partial, outside, here, beside, distant, vectors, own, early,
        numbers,
    )
    return (out_v[None], out_w[None])


def solution(mesh):
    return jax.shard_map(
        per_device,
        mesh=mesh,
        in_specs=(
            P("gx", "gy", None),
            P("gx", "gy", None),
            P(None, "gx", "gy", None),
            P(None, "gx", "gy", None),
            P("gx", "gy", None),
            P(),
            P(),
            P(),
            P(),
        ),
        out_specs=(P("gx", "gy", None), P("gx", "gy", None)),
        check_vma=False,
    )
```

```python
import jax
import jax.numpy as jnp
from jax import lax
from jax.experimental import pallas as pl
from jax.experimental.pallas import tpu as pltpu
from jax.sharding import PartitionSpec as P

SWEEPS = 11
ZB = 128
LB = 128
HB = 64
SLOTS = 5

TIME_STEP = 0.2
RECOVERY_RATE = 0.25
EXCITATION = 8.0
THRESHOLD = 0.15

BOTH = ("gx", "gy")
VMEM = pl.BlockSpec(memory_space=pltpu.VMEM)
HBM = pl.BlockSpec(memory_space=pltpu.HBM)
F32 = jnp.float32
FAR = HB + 8
GAIN, LEAD = pl.ds(FAR, HB), pl.ds(FAR + HB, HB)
EDGE_IN, SUM_IN, EDGE_OUT, SUM_OUT, WEIGHTS, SHARED = 0, 1, 2, 3, 4, 7


def gain(voltage, gating):
    slope = (
        EXCITATION
        * (-3.0 * voltage * voltage + 2.0 * (1.0 + THRESHOLD) * voltage - THRESHOLD)
        - gating
    )
    return 1.0 + TIME_STEP * slope


def start_copies(pairs, sems):
    copies = [pltpu.make_async_copy(a, b, sems.at[n]) for n, (a, b) in enumerate(pairs)]
    for copy in copies:
        copy.start()
    return copies


def first_kernel(fwd_v_in, fwd_g_in, label_in, tile, gains, v, g, label, sems):
    later = fwd_v_in.shape[0] - 1
    copies = start_copies([(fwd_v_in.at[later], v), (fwd_g_in.at[later], g), (label_in, label)], sems)
    for copy in copies:
        copy.wait()
    gains[...] = gain(v[...].astype(F32), g[...].astype(F32))
    blocks = label.shape[0]
    tile[...] = jnp.zeros(tile.shape, F32)
    tile[0:blocks, 0:HB] = label[...].astype(F32)


def lookup(label, regions):
    count = regions.shape[0] // 3
    zero = jnp.zeros(label.shape, F32)
    tables = [zero, zero, zero]
    for region in range(1, count):
        here = label == float(region)
        for k in range(3):
            at = k * count + region
            tables[k] = jnp.where(here, regions[at : at + 1], tables[k])
    tables.append((label > 0.0).astype(F32))
    return tables


def upright(row):
    z = lax.broadcasted_iota(jnp.int32, (HB, LB), 0)
    lane = lax.broadcasted_iota(jnp.int32, (HB, LB), 1)
    column = jnp.sum(jnp.where(z == lane, row, 0.0), axis=1, keepdims=True)
    return jnp.broadcast_to(column, (HB, LB))


def fill_plane(plane, table, at, label_blocks):
    for block in range(label_blocks):
        plane[:, block * LB : (block + 1) * LB] = upright(table[at + block : at + block + 1])


def aside_kernel(
    near, gating_in, fwd_v_in, fwd_g_in, axial_in, shear_in, rate_in, inverse_in,
    regions, numbers, vectors, own, lines, planes, early,
    w, v, g, label, inverse, rate, axial, shear, sems,
):
    width = w.shape[1]
    label_blocks = width // LB
    me = lax.axis_index("gy")
    upper, mine = lax.rem(me, 2) == 1, lax.div(me, 2)
    for copy in start_copies(
        [
            (inverse_in, inverse), (axial_in, axial), (shear_in, shear), (rate_in, rate),
            (gating_in, w), (fwd_v_in, v), (fwd_g_in, g),
        ],
        sems,
    ):
        copy.wait()
    inner, outer, inner_column, outer_column, bridge, square = half_vectors(inverse, mine, upper)
    vectors[0] = jnp.broadcast_to(inner_column, (HB, width))
    vectors[1] = jnp.broadcast_to(outer_column, (HB, width))
    own[...] = left_parts(square)
    for n, value in enumerate(edge_constants(inverse, rate)):
        numbers[n : n + 1] = jnp.broadcast_to(value, (1, width))
    lines[0:1] = inner
    lines[1:2] = outer
    lines[2:3] = jnp.broadcast_to(bridge, (1, ZB))
    count = axial.shape[1]
    for region in range(count):
        for k, table in enumerate((axial[0:1], axial[1:2], shear[...])):
            at = k * count + region
            regions[at : at + 1] = jnp.broadcast_to(table[:, region : region + 1], (1, LB))
    label[...] = jnp.zeros(label.shape, F32)
    label[0:label_blocks] = near[HB : HB + label_blocks, :LB]
    for k, table in enumerate(lookup(label[...], regions)):
        fill_plane(planes.at[k], table, 0, label_blocks)
    tissue = planes[3]
    late_v, early_v = v[1].astype(F32), v[0].astype(F32)
    early[0] = (1.0 - TIME_STEP * RECOVERY_RATE) * (tissue * w[...])
    early[1] = TIME_STEP * (tissue * late_v)
    early[2] = TIME_STEP * (tissue * early_v)
    early[3] = tissue * gain(early_v, g[0].astype(F32)) - (2.0 * TIME_STEP) * (
        planes[0] + planes[1]
    )


def two_parts(value):
    high = value.astype(jnp.bfloat16)
    return high, (value - high.astype(F32)).astype(jnp.bfloat16)


def left_parts(matrix):
    high, low = two_parts(matrix)
    return jnp.concatenate([high, high, low, low], axis=1)


def times(parts, field):
    high, low = two_parts(field)
    return jnp.dot(
        parts, jnp.concatenate([high, low, high, low], axis=0), preferred_element_type=F32
    )


def half_vectors(inverse, mine, upper):
    def row(index):
        return inverse[mine, index : index + 1, :]

    bridge = row(HB - 1)[:, HB : HB + 1]
    inner = jnp.where(upper, pltpu.roll(row(HB - 1), HB, 1), row(HB)) / bridge
    outer = jnp.where(upper, pltpu.roll(row(ZB - 1), HB, 1), row(0))
    rows = inverse[mine, pl.ds(pl.multiple_of(jnp.where(upper, HB, 0), HB), HB), :]
    swapped = jnp.where(upper, pltpu.roll(rows, HB, 1), rows)
    inner_column = jnp.where(upper, swapped[:, ZB - 1 :], swapped[:, HB : HB + 1]) / bridge
    outer_column = jnp.where(upper, swapped[:, HB - 1 : HB], swapped[:, 0:1])
    return inner, outer, inner_column, outer_column, bridge, swapped[:, :HB]


def y_shifts(plus, minus):
    width = plus.shape[1]
    lane = lax.broadcasted_iota(jnp.int32, plus.shape, 1)
    return jnp.where(lane == width - 1, 0.0, pltpu.roll(plus, width - 1, 1)) + jnp.where(
        lane == 0, 0.0, pltpu.roll(minus, 1, 1)
    )


def stencil(slot, field, center, coef, sign):
    along, across, shear, tissue = coef
    level = TIME_STEP * (across(slot) * field[slot])
    twist, beside = 0.0, 0.0
    for step in (1, -1):
        other = slot + step
        if field[other] is not None:
            twist = twist + (step * 0.5 * TIME_STEP * sign) * (shear(other) * field[other])
            beside = beside + TIME_STEP * (along(other) * field[other])
    return center * field[slot] + tissue(slot) * (y_shifts(level + twist, level - twist) + beside)


def reach(slot, other, field, coef, sign):
    twist = ((other - slot) * 0.5 * TIME_STEP * sign) * (coef[2](other) * field)
    return coef[3](slot) * (y_shifts(twist, -twist) + TIME_STEP * (coef[0](other) * field))


def centre(gains, slot, coef):
    along, across, _, tissue = coef
    return tissue(slot) * gains - (2.0 * TIME_STEP) * (along(slot) + across(slot))


def coefficients(here, beside, beyond):
    def reader(k):
        def read(slot):
            if slot == 2:
                return here[k]
            if slot in (1, 3):
                return beside[2 * k + slot // 2]
            return beyond[k + slot // 4]

        return read

    return [reader(k) for k in range(4)]


def orientation():
    line = lax.axis_index("gx")
    return jnp.where(lax.rem(line, 2) == 0, 1.0, -1.0)


def put_total(share, kind, slot, value):
    row = slot + 4 * (kind % 2)
    share[kind // 2, row : row + 1, :] = jnp.sum(value, axis=0, keepdims=True)


def label_rows(rows, given, label_blocks):
    line, last = lax.axis_index("gx"), lax.axis_size("gx") - 1
    even = lax.rem(line, 2) == 0
    inside = {
        1: jnp.logical_and(line > 0, line < last),
        4: jnp.where(even, line + 2 <= last, line >= 2),
        0: jnp.where(even, line >= 2, line + 2 <= last),
    }
    rows[...] = jnp.zeros(rows.shape, F32)
    for slot, ref in given.items():
        label = ref[HB : HB + label_blocks, :LB]
        if slot in inside:
            label = jnp.where(inside[slot], label, 0.0)
        rows[slot * label_blocks : (slot + 1) * label_blocks] = label
    return rows[...]


def solve_planes(own, fields, width):
    product = times(own[...], jnp.concatenate(fields, axis=1))
    return [product[:, n * width : (n + 1) * width] for n in range(len(fields))]


def gather_kernel(
    near, pair, after, regions, vectors, own, lines, here,
    share, solved, centres, partial, beside, rows,
):
    width = near.shape[1]
    label_blocks = width // LB
    given = {1: after, 2: near, 3: pair}
    tables = lookup(label_rows(rows, {1: after, 3: pair}, label_blocks), regions)
    for k in range(4):
        for slot in (1, 3):
            fill_plane(beside.at[2 * k + slot // 2], tables[k], slot * label_blocks, label_blocks)
    coef = coefficients(here, beside, None)
    sign = orientation()
    bridge = lines[2:3, 0:1]
    inner_plane, outer_plane = vectors[0], vectors[1]
    fields = [given[slot][0:HB] for slot in (1, 2, 3)]
    parts = [None] + solve_planes(own, fields, width) + [None]
    solved[...] = parts[2]
    share[...] = jnp.zeros(share.shape, F32)
    for slot in (1, 2, 3):
        put_total(share, EDGE_IN, slot, bridge * (inner_plane * fields[slot - 1]))
        put_total(share, EDGE_OUT, slot, outer_plane * fields[slot - 1])
    weights = (inner_plane * inner_plane, inner_plane * outer_plane, outer_plane * outer_plane)
    for slot in (1, 2, 3):
        center = centre(given[slot][GAIN], slot, coef)
        lead = (TIME_STEP * RECOVERY_RATE * EXCITATION) * given[slot][LEAD]
        part = stencil(slot, parts, center, coef, sign) + coef[3](slot) * lead
        centres[slot - 1] = center
        partial[slot - 1] = part
        if slot == 2:
            put_total(share, SUM_IN, slot, inner_plane * part)
            put_total(share, SUM_OUT, slot, outer_plane * part)
        for k, weight in enumerate(weights):
            put_total(share, WEIGHTS + k, slot, weight * center)


def complete_kernel(
    near, pair, after, before, beyond, regions, vectors, own, lines, here,
    begun, most, beside, share, outside, distant, rows,
):
    width = near.shape[1]
    label_blocks = width // LB
    given = {0: before, 1: after, 2: near, 3: pair, 4: beyond}
    tables = lookup(label_rows(rows, given, label_blocks), regions)
    for k in range(2):
        for slot in (0, 4):
            fill_plane(
                distant.at[2 * k + slot // 4], tables[2 * k], slot * label_blocks, label_blocks
            )
    coef = coefficients(here, beside, distant)
    sign = orientation()
    inner, outer, bridge = lines[0:1], lines[1:2], lines[2:3, 0:1]
    inner_plane, outer_plane = vectors[0], vectors[1]
    share[...] = begun[...]

    def total(kind, slot, value):
        put_total(share, kind, slot, value)

    fields = [before[0:HB], beyond[0:HB]]
    parts = solve_planes(own, fields, width)
    for n, slot in enumerate((0, 4)):
        total(EDGE_IN, slot, bridge * (inner_plane * fields[n]))
        total(EDGE_OUT, slot, outer_plane * fields[n])
        middle = 1 + 2 * n
        part = most[middle - 1] + reach(middle, slot, parts[n], coef, sign)
        outside[n] = part
        total(SUM_IN, middle, inner_plane * part)
        total(SUM_OUT, middle, outer_plane * part)
    if label_blocks == 1:
        lane = lax.broadcasted_iota(jnp.int32, (1, ZB), 1)
        inner = jnp.where(lane < HB, inner, 0.0)
        outer = jnp.where(lane < HB, outer, 0.0)
        pairs = (inner * inner, inner * outer, outer * outer)
        along, across, shears, tissue = tables
        up, down = rows.shape[0] - 1, 1
        kinds = (
            across,
            tissue * pltpu.roll(along, up, 0),
            tissue * pltpu.roll(along, down, 0),
            tissue * pltpu.roll(shears, up, 0),
            tissue * pltpu.roll(shears, down, 0),
        )
        lanes = lax.broadcasted_iota(jnp.int32, (8, ZB), 1)
        packed = jnp.zeros((8, ZB), F32)
        for n, kind in enumerate(kinds):
            for k, vector in enumerate(pairs):
                value = jnp.sum(kind * vector, axis=1, keepdims=True)
                packed = jnp.where(lanes == 3 * n + k, value, packed)
        share[SHARED // 2, 5:8] = packed[1:4]
    else:
        none = jnp.zeros((HB, width), F32)
        weights = (
            inner_plane * inner_plane, inner_plane * outer_plane, outer_plane * outer_plane
        )
        for slot in (1, 2, 3):
            here = coef[3](slot)
            kinds = (
                here * y_shifts(coef[1](slot), none),
                here * y_shifts(none, coef[1](slot)),
                here * coef[0](slot + 1),
                here * coef[0](slot - 1),
                here * y_shifts(coef[2](slot + 1), none),
                here * y_shifts(none, coef[2](slot + 1)),
                here * y_shifts(coef[2](slot - 1), none),
                here * y_shifts(none, coef[2](slot - 1)),
            )
            for n, kind in enumerate(kinds):
                for k, weight in enumerate(weights):
                    total(SHARED + 3 * n + k, slot, weight * kind)


def share_tiles(width):
    return -(-(SHARED + (1 if width == LB else 24)) // 2)


def edge_constants(inverse, rate):
    blocks = inverse.shape[0]
    links = [jnp.minimum(rate[:, b : b + 1], rate[:, b + 1 : b + 2]) for b in range(blocks - 1)]
    none = jnp.zeros((1, 1), F32)
    links = [none] + links + [none]
    found = []
    for b in range(blocks):
        top, bottom = inverse[b, 0:1], inverse[b, ZB - 1 : ZB]
        middle = inverse[b, HB - 1 : HB]
        bridge = middle[:, HB : HB + 1]
        below, above = links[b], links[b + 1]
        found += [
            top[:, HB : HB + 1] / bridge, bottom[:, HB - 1 : HB] / bridge,
            below * top[:, 0:1], above * top[:, ZB - 1 :],
            below * bottom[:, 0:1], above * bottom[:, ZB - 1 :],
            middle[:, ZB - 1 :], inverse[b, HB : HB + 1][:, 0:1],
            below, above, bridge,
        ]
    return found


KINDS = 11


def edge_couplings(edge_in, edge_out, numbers):
    blocks = numbers.shape[0] // KINDS

    def number(b, kind):
        return numbers[KINDS * b + kind : KINDS * b + kind + 1]

    first = [edge_out[2 * b] + number(b, 0) * edge_in[2 * b + 1] for b in range(blocks)]
    last = [edge_out[2 * b + 1] + number(b, 1) * edge_in[2 * b] for b in range(blocks)]
    down = [None] + [
        (number(b, 2), number(b, 3) if b < blocks - 1 else None) for b in range(1, blocks)
    ]
    ups = [(number(b, 4) if b else None, number(b, 5)) for b in range(blocks - 1)]
    u_first, u_last = list(first), list(last)
    for _ in range(SWEEPS - 1):
        n_first, n_last = list(first), list(last)
        for b in range(1, blocks):
            n_first[b] = first[b] + down[b][0] * u_last[b - 1]
            if down[b][1] is not None:
                n_first[b] = n_first[b] + down[b][1] * u_first[b + 1]
        for b in range(blocks - 1):
            n_last[b] = last[b] + ups[b][1] * u_first[b + 1]
            if ups[b][0] is not None:
                n_last[b] = n_last[b] + ups[b][0] * u_last[b - 1]
        u_first, u_last = n_first, n_last
    factors = []
    zero = jnp.zeros_like(first[0])
    for b in range(blocks):
        below = number(b, 8) * u_last[b - 1] if b else zero
        above = number(b, 9) * u_first[b + 1] if b < blocks - 1 else zero
        factors.append((edge_in[2 * b + 1] + number(b, 6) * above, below))
        factors.append((edge_in[2 * b] + number(b, 7) * below, above))
    return factors


def shift_lanes(tile, by):
    width = tile.shape[1]
    lane = lax.broadcasted_iota(jnp.int32, tile.shape, 1)
    if by > 0:
        return jnp.where(lane == width - 1, 0.0, pltpu.roll(tile, width - 1, 1))
    return jnp.where(lane == 0, 0.0, pltpu.roll(tile, 1, 1))


def finish_kernel(halves, *refs):
    shares = refs[:halves]
    (
        solved, centres, partial, outside, here, beside, distant, vectors, own, early, numbers,
    ) = refs[halves : halves + 11]
    out_v, out_w, board = refs[halves + 11 :]
    width = out_v.shape[1]
    me = lax.axis_index("gy")
    sign = orientation()
    for d in range(halves):
        board[d] = shares[d][...]

    def tile(half, kind):
        found = board[lax.bitwise_xor(half, me), kind // 2]
        return pltpu.roll(found, 4, 0) if kind % 2 else found

    every = range(halves)
    first = edge_couplings(
        [tile(h, EDGE_IN) for h in every], [tile(h, EDGE_OUT) for h in every], numbers
    )
    inner_plane, outer_plane = vectors[0], vectors[1]
    coef = coefficients(here, beside, distant)

    def pick(factors):
        chosen = factors[0]
        for h in range(1, halves):
            chosen = [jnp.where(me == h, new, old) for new, old in zip(factors[h], chosen)]
        return chosen

    alpha, beta = pick(first)
    added = [
        inner_plane * alpha[s : s + 1] + outer_plane * beta[s : s + 1] for s in range(SLOTS)
    ]
    nexts = [
        (partial[1] if s == 2 else outside[s // 2])
        + stencil(s, added, centres[s - 1], coef, sign)
        for s in (1, 2, 3)
    ]
    product = times(own[...], jnp.concatenate(nexts, axis=1))

    rolls = (7, 1)
    sums_in, sums_out = [], []
    half_sign = 0.5 * sign
    for h in every:
        totals = [tile(h, SUM_IN), tile(h, SUM_OUT)]
        if width == LB:
            packed = tile(h, SHARED)

            def shared(kind, k):
                at = 3 * kind + k
                return jnp.broadcast_to(packed[:, at : at + 1], (8, width))

            kinds = [0, 0, 1, 2, 3, 3, 4, 4]
        else:

            def shared(kind, k):
                return tile(h, SHARED + 3 * kind + k)

            kinds = range(8)
        for v, factor in enumerate(first[h]):
            high, low = shift_lanes(factor, 1), shift_lanes(factor, -1)
            up, down = (pltpu.roll(factor, r, 0) for r in rolls)
            up_high, down_high = (pltpu.roll(high, r, 0) for r in rolls)
            up_low, down_low = (pltpu.roll(low, r, 0) for r in rolls)
            for g in range(2):
                k = v + g
                spread = (
                    shared(kinds[2], k) * up
                    + shared(kinds[3], k) * down
                )
                if width == LB:
                    spread = spread + shared(0, k) * (high + low)
                    spread = spread + half_sign * (
                        shared(3, k) * (up_high - up_low) - shared(4, k) * (down_high - down_low)
                    )
                else:
                    spread = spread + shared(0, k) * high + shared(1, k) * low
                    spread = spread + half_sign * (
                        shared(4, k) * up_high - shared(5, k) * up_low
                        - shared(6, k) * down_high + shared(7, k) * down_low
                    )
                totals[g] = totals[g] + tile(h, WEIGHTS + k) * factor + TIME_STEP * spread
        at = KINDS * (h // 2) + 10
        sums_in.append(numbers[at : at + 1] * totals[0])
        sums_out.append(totals[1])
    alpha, beta = pick(edge_couplings(sums_in, sums_out, numbers))
    final = [None] * SLOTS
    for s in (1, 2, 3):
        final[s] = (
            product[:, (s - 1) * width : s * width]
            + inner_plane * alpha[s : s + 1]
            + outer_plane * beta[s : s + 1]
        )
    w = early[0] - early[1] * (solved[...] + added[2])
    out_w[...] = (1.0 - TIME_STEP * RECOVERY_RATE) * w - early[2] * final[2]
    out_v[...] = stencil(2, final, early[3], coef, sign) + (
        TIME_STEP * RECOVERY_RATE * EXCITATION
    ) * w


def swaps(lines, lanes, partner):
    found = []
    for i in range(lines):
        for j in range(lanes):
            k, m = partner(i, j)
            found.append((i * lanes + j, k * lanes + m))
    return found


def per_device(
    adj_voltage,
    adj_gating,
    fwd_voltage,
    fwd_gating,
    region_labels,
    region_axial,
    region_shear,
    block_rate,
    block_inverse,
):
    lanes, lines = lax.axis_size("gy"), lax.axis_size("gx")
    _, depth, width = adj_voltage.shape
    label_blocks = region_labels.shape[2]
    assert depth == HB and block_inverse.shape[1] == ZB and lines % 4 == 0
    shape = jax.ShapeDtypeStruct
    room = pltpu.CompilerParams(vmem_limit_bytes=(8 << 20) * (width // LB))
    in_hbm = lambda *arrays: [pltpu.with_memory_space_constraint(x, pltpu.HBM) for x in arrays]
    voltages, gatings = fwd_voltage[:, 0], fwd_gating[:, 0]
    late = pltpu.VMEM((HB, width), fwd_voltage.dtype)
    tile, gains = pl.pallas_call(
        first_kernel,
        out_shape=(shape((8, width), F32), shape((HB, width), F32)),
        in_specs=[HBM] * 3,
        out_specs=(VMEM,) * 2,
        scratch_shapes=[
            late, late, pltpu.VMEM((label_blocks, HB), jnp.int32), pltpu.SemaphoreType.DMA((3,)),
        ],
        compiler_params=room,
    )(*in_hbm(voltages, gatings, region_labels[0].T))
    near = jnp.concatenate([adj_voltage[0], tile, gains, adj_gating[0]], axis=0)
    both = pltpu.VMEM((2, HB, width), fwd_voltage.dtype)
    regions, numbers, vectors, own, own_rows, here, early = pl.pallas_call(
        aside_kernel,
        out_shape=(
            shape((3 * region_axial.shape[1], LB), F32),
            shape((KINDS * block_inverse.shape[0], width), F32),
            shape((2, HB, width), F32), shape((HB, 4 * HB), jnp.bfloat16), shape((8, ZB), F32),
            shape((4, HB, width), F32), shape((4, HB, width), F32),
        ),
        in_specs=[VMEM] + [HBM] * 7,
        out_specs=(VMEM,) * 7,
        scratch_shapes=[
            pltpu.VMEM((HB, width), F32), both, both, pltpu.VMEM((8, LB), F32),
            pltpu.VMEM(block_inverse.shape, F32), pltpu.VMEM((1,) + block_rate.shape, F32),
            pltpu.VMEM(region_axial.shape, F32), pltpu.VMEM((1,) + region_shear.shape, F32),
            pltpu.SemaphoreType.DMA((7,)),
        ],
        compiler_params=room,
        cost_estimate=pl.CostEstimate(flops=1 << 20, bytes_accessed=1 << 20, transcendentals=0),
    )(
        near,
        *in_hbm(
            adj_gating[0], voltages, gatings, region_axial, region_shear[None], block_rate[None],
            block_inverse,
        ),
    )
    ends = (0, lines - 1)
    cycle = list(range(0, lines, 2)) + list(range(lines - 1, 0, -2))
    onward = {i: cycle[(n + 1) % lines] for n, i in enumerate(cycle)}
    pairing = swaps(lines, lanes, lambda i, j: (i ^ 1, j))
    after = lax.ppermute(
        near, BOTH,
        swaps(lines, lanes, lambda i, j: (i, j ^ 1) if i in ends else (i - 1 + 2 * (i % 2), j)),
    )
    before = lax.ppermute(near[:FAR], BOTH, swaps(lines, lanes, lambda i, j: (onward[i], j)))
    pair = lax.ppermute(near, BOTH, pairing)
    relayed, own_rows = lax.optimization_barrier((after[:FAR], own_rows))
    beyond = lax.ppermute(relayed, BOTH, pairing)
    count = -(-SLOTS * label_blocks // 8) * 8
    share_shape = (share_tiles(width), 8, width)
    label_scratch = [pltpu.VMEM((count, LB), F32)]
    begun, solved, centres, partial, beside = pl.pallas_call(
        gather_kernel,
        out_shape=(
            shape(share_shape, F32), shape((HB, width), F32), shape((3, HB, width), F32),
            shape((3, HB, width), F32), shape((8, HB, width), F32),
        ),
        in_specs=[VMEM] * 8,
        out_specs=(VMEM,) * 5,
        scratch_shapes=label_scratch,
        compiler_params=room,
        cost_estimate=pl.CostEstimate(flops=1 << 20, bytes_accessed=1 << 20, transcendentals=0),
    )(near, pair, after, regions, vectors, own, own_rows, here)
    share, outside, distant = pl.pallas_call(
        complete_kernel,
        out_shape=(
            shape(share_shape, F32), shape((2, HB, width), F32), shape((4, HB, width), F32),
        ),
        in_specs=[VMEM] * 13,
        out_specs=(VMEM,) * 3,
        scratch_shapes=label_scratch,
        compiler_params=room,
    )(
        near, pair, after, before, beyond, regions, vectors, own, own_rows, here, begun,
        partial, beside,
    )
    shares = [share] + [
        lax.ppermute(share, BOTH, swaps(lines, lanes, lambda i, j: (i, j ^ d)))
        for d in range(1, lanes)
    ]
    out_v, out_w = pl.pallas_call(
        lambda *refs: finish_kernel(lanes, *refs),
        out_shape=(shape((HB, width), F32),) * 2,
        in_specs=[VMEM] * (lanes + 11),
        out_specs=(VMEM,) * 2,
        scratch_shapes=[pltpu.VMEM((lanes,) + share_shape, F32)],
        compiler_params=room,
    )(
        *shares, solved, centres, partial, outside, here, beside, distant, vectors, own, early,
        numbers,
    )
    return (out_v[None], out_w[None])


def solution(mesh):
    return jax.shard_map(
        per_device,
        mesh=mesh,
        in_specs=(
            P("gx", "gy", None),
            P("gx", "gy", None),
            P(None, "gx", "gy", None),
            P(None, "gx", "gy", None),
            P("gx", "gy", None),
            P(),
            P(),
            P(),
            P(),
        ),
        out_specs=(P("gx", "gy", None), P("gx", "gy", None)),
        check_vma=False,
    )
```

```python
import jax
import jax.numpy as jnp
from jax import lax
from jax.experimental import pallas as pl
from jax.experimental.pallas import tpu as pltpu
from jax.sharding import PartitionSpec as P

SWEEPS = 11
ZB = 128
LB = 128
HB = 64
SLOTS = 5

TIME_STEP = 0.2
RECOVERY_RATE = 0.25
EXCITATION = 8.0
THRESHOLD = 0.15

BOTH = ("gx", "gy")
VMEM = pl.BlockSpec(memory_space=pltpu.VMEM)
HBM = pl.BlockSpec(memory_space=pltpu.HBM)
F32 = jnp.float32
FAR = HB + 8
GAIN, LEAD = pl.ds(FAR, HB), pl.ds(FAR + HB, HB)
EDGE_IN, SUM_IN, EDGE_OUT, SUM_OUT, WEIGHTS, SHARED = 0, 1, 2, 3, 4, 7


def gain(voltage, gating):
    slope = (
        EXCITATION
        * (-3.0 * voltage * voltage + 2.0 * (1.0 + THRESHOLD) * voltage - THRESHOLD)
        - gating
    )
    return 1.0 + TIME_STEP * slope


def start_copies(pairs, sems):
    copies = [pltpu.make_async_copy(a, b, sems.at[n]) for n, (a, b) in enumerate(pairs)]
    for copy in copies:
        copy.start()
    return copies


def first_kernel(fwd_v_in, fwd_g_in, label_in, tile, gains, v, g, label, sems):
    later = fwd_v_in.shape[0] - 1
    copies = start_copies([(fwd_v_in.at[later], v), (fwd_g_in.at[later], g), (label_in, label)], sems)
    for copy in copies:
        copy.wait()
    gains[...] = gain(v[...].astype(F32), g[...].astype(F32))
    blocks = label.shape[0]
    tile[...] = jnp.zeros(tile.shape, F32)
    tile[0:blocks, 0:HB] = label[...].astype(F32)


def lookup(label, regions):
    count = regions.shape[0] // 3
    zero = jnp.zeros(label.shape, F32)
    tables = [zero, zero, zero]
    for region in range(1, count):
        here = label == float(region)
        for k in range(3):
            at = k * count + region
            tables[k] = jnp.where(here, regions[at : at + 1], tables[k])
    tables.append((label > 0.0).astype(F32))
    return tables


def upright(row):
    z = lax.broadcasted_iota(jnp.int32, (HB, LB), 0)
    lane = lax.broadcasted_iota(jnp.int32, (HB, LB), 1)
    column = jnp.sum(jnp.where(z == lane, row, 0.0), axis=1, keepdims=True)
    return jnp.broadcast_to(column, (HB, LB))


def fill_plane(plane, table, at, label_blocks):
    for block in range(label_blocks):
        plane[:, block * LB : (block + 1) * LB] = upright(table[at + block : at + block + 1])


def aside_kernel(
    near, inverse, gating_in, fwd_v_in, fwd_g_in, axial_in, shear_in, rate_in,
    regions, numbers, vectors, own, lines, planes, early,
    w, v, g, label, rate, axial, shear, sems,
):
    width = w.shape[1]
    label_blocks = width // LB
    me = lax.axis_index("gy")
    upper, mine = lax.rem(me, 2) == 1, lax.div(me, 2)
    for copy in start_copies(
        [
            (axial_in, axial), (shear_in, shear), (rate_in, rate),
            (gating_in, w), (fwd_v_in, v), (fwd_g_in, g),
        ],
        sems,
    ):
        copy.wait()
    inner, outer, inner_column, outer_column, bridge, square = half_vectors(inverse, mine, upper)
    vectors[0] = jnp.broadcast_to(inner_column, (HB, width))
    vectors[1] = jnp.broadcast_to(outer_column, (HB, width))
    own[...] = left_parts(square)
    for n, value in enumerate(edge_constants(inverse, rate)):
        numbers[n : n + 1] = jnp.broadcast_to(value, (1, width))
    lines[0:1] = inner
    lines[1:2] = outer
    lines[2:3] = jnp.broadcast_to(bridge, (1, ZB))
    count = axial.shape[1]
    for region in range(count):
        for k, table in enumerate((axial[0:1], axial[1:2], shear[...])):
            at = k * count + region
            regions[at : at + 1] = jnp.broadcast_to(table[:, region : region + 1], (1, LB))
    label[...] = jnp.zeros(label.shape, F32)
    label[0:label_blocks] = near[HB : HB + label_blocks, :LB]
    for k, table in enumerate(lookup(label[...], regions)):
        fill_plane(planes.at[k], table, 0, label_blocks)
    tissue = planes[3]
    late_v, early_v = v[1].astype(F32), v[0].astype(F32)
    early[0] = (1.0 - TIME_STEP * RECOVERY_RATE) * (tissue * w[...])
    early[1] = TIME_STEP * (tissue * late_v)
    early[2] = TIME_STEP * (tissue * early_v)
    early[3] = tissue * gain(early_v, g[0].astype(F32)) - (2.0 * TIME_STEP) * (
        planes[0] + planes[1]
    )


def two_parts(value):
    high = value.astype(jnp.bfloat16)
    return high, (value - high.astype(F32)).astype(jnp.bfloat16)


def left_parts(matrix):
    high, low = two_parts(matrix)
    return jnp.concatenate([high, high, low, low], axis=1)


def times(parts, field):
    high, low = two_parts(field)
    return jnp.dot(
        parts, jnp.concatenate([high, low, high, low], axis=0), preferred_element_type=F32
    )


def half_vectors(inverse, mine, upper):
    def row(index):
        return inverse[mine, index : index + 1, :]

    bridge = row(HB - 1)[:, HB : HB + 1]
    inner = jnp.where(upper, pltpu.roll(row(HB - 1), HB, 1), row(HB)) / bridge
    outer = jnp.where(upper, pltpu.roll(row(ZB - 1), HB, 1), row(0))
    rows = inverse[mine, pl.ds(pl.multiple_of(jnp.where(upper, HB, 0), HB), HB), :]
    swapped = jnp.where(upper, pltpu.roll(rows, HB, 1), rows)
    inner_column = jnp.where(upper, swapped[:, ZB - 1 :], swapped[:, HB : HB + 1]) / bridge
    outer_column = jnp.where(upper, swapped[:, HB - 1 : HB], swapped[:, 0:1])
    return inner, outer, inner_column, outer_column, bridge, swapped[:, :HB]


def y_shifts(plus, minus):
    width = plus.shape[1]
    lane = lax.broadcasted_iota(jnp.int32, plus.shape, 1)
    return jnp.where(lane == width - 1, 0.0, pltpu.roll(plus, width - 1, 1)) + jnp.where(
        lane == 0, 0.0, pltpu.roll(minus, 1, 1)
    )


def stencil(slot, field, center, coef, sign):
    along, across, shear, tissue = coef
    level = TIME_STEP * (across(slot) * field[slot])
    twist, beside = 0.0, 0.0
    for step in (1, -1):
        other = slot + step
        if field[other] is not None:
            twist = twist + (step * 0.5 * TIME_STEP * sign) * (shear(other) * field[other])
            beside = beside + TIME_STEP * (along(other) * field[other])
    return center * field[slot] + tissue(slot) * (y_shifts(level + twist, level - twist) + beside)


def reach(slot, other, field, coef, sign):
    twist = ((other - slot) * 0.5 * TIME_STEP * sign) * (coef[2](other) * field)
    return coef[3](slot) * (y_shifts(twist, -twist) + TIME_STEP * (coef[0](other) * field))


def centre(gains, slot, coef):
    along, across, _, tissue = coef
    return tissue(slot) * gains - (2.0 * TIME_STEP) * (along(slot) + across(slot))


def coefficients(here, beside, beyond):
    def reader(k):
        def read(slot):
            if slot == 2:
                return here[k]
            if slot in (1, 3):
                return beside[2 * k + slot // 2]
            return beyond[k + slot // 4]

        return read

    return [reader(k) for k in range(4)]


def orientation():
    line = lax.axis_index("gx")
    return jnp.where(lax.rem(line, 2) == 0, 1.0, -1.0)


def put_total(share, kind, slot, value):
    row = slot + 4 * (kind % 2)
    share[kind // 2, row : row + 1, :] = jnp.sum(value, axis=0, keepdims=True)


def label_rows(rows, given, label_blocks):
    line, last = lax.axis_index("gx"), lax.axis_size("gx") - 1
    even = lax.rem(line, 2) == 0
    inside = {
        1: jnp.logical_and(line > 0, line < last),
        4: jnp.where(even, line + 2 <= last, line >= 2),
        0: jnp.where(even, line >= 2, line + 2 <= last),
    }
    rows[...] = jnp.zeros(rows.shape, F32)
    for slot, ref in given.items():
        label = ref[HB : HB + label_blocks, :LB]
        if slot in inside:
            label = jnp.where(inside[slot], label, 0.0)
        rows[slot * label_blocks : (slot + 1) * label_blocks] = label
    return rows[...]


def solve_planes(own, fields, width):
    product = times(own[...], jnp.concatenate(fields, axis=1))
    return [product[:, n * width : (n + 1) * width] for n in range(len(fields))]


def gather_kernel(
    near, pair, after, regions, vectors, own, lines, here,
    share, solved, centres, partial, beside, rows,
):
    width = near.shape[1]
    label_blocks = width // LB
    given = {1: after, 2: near, 3: pair}
    tables = lookup(label_rows(rows, {1: after, 3: pair}, label_blocks), regions)
    for k in range(4):
        for slot in (1, 3):
            fill_plane(beside.at[2 * k + slot // 2], tables[k], slot * label_blocks, label_blocks)
    coef = coefficients(here, beside, None)
    sign = orientation()
    bridge = lines[2:3, 0:1]
    inner_plane, outer_plane = vectors[0], vectors[1]
    fields = [given[slot][0:HB] for slot in (1, 2, 3)]
    parts = [None] + solve_planes(own, fields, width) + [None]
    solved[...] = parts[2]
    share[...] = jnp.zeros(share.shape, F32)
    for slot in (1, 2, 3):
        put_total(share, EDGE_IN, slot, bridge * (inner_plane * fields[slot - 1]))
        put_total(share, EDGE_OUT, slot, outer_plane * fields[slot - 1])
    weights = (inner_plane * inner_plane, inner_plane * outer_plane, outer_plane * outer_plane)
    for slot in (1, 2, 3):
        center = centre(given[slot][GAIN], slot, coef)
        lead = (TIME_STEP * RECOVERY_RATE * EXCITATION) * given[slot][LEAD]
        part = stencil(slot, parts, center, coef, sign) + coef[3](slot) * lead
        centres[slot - 1] = center
        partial[slot - 1] = part
        if slot == 2:
            put_total(share, SUM_IN, slot, inner_plane * part)
            put_total(share, SUM_OUT, slot, outer_plane * part)
        for k, weight in enumerate(weights):
            put_total(share, WEIGHTS + k, slot, weight * center)


def complete_kernel(
    near, pair, after, before, beyond, regions, vectors, own, lines, here,
    begun, most, beside, share, outside, distant, rows,
):
    width = near.shape[1]
    label_blocks = width // LB
    given = {0: before, 1: after, 2: near, 3: pair, 4: beyond}
    tables = lookup(label_rows(rows, given, label_blocks), regions)
    for k in range(2):
        for slot in (0, 4):
            fill_plane(
                distant.at[2 * k + slot // 4], tables[2 * k], slot * label_blocks, label_blocks
            )
    coef = coefficients(here, beside, distant)
    sign = orientation()
    inner, outer, bridge = lines[0:1], lines[1:2], lines[2:3, 0:1]
    inner_plane, outer_plane = vectors[0], vectors[1]
    share[...] = begun[...]

    def total(kind, slot, value):
        put_total(share, kind, slot, value)

    fields = [before[0:HB], beyond[0:HB]]
    parts = solve_planes(own, fields, width)
    for n, slot in enumerate((0, 4)):
        total(EDGE_IN, slot, bridge * (inner_plane * fields[n]))
        total(EDGE_OUT, slot, outer_plane * fields[n])
        middle = 1 + 2 * n
        part = most[middle - 1] + reach(middle, slot, parts[n], coef, sign)
        outside[n] = part
        total(SUM_IN, middle, inner_plane * part)
        total(SUM_OUT, middle, outer_plane * part)
    if label_blocks == 1:
        lane = lax.broadcasted_iota(jnp.int32, (1, ZB), 1)
        inner = jnp.where(lane < HB, inner, 0.0)
        outer = jnp.where(lane < HB, outer, 0.0)
        pairs = (inner * inner, inner * outer, outer * outer)
        along, across, shears, tissue = tables
        up, down = rows.shape[0] - 1, 1
        kinds = (
            across,
            tissue * pltpu.roll(along, up, 0),
            tissue * pltpu.roll(along, down, 0),
            tissue * pltpu.roll(shears, up, 0),
            tissue * pltpu.roll(shears, down, 0),
        )
        lanes = lax.broadcasted_iota(jnp.int32, (8, ZB), 1)
        packed = jnp.zeros((8, ZB), F32)
        for n, kind in enumerate(kinds):
            for k, vector in enumerate(pairs):
                value = jnp.sum(kind * vector, axis=1, keepdims=True)
                packed = jnp.where(lanes == 3 * n + k, value, packed)
        share[SHARED // 2, 5:8] = packed[1:4]
    else:
        none = jnp.zeros((HB, width), F32)
        weights = (
            inner_plane * inner_plane, inner_plane * outer_plane, outer_plane * outer_plane
        )
        for slot in (1, 2, 3):
            here = coef[3](slot)
            kinds = (
                here * y_shifts(coef[1](slot), none),
                here * y_shifts(none, coef[1](slot)),
                here * coef[0](slot + 1),
                here * coef[0](slot - 1),
                here * y_shifts(coef[2](slot + 1), none),
                here * y_shifts(none, coef[2](slot + 1)),
                here * y_shifts(coef[2](slot - 1), none),
                here * y_shifts(none, coef[2](slot - 1)),
            )
            for n, kind in enumerate(kinds):
                for k, weight in enumerate(weights):
                    total(SHARED + 3 * n + k, slot, weight * kind)


def share_tiles(width):
    return -(-(SHARED + (1 if width == LB else 24)) // 2)


def edge_constants(inverse, rate):
    blocks = inverse.shape[0]
    links = [jnp.minimum(rate[:, b : b + 1], rate[:, b + 1 : b + 2]) for b in range(blocks - 1)]
    none = jnp.zeros((1, 1), F32)
    links = [none] + links + [none]
    found = []
    for b in range(blocks):
        top, bottom = inverse[b, 0:1], inverse[b, ZB - 1 : ZB]
        middle = inverse[b, HB - 1 : HB]
        bridge = middle[:, HB : HB + 1]
        below, above = links[b], links[b + 1]
        found += [
            top[:, HB : HB + 1] / bridge, bottom[:, HB - 1 : HB] / bridge,
            below * top[:, 0:1], above * top[:, ZB - 1 :],
            below * bottom[:, 0:1], above * bottom[:, ZB - 1 :],
            middle[:, ZB - 1 :], inverse[b, HB : HB + 1][:, 0:1],
            below, above, bridge,
        ]
    return found


KINDS = 11


def edge_couplings(edge_in, edge_out, numbers):
    blocks = numbers.shape[0] // KINDS

    def number(b, kind):
        return numbers[KINDS * b + kind : KINDS * b + kind + 1]

    first = [edge_out[2 * b] + number(b, 0) * edge_in[2 * b + 1] for b in range(blocks)]
    last = [edge_out[2 * b + 1] + number(b, 1) * edge_in[2 * b] for b in range(blocks)]
    down = [None] + [
        (number(b, 2), number(b, 3) if b < blocks - 1 else None) for b in range(1, blocks)
    ]
    ups = [(number(b, 4) if b else None, number(b, 5)) for b in range(blocks - 1)]
    u_first, u_last = list(first), list(last)
    for _ in range(SWEEPS - 1):
        n_first, n_last = list(first), list(last)
        for b in range(1, blocks):
            n_first[b] = first[b] + down[b][0] * u_last[b - 1]
            if down[b][1] is not None:
                n_first[b] = n_first[b] + down[b][1] * u_first[b + 1]
        for b in range(blocks - 1):
            n_last[b] = last[b] + ups[b][1] * u_first[b + 1]
            if ups[b][0] is not None:
                n_last[b] = n_last[b] + ups[b][0] * u_last[b - 1]
        u_first, u_last = n_first, n_last
    factors = []
    zero = jnp.zeros_like(first[0])
    for b in range(blocks):
        below = number(b, 8) * u_last[b - 1] if b else zero
        above = number(b, 9) * u_first[b + 1] if b < blocks - 1 else zero
        factors.append((edge_in[2 * b + 1] + number(b, 6) * above, below))
        factors.append((edge_in[2 * b] + number(b, 7) * below, above))
    return factors


def shift_lanes(tile, by):
    width = tile.shape[1]
    lane = lax.broadcasted_iota(jnp.int32, tile.shape, 1)
    if by > 0:
        return jnp.where(lane == width - 1, 0.0, pltpu.roll(tile, width - 1, 1))
    return jnp.where(lane == 0, 0.0, pltpu.roll(tile, 1, 1))


def finish_kernel(halves, *refs):
    shares = refs[:halves]
    (
        solved, centres, partial, outside, here, beside, distant, vectors, own, early, numbers,
    ) = refs[halves : halves + 11]
    out_v, out_w, board = refs[halves + 11 :]
    width = out_v.shape[1]
    me = lax.axis_index("gy")
    sign = orientation()
    for d in range(halves):
        board[d] = shares[d][...]

    def tile(half, kind):
        found = board[lax.bitwise_xor(half, me), kind // 2]
        return pltpu.roll(found, 4, 0) if kind % 2 else found

    every = range(halves)
    first = edge_couplings(
        [tile(h, EDGE_IN) for h in every], [tile(h, EDGE_OUT) for h in every], numbers
    )
    inner_plane, outer_plane = vectors[0], vectors[1]
    coef = coefficients(here, beside, distant)

    def pick(factors):
        chosen = factors[0]
        for h in range(1, halves):
            chosen = [jnp.where(me == h, new, old) for new, old in zip(factors[h], chosen)]
        return chosen

    alpha, beta = pick(first)
    added = [
        inner_plane * alpha[s : s + 1] + outer_plane * beta[s : s + 1] for s in range(SLOTS)
    ]
    nexts = [
        (partial[1] if s == 2 else outside[s // 2])
        + stencil(s, added, centres[s - 1], coef, sign)
        for s in (1, 2, 3)
    ]
    product = times(own[...], jnp.concatenate(nexts, axis=1))

    rolls = (7, 1)
    sums_in, sums_out = [], []
    half_sign = 0.5 * sign
    for h in every:
        totals = [tile(h, SUM_IN), tile(h, SUM_OUT)]
        if width == LB:
            packed = tile(h, SHARED)

            def shared(kind, k):
                at = 3 * kind + k
                return jnp.broadcast_to(packed[:, at : at + 1], (8, width))

            kinds = [0, 0, 1, 2, 3, 3, 4, 4]
        else:

            def shared(kind, k):
                return tile(h, SHARED + 3 * kind + k)

            kinds = range(8)
        for v, factor in enumerate(first[h]):
            high, low = shift_lanes(factor, 1), shift_lanes(factor, -1)
            up, down = (pltpu.roll(factor, r, 0) for r in rolls)
            up_high, down_high = (pltpu.roll(high, r, 0) for r in rolls)
            up_low, down_low = (pltpu.roll(low, r, 0) for r in rolls)
            for g in range(2):
                k = v + g
                spread = (
                    shared(kinds[2], k) * up
                    + shared(kinds[3], k) * down
                )
                if width == LB:
                    spread = spread + shared(0, k) * (high + low)
                    spread = spread + half_sign * (
                        shared(3, k) * (up_high - up_low) - shared(4, k) * (down_high - down_low)
                    )
                else:
                    spread = spread + shared(0, k) * high + shared(1, k) * low
                    spread = spread + half_sign * (
                        shared(4, k) * up_high - shared(5, k) * up_low
                        - shared(6, k) * down_high + shared(7, k) * down_low
                    )
                totals[g] = totals[g] + tile(h, WEIGHTS + k) * factor + TIME_STEP * spread
        at = KINDS * (h // 2) + 10
        sums_in.append(numbers[at : at + 1] * totals[0])
        sums_out.append(totals[1])
    alpha, beta = pick(edge_couplings(sums_in, sums_out, numbers))
    final = [None] * SLOTS
    for s in (1, 2, 3):
        final[s] = (
            product[:, (s - 1) * width : s * width]
            + inner_plane * alpha[s : s + 1]
            + outer_plane * beta[s : s + 1]
        )
    w = early[0] - early[1] * (solved[...] + added[2])
    out_w[...] = (1.0 - TIME_STEP * RECOVERY_RATE) * w - early[2] * final[2]
    out_v[...] = stencil(2, final, early[3], coef, sign) + (
        TIME_STEP * RECOVERY_RATE * EXCITATION
    ) * w


def swaps(lines, lanes, partner):
    found = []
    for i in range(lines):
        for j in range(lanes):
            k, m = partner(i, j)
            found.append((i * lanes + j, k * lanes + m))
    return found


def per_device(
    adj_voltage,
    adj_gating,
    fwd_voltage,
    fwd_gating,
    region_labels,
    region_axial,
    region_shear,
    block_rate,
    block_inverse,
):
    lanes, lines = lax.axis_size("gy"), lax.axis_size("gx")
    _, depth, width = adj_voltage.shape
    label_blocks = region_labels.shape[2]
    assert depth == HB and block_inverse.shape[1] == ZB and lines % 4 == 0
    shape = jax.ShapeDtypeStruct
    room = pltpu.CompilerParams(vmem_limit_bytes=(8 << 20) * (width // LB))
    in_hbm = lambda *arrays: [pltpu.with_memory_space_constraint(x, pltpu.HBM) for x in arrays]
    voltages, gatings = fwd_voltage[:, 0], fwd_gating[:, 0]
    late = pltpu.VMEM((HB, width), fwd_voltage.dtype)
    tile, gains = pl.pallas_call(
        first_kernel,
        out_shape=(shape((8, width), F32), shape((HB, width), F32)),
        in_specs=[HBM] * 3,
        out_specs=(VMEM,) * 2,
        scratch_shapes=[
            late, late, pltpu.VMEM((label_blocks, HB), jnp.int32), pltpu.SemaphoreType.DMA((3,)),
        ],
        compiler_params=room,
    )(*in_hbm(voltages, gatings, region_labels[0].T))
    near = jnp.concatenate([adj_voltage[0], tile, gains, adj_gating[0]], axis=0)
    both = pltpu.VMEM((2, HB, width), fwd_voltage.dtype)
    regions, numbers, vectors, own, own_rows, here, early = pl.pallas_call(
        aside_kernel,
        out_shape=(
            shape((3 * region_axial.shape[1], LB), F32),
            shape((KINDS * block_inverse.shape[0], width), F32),
            shape((2, HB, width), F32), shape((HB, 4 * HB), jnp.bfloat16), shape((8, ZB), F32),
            shape((4, HB, width), F32), shape((4, HB, width), F32),
        ),
        in_specs=[VMEM] * 2 + [HBM] * 6,
        out_specs=(VMEM,) * 7,
        scratch_shapes=[
            pltpu.VMEM((HB, width), F32), both, both, pltpu.VMEM((8, LB), F32),
            pltpu.VMEM((1,) + block_rate.shape, F32),
            pltpu.VMEM(region_axial.shape, F32), pltpu.VMEM((1,) + region_shear.shape, F32),
            pltpu.SemaphoreType.DMA((6,)),
        ],
        compiler_params=room,
        cost_estimate=pl.CostEstimate(flops=1 << 20, bytes_accessed=1 << 20, transcendentals=0),
    )(
        near,
        block_inverse,
        *in_hbm(
            adj_gating[0], voltages, gatings, region_axial, region_shear[None], block_rate[None],
        ),
    )
    ends = (0, lines - 1)
    cycle = list(range(0, lines, 2)) + list(range(lines - 1, 0, -2))
    onward = {i: cycle[(n + 1) % lines] for n, i in enumerate(cycle)}
    pairing = swaps(lines, lanes, lambda i, j: (i ^ 1, j))
    after = lax.ppermute(
        near, BOTH,
        swaps(lines, lanes, lambda i, j: (i, j ^ 1) if i in ends else (i - 1 + 2 * (i % 2), j)),
    )
    before = lax.ppermute(near[:FAR], BOTH, swaps(lines, lanes, lambda i, j: (onward[i], j)))
    pair = lax.ppermute(near, BOTH, pairing)
    relayed, own_rows = lax.optimization_barrier((after[:FAR], own_rows))
    beyond = lax.ppermute(relayed, BOTH, pairing)
    count = -(-SLOTS * label_blocks // 8) * 8
    share_shape = (share_tiles(width), 8, width)
    label_scratch = [pltpu.VMEM((count, LB), F32)]
    begun, solved, centres, partial, beside = pl.pallas_call(
        gather_kernel,
        out_shape=(
            shape(share_shape, F32), shape((HB, width), F32), shape((3, HB, width), F32),
            shape((3, HB, width), F32), shape((8, HB, width), F32),
        ),
        in_specs=[VMEM] * 8,
        out_specs=(VMEM,) * 5,
        scratch_shapes=label_scratch,
        compiler_params=room,
        cost_estimate=pl.CostEstimate(flops=1 << 20, bytes_accessed=1 << 20, transcendentals=0),
    )(near, pair, after, regions, vectors, own, own_rows, here)
    share, outside, distant = pl.pallas_call(
        complete_kernel,
        out_shape=(
            shape(share_shape, F32), shape((2, HB, width), F32), shape((4, HB, width), F32),
        ),
        in_specs=[VMEM] * 13,
        out_specs=(VMEM,) * 3,
        scratch_shapes=label_scratch,
        compiler_params=room,
    )(
        near, pair, after, before, beyond, regions, vectors, own, own_rows, here, begun,
        partial, beside,
    )
    shares = [share] + [
        lax.ppermute(share, BOTH, swaps(lines, lanes, lambda i, j: (i, j ^ d)))
        for d in range(1, lanes)
    ]
    out_v, out_w = pl.pallas_call(
        lambda *refs: finish_kernel(lanes, *refs),
        out_shape=(shape((HB, width), F32),) * 2,
        in_specs=[VMEM] * (lanes + 11),
        out_specs=(VMEM,) * 2,
        scratch_shapes=[pltpu.VMEM((lanes,) + share_shape, F32)],
        compiler_params=room,
    )(
        *shares, solved, centres, partial, outside, here, beside, distant, vectors, own, early,
        numbers,
    )
    return (out_v[None], out_w[None])


def solution(mesh):
    return jax.shard_map(
        per_device,
        mesh=mesh,
        in_specs=(
            P("gx", "gy", None),
            P("gx", "gy", None),
            P(None, "gx", "gy", None),
            P(None, "gx", "gy", None),
            P("gx", "gy", None),
            P(),
            P(),
            P(),
            P(),
        ),
        out_specs=(P("gx", "gy", None), P("gx", "gy", None)),
        check_vma=False,
    )
```
